32 devices in a mesh: groups: 2 (over x), ctx: 8 (over z, y), tp: 2 (over core).
Axes of the slice: x: 2, y: 2, z: 4, core: 2. Of those that a mesh axis runs over, the one named last changes fastest.
Arguments:
- enc_input: bfloat16 [2048, 4096], P(('groups', 'ctx')), parts along dimension 0, may hold values from -6 to 6
- enc_query: bfloat16 [2048, 1024], P(('groups', 'ctx'), 'tp'), parts along dimension 0
- enc_key: bfloat16 [2048, 1024], P(('groups', 'ctx'), 'tp'), parts along dimension 0
- enc_value: bfloat16 [2048, 1024], P(('groups', 'ctx'), 'tp'), parts along dimension 0, may hold values from -6 to 6
- seq_length: int32 [2], P('groups'), parts along dimension 0, may hold values from 256 to 1024
- attn_out_weight: bfloat16 [1024, 4096], P('tp'), may hold values from -0.1875 to 0.1875
- enc_gain: bfloat16 [4096], replicated, may hold values from 0.25 to 1.75
- cross_key_weight: bfloat16 [4096, 1024], P('ctx', 'tp'), may hold values from -0.09375 to 0.09375
- cross_value_weight: bfloat16 [4096, 1024], P('ctx', 'tp'), may hold values from -0.09375 to 0.09375
- embed_table: bfloat16 [32128, 4096], P('tp', 'ctx')
- dec_ids: int32 [32, 2], P('groups'), parts along dimension 0, may hold values from 0 to 32127
- dec_gain: bfloat16 [4096], P('ctx'), may hold values from 0.25 to 1.75
- cross_query_weight: bfloat16 [4096, 1024], P('ctx', 'tp')
- cross_out_weight: bfloat16 [1024, 4096], P('tp', 'ctx'), may hold values from -0.1875 to 0.1875
Outputs:
- cross_keys: bfloat16 [16, 128, 1024], P(('groups', 'ctx'), None, 'tp'), parts along dimension 0
- cross_values: bfloat16 [16, 128, 1024], P(('groups', 'ctx'), None, 'tp'), parts along dimension 0
- decoded: bfloat16 [32, 2, 4096], P('groups', None, 'ctx'), parts along dimension 0
The draws below stay inside these ranges and needn't reach their ends.
There are 2 independent parts, one for each index of `groups`. The reference program is written for one: setup_inputs(seed, part) draws one part's arguments, and reference() takes and returns one part's arrays. A program takes and returns all parts, laid end to end along the dimension named above; an argument that names none is the same for every part. Nothing has to cross between parts.
Inputs may be any that keep to these rules, and one draw needn't show every extreme that they name: `seq_length`: the input's real length.
All inputs are finite; a program needn't handle non-finite values.
Results may differ from the reference program's by a relative error of at most 0.04.
Values may be sent and summed in bfloat16 or wider, within the bound.
A program may use at most 128 MiB of HBM per device.

```python
import math
import jax
import jax.numpy as jnp
import numpy as np
from jax import lax

D = 4096
HEADS = 8
HD = 128
VOCAB = 32128
BEAMS = 16
INNER = 1024
SEQ = 1024
N_CTX = 8


def attention_pair(key):
    queries = 1.7 * jnp.clip(jax.random.normal(jax.random.fold_in(key, 11), (SEQ, INNER), jnp.float32), -6.0, 6.0)
    keys = 1.7 * jnp.clip(jax.random.normal(jax.random.fold_in(key, 12), (SEQ, INNER), jnp.float32), -6.0, 6.0)
    return (queries, keys)


def draw_enc_query(key, part):
    return attention_pair(key)[0].astype(jnp.bfloat16)


def draw_enc_key(key, part):
    return attention_pair(key)[1].astype(jnp.bfloat16)


def draw_embed_table(key, part):
    row_scale = jnp.exp(jax.random.uniform(jax.random.fold_in(key, 21), (VOCAB, 1), jnp.float32, math.log(0.4), math.log(1.6)))
    col_scale = jnp.exp(jnp.linspace(math.log(0.4), math.log(1.6), D, dtype=jnp.float32))[None, :]
    base = 0.8 * jnp.clip(jax.random.normal(jax.random.fold_in(key, 22), (VOCAB, D), jnp.float32), -3.0, 3.0)
    return (base * row_scale * col_scale).astype(jnp.bfloat16)


def draw_cross_query_weight(key, part):
    spread = 6.0 / math.sqrt(D)
    base = jnp.clip(jax.random.normal(jax.random.fold_in(key, 33), (D, INNER), jnp.float32), -5.0, 5.0)
    return (base * spread).astype(jnp.bfloat16)


def touch_ends(values, rng, least, largest):
    longest = values.shape.index(max(values.shape))
    spots = []
    for shift in (0, 1):
        where = [jax.random.randint(jax.random.fold_in(rng, axis), (), 0, length) for axis, length in enumerate(values.shape)]
        where[longest] = (where[longest] + shift) % values.shape[longest]
        spots.append(tuple(where))
    return values.at[spots[0]].set(least).at[spots[1]].set(largest)


def shard_levels(stream_key, extent, pieces, least, top_value):
    gain, own = 1.0, jax.random.fold_in(stream_key, 6)
    for axis_at, blocks in pieces:
        heights = jnp.exp(jax.random.uniform(jax.random.fold_in(own, axis_at), (blocks,), jnp.float32, least / len(pieces), top_value / len(pieces)))
        gain = gain * jnp.repeat(heights, extent[axis_at] // blocks).reshape([-1 if axis == axis_at else 1 for axis in range(len(extent))])
    return gain


def rank_table(amount, lean):
    weights = [(1 << 20) // math.isqrt(standing ** lean) + 1 for standing in range(1, amount + 1)]
    deviation = 1 + sum(weights) // (1 << 30)
    return np.cumsum(np.array([max(1, weight // deviation) for weight in weights]))


def ranked_ids(rng, shape, amount, lean):
    table = rank_table(amount, lean)
    pick = jax.random.randint(jax.random.fold_in(rng, 1), shape, 0, int(table[amount - 1]))
    standing = jnp.searchsorted(jnp.asarray(table, jnp.int32), pick, side="right")
    return jax.random.permutation(jax.random.fold_in(rng, 2), amount)[standing].astype(jnp.int32)


def bell_draw(stream_key, dims, scale, reach, shards=(), held_as=jnp.bfloat16):
    entries = scale * jax.random.normal(stream_key, dims, jnp.float32)
    if shards:
        entries = entries * shard_levels(stream_key, dims, shards, -0.22, 0.18)
    return jnp.clip(entries, -reach, reach).astype(held_as)


def setup_inputs(seed: int = 0, part: int = 0) -> dict:
    splits = jax.random.split(jax.random.key(seed), 15)
    part_keys = jax.random.split(jax.random.fold_in(splits[14], part), 15)
    enc_input = bell_draw(part_keys[0], (SEQ, D), 1.0, 6.0, ((0, 8),))
    enc_query = draw_enc_query(jax.random.fold_in(jax.random.fold_in(splits[14], part), 71), part)
    enc_key = draw_enc_key(jax.random.fold_in(jax.random.fold_in(splits[14], part), 71), part)
    enc_value = bell_draw(part_keys[3], (SEQ, INNER), 1.0, 6.0, ((0, 8), (1, 2)))
    seq_length = jax.random.randint(part_keys[4], (1,), SEQ // 4, SEQ + 1).astype(jnp.int32)
    attn_out_weight = bell_draw(splits[5], (INNER, D), INNER ** -0.5, 0.1875, ((0, 2),))
    enc_gain = jnp.clip(1.0 + 0.15 * jax.random.normal(splits[6], (D,), jnp.float32), 0.25, 1.75).astype(jnp.bfloat16)
    cross_key_weight = bell_draw(splits[7], (D, INNER), D ** -0.5, 0.09375, ((0, 8), (1, 2)))
    cross_value_weight = bell_draw(splits[8], (D, INNER), D ** -0.5, 0.09375, ((0, 8), (1, 2)))
    embed_table = draw_embed_table(jax.random.fold_in(splits[14], 71), part)
    dec_ids = touch_ends(ranked_ids(part_keys[10], (BEAMS, 2), VOCAB, 2), jax.random.fold_in(part_keys[10], 3), 0, VOCAB - 1).astype(jnp.int32)
    dec_gain = jnp.clip(1.0 + 0.15 * jax.random.normal(splits[11], (D,), jnp.float32), 0.25, 1.75).astype(jnp.bfloat16)
    cross_query_weight = draw_cross_query_weight(jax.random.fold_in(splits[14], 71), part)
    cross_out_weight = bell_draw(splits[13], (INNER, D), INNER ** -0.5, 0.1875, ((0, 2), (1, 8)))
    return dict(enc_input=enc_input, enc_query=enc_query, enc_key=enc_key, enc_value=enc_value, seq_length=seq_length, attn_out_weight=attn_out_weight, enc_gain=enc_gain, cross_key_weight=cross_key_weight, cross_value_weight=cross_value_weight, embed_table=embed_table, dec_ids=dec_ids, dec_gain=dec_gain, cross_query_weight=cross_query_weight, cross_out_weight=cross_out_weight)


EPSILON = 1e-06
FLOOR = -1e+30

def soft_attend(queries, keys, values, valid, factor):
    scores = jnp.einsum('qhd,khd->hqk', queries.astype(jnp.float32), keys) * factor
    scores = jnp.where(valid[None, None, :], scores, FLOOR)
    top = lax.optimization_barrier(jnp.max(scores, axis=-1, keepdims=True))
    probs = jnp.where(valid[None, None, :], jnp.exp(scores - top), 0.0)
    total = lax.optimization_barrier(jnp.sum(probs, axis=-1))
    weights = lax.optimization_barrier(probs.astype(jnp.bfloat16)).astype(jnp.float32)
    mixed = jnp.einsum('hqk,khd->qhd', weights, values)
    return mixed / jnp.transpose(total)[:, :, None]

def reference(enc_input, enc_query, enc_key, enc_value, seq_length, attn_out_weight, enc_gain, cross_key_weight, cross_value_weight, embed_table, dec_ids, dec_gain, cross_query_weight, cross_out_weight):
    valid = jnp.arange(SEQ, dtype=jnp.int32) < seq_length[0]
    block = math.gcd(SEQ, 512)
    keys = enc_key.reshape(SEQ, HEADS, HD).astype(jnp.float32)
    values = enc_value.reshape(SEQ, HEADS, HD).astype(jnp.float32)
    query_blocks = enc_query.reshape(SEQ // block, block, HEADS, HD)

    def one_block(qblk):
        return soft_attend(qblk, keys, values, valid, HD ** (-0.5))
    context = lax.map(one_block, query_blocks).reshape(SEQ, INNER).astype(jnp.bfloat16)
    attended = jnp.dot(context, attn_out_weight, preferred_element_type=jnp.float32)
    resid = enc_input.astype(jnp.float32) + attended
    scale = lax.rsqrt(lax.optimization_barrier(jnp.mean(resid * resid, axis=-1, keepdims=True)) + EPSILON)
    memory = (resid * scale * enc_gain.astype(jnp.float32)).astype(jnp.bfloat16)
    keys_full = jnp.dot(memory, cross_key_weight, preferred_element_type=jnp.float32).astype(jnp.bfloat16)
    values_full = jnp.dot(memory, cross_value_weight, preferred_element_type=jnp.float32).astype(jnp.bfloat16)
    cross_keys = jnp.transpose(keys_full.reshape(SEQ // N_CTX, N_CTX, INNER), (1, 0, 2))
    cross_values = jnp.transpose(values_full.reshape(SEQ // N_CTX, N_CTX, INNER), (1, 0, 2))
    hidden = jnp.take(embed_table, dec_ids.reshape(-1), axis=0).astype(jnp.float32)
    scaled = (hidden * dec_gain.astype(jnp.float32)).astype(jnp.bfloat16)
    raw = jnp.dot(scaled, cross_query_weight, preferred_element_type=jnp.float32)
    factor = lax.rsqrt(lax.optimization_barrier(jnp.sum(hidden * hidden, axis=-1, keepdims=True)) / D + EPSILON)
    query = (raw * factor * HD ** (-0.5)).astype(jnp.bfloat16).reshape(-1, HEADS, HD)
    mixed = soft_attend(query, keys_full.reshape(SEQ, HEADS, HD).astype(jnp.float32), values_full.reshape(SEQ, HEADS, HD).astype(jnp.float32), valid, 1.0)
    attn = mixed.reshape(-1, INNER).astype(jnp.bfloat16)
    out = jnp.dot(attn, cross_out_weight, preferred_element_type=jnp.float32) + hidden
    decoded = out.astype(jnp.bfloat16).reshape(BEAMS, 2, D)
    return (cross_keys, cross_values, decoded)
```

```python
import math

import jax
import jax.numpy as jnp
from jax import lax
from jax.experimental import pallas as pl
from jax.experimental.pallas import tpu as pltpu
from jax.sharding import PartitionSpec as P

D = 4096
HD = 128


EPSILON = 1e-06
FLOOR = -1e30


def joined(value, axis, join):
    pieces = jax.tree.map(lambda part: lax.all_gather(part, axis), value)
    head = jax.tree.map(lambda part: part[0], pieces)
    tail = jax.tree.map(lambda part: part[1:], pieces)
    total, _ = lax.scan(lambda total, piece: (join(total, piece), None), head, tail)
    return total


def softmax_merge(first, second):
    top_first, total_first, mixed_first = first
    top_second, total_second, mixed_second = second
    top = jnp.maximum(top_first, top_second)
    weight_first = jnp.exp(top_first - top)
    weight_second = jnp.exp(top_second - top)
    total = total_first * weight_first + total_second * weight_second
    mixed = mixed_first * weight_first[..., None] + mixed_second * weight_second[..., None]
    return (top, total, mixed)


def partial_softmax(queries, keys, values, valid, factor):
    scores = jnp.einsum("qhd,khd->hqk", queries, keys, preferred_element_type=jnp.float32) * factor
    scores = jnp.where(valid[None, None, :], scores, FLOOR)
    top = jnp.max(scores, axis=-1)
    probs = jnp.where(valid[None, None, :], jnp.exp(scores - top[..., None]), 0.0)
    total = jnp.sum(probs, axis=-1)
    mixed = jnp.einsum(
        "hqk,khd->hqd", probs.astype(jnp.bfloat16), values, preferred_element_type=jnp.float32
    )
    return (top, total, mixed)


def norm_rows(resid, gain):
    scale = lax.rsqrt(jnp.mean(resid * resid, axis=-1, keepdims=True) + EPSILON)
    return (resid * scale * gain.astype(jnp.float32)).astype(jnp.bfloat16)


def local(
    enc_input,
    enc_query,
    enc_key,
    enc_value,
    seq_length,
    attn_out_weight,
    enc_gain,
    cross_key_weight,
    cross_value_weight,
    embed_table,
    dec_ids,
    dec_gain,
    cross_query_weight,
    cross_out_weight,
):
    rows, inner_local = enc_query.shape
    heads_local = inner_local // HD
    limit = seq_length[0]
    queries = enc_query.reshape(rows, heads_local, HD)
    start_state = (
        jnp.full((heads_local, rows), FLOOR, jnp.float32),
        jnp.zeros((heads_local, rows), jnp.float32),
        jnp.zeros((heads_local, rows, HD), jnp.float32),
    )
    carry = start_state
    key_rows = lax.all_gather(enc_key, "ctx", axis=0, tiled=True)
    value_rows = lax.all_gather(enc_value, "ctx", axis=0, tiled=True)
    count = key_rows.shape[0]
    block = math.gcd(count, 2048)
    blocks = count // block
    key_blocks = key_rows.reshape(blocks, block, heads_local, HD)
    value_blocks = value_rows.reshape(blocks, block, heads_local, HD)
    offsets = jnp.arange(blocks, dtype=jnp.int32) * block

    def one_block(state, item):
        key_block, value_block, offset = item
        positions = offset + jnp.arange(block, dtype=jnp.int32)
        update = partial_softmax(queries, key_block, value_block, positions < limit, HD ** (-0.5))
        return (softmax_merge(state, update), None)

    carry, unused = lax.scan(one_block, carry, (key_blocks, value_blocks, offsets))
    top, total, mixed = carry
    context = (
        jnp.transpose(mixed / total[..., None], (1, 0, 2))
        .reshape(rows, inner_local)
        .astype(jnp.bfloat16)
    )
    summed = lax.psum(jnp.dot(context, attn_out_weight, preferred_element_type=jnp.float32), "tp")
    memory = norm_rows(enc_input.astype(jnp.float32) + summed, enc_gain)
    ctx_count = lax.axis_size("ctx")
    slots = rows // ctx_count
    key_sum = jnp.dot(
        memory,
        lax.all_gather(cross_key_weight, "ctx", axis=0, tiled=True),
        preferred_element_type=jnp.float32,
    )
    value_sum = jnp.dot(
        memory,
        lax.all_gather(cross_value_weight, "ctx", axis=0, tiled=True),
        preferred_element_type=jnp.float32,
    )
    key_rows = key_sum.astype(jnp.bfloat16)
    value_rows = value_sum.astype(jnp.bfloat16)
    keys_moved, values_moved = (
        lax.all_to_all(
            key_rows.reshape(slots, ctx_count, inner_local),
            "ctx",
            split_axis=1,
            concat_axis=0,
            tiled=True,
        ),
        lax.all_to_all(
            value_rows.reshape(slots, ctx_count, inner_local),
            "ctx",
            split_axis=1,
            concat_axis=0,
            tiled=True,
        ),
    )
    keys_cache = keys_moved.reshape(rows, inner_local)
    values_cache = values_moved.reshape(rows, inner_local)
    beams = dec_ids.shape[0]
    vocab_local = embed_table.shape[0]
    flat_ids = dec_ids.reshape(-1) - lax.axis_index("tp") * vocab_local
    inside = (flat_ids >= 0) & (flat_ids < vocab_local)
    looked = jnp.take(embed_table, jnp.clip(flat_ids, 0, vocab_local - 1), axis=0)
    own_rows = jnp.where(inside[:, None], looked.astype(jnp.float32), 0.0)
    hidden = lax.psum(own_rows.astype(jnp.bfloat16), "tp").astype(jnp.float32)
    scaled = (hidden * dec_gain.astype(jnp.float32)).astype(jnp.bfloat16)
    raw_part = jnp.dot(scaled, cross_query_weight, preferred_element_type=jnp.float32)
    square_part = jnp.sum(hidden * hidden, axis=-1)
    raw, squares = lax.psum((raw_part, square_part), "ctx")
    factor = lax.rsqrt(squares / D + EPSILON)
    query = (raw * factor[:, None] * HD ** (-0.5)).astype(jnp.bfloat16).reshape(-1, heads_local, HD)
    positions = jnp.arange(rows, dtype=jnp.int32) * ctx_count + lax.axis_index("ctx")
    local_part = partial_softmax(
        query,
        keys_cache.reshape(rows, heads_local, HD),
        values_cache.reshape(rows, heads_local, HD),
        positions < limit,
        1.0,
    )
    top_all, total_all, mixed_all = joined(local_part, "ctx", softmax_merge)
    attn = (
        jnp.transpose(mixed_all / total_all[..., None], (1, 0, 2))
        .reshape(-1, inner_local)
        .astype(jnp.bfloat16)
    )
    out_part = jnp.dot(attn, cross_out_weight, preferred_element_type=jnp.float32)
    out = lax.psum(out_part, "tp")
    decoded = (out + hidden).astype(jnp.bfloat16).reshape(beams, 2, -1)
    return (keys_cache[None], values_cache[None], decoded)


MESH = pl.DeviceIdType.MESH
F32 = jnp.float32
BF16 = jnp.bfloat16
ORDER = (3, 0, 2, 1)


def pick_kernel(ids_ref, table_ref, out_ref, held, rows, sems):
    count = out_ref.shape[0]
    vocab_local = table_ref.shape[0]
    base = lax.axis_index("tp") * vocab_local
    copies = []
    for j in range(count):
        own = jnp.clip(ids_ref[j % 2, j // 2] - base, 0, vocab_local - 1)
        start = pl.multiple_of(lax.div(own, 16) * 16, 16)
        copy = pltpu.make_async_copy(table_ref.at[pl.ds(start, 16)], held.at[j], sems.at[j])
        copy.start()
        copies.append(copy)
    spots = lax.broadcasted_iota(jnp.int32, held.shape[1:], 0)
    for j in range(count):
        copies[j].wait()
        own = ids_ref[j % 2, j // 2] - base
        inside = (own >= 0) & (own < vocab_local)
        spot = jnp.where(inside, lax.rem(jnp.clip(own, 0, vocab_local - 1), 16), -1)
        block = held[j].astype(F32)
        rows[pl.ds(j, 1)] = jnp.sum(jnp.where(spots == spot, block, 0.0), axis=0, keepdims=True)
    out_ref[...] = rows[...].astype(BF16)


def hand_kernel(keys_ref, values_ref, decoded_ref, keys_out, values_out, decoded_out):
    keys_out[0] = keys_ref[...]
    values_out[0] = values_ref[...]
    for i in range(decoded_out.shape[0]):
        decoded_out[i] = decoded_ref[2 * i : 2 * i + 2].astype(BF16)


def fused_kernel(
    length, gains, q, k, v, ein, looked_hbm, wq, wo, wk, wv, wout,
    keys_out, values_out, decoded_out,
    q_own, q_turned, ein_own, ein_turned, looked, looked_far, wq_own, wout_own,
    kg, vg, qg, eg, wo_all, wk_all, wv_all, ctx_all, gained, square_own, square_far, square_sum, square_in,
    part_k, part_v, pair_k, pair_v, near_k, near_v, far_k, far_v, keys_own, values_own,
    raw_own, raw_out, raw_in, query_in, query_all, mix_own, mix_out, mix_in, attn_in, attn_all, proj_out, proj_in, hidden_ref,
    send, r_look, r_wo, r_q, r_k, r_v, r_wk, r_wv, r_raw, r_query, r_ein, r_ctx, r_gained, r_square_far, r_square,
    r_pair, r_near, r_far, r_mix, r_attn, r_proj, fetched, stored,
):
    c = lax.axis_index("ctx")
    t = lax.axis_index("tp")
    z, y = lax.div(c, 2), lax.rem(c, 2)
    mate, other = c + 1 - 2 * y, 1 - t
    line = [lax.rem(z + d, 4) for d in (2, 1, 3)]
    peers = [lax.rem(c + d, 8) for d in range(1, 8)]
    rows = q.shape[0]
    inner = q.shape[1]
    width = wq.shape[0]
    half = rows // 2
    each = rows // 8
    own_block = z * 2 + t
    heads = inner // HD
    pending = []

    def remote(source, target, arrival, to_ctx, to_tp):
        return pltpu.make_async_remote_copy(
            src_ref=source, dst_ref=target, send_sem=send, recv_sem=arrival,
            device_id={"ctx": to_ctx, "tp": to_tp}, device_id_type=MESH,
        )

    def put(source, target, arrival, to_ctx, to_tp):
        copy = remote(source, target, arrival, to_ctx, to_tp)
        copy.start()
        pending.append(copy)

    def got(target, arrival):
        remote(target, target, arrival, mate, t).wait_recv()

    def fetch(source, target, arrival):
        copy = pltpu.make_async_copy(source, target, arrival)
        copy.start()
        return copy

    def cols(index, size):
        return pl.ds(pl.multiple_of(index * size, size), size)

    barrier = pltpu.get_barrier_semaphore()
    for peer in peers:
        pl.semaphore_signal(barrier, inc=1, device_id={"ctx": peer, "tp": t}, device_id_type=MESH)
    pl.semaphore_signal(barrier, inc=1, device_id={"ctx": c, "tp": other}, device_id_type=MESH)

    q_fetch = fetch(q, q_own, fetched.at[0])
    k_fetch = fetch(k.at[:, cols(z, HD)], kg.at[c], fetched.at[1])
    v_fetch = fetch(v.at[:, cols(z, HD)], vg.at[c], fetched.at[2])
    ein_fetches = [
        fetch(ein.at[:, cols(far * 2 + t, width)], ein_own.at[far], fetched.at[3 + far]) for far in range(4)
    ]
    looked_fetch = fetch(looked_hbm, looked, fetched.at[7])
    wq_fetch = fetch(wq, wq_own, fetched.at[8])
    late = [
        fetch(wo.at[:, cols(own_block, width)], wo_all.at[cols(t, inner)], fetched.at[9]),
        fetch(wk, wk_all.at[y], fetched.at[10]),
        fetch(wv, wv_all.at[y], fetched.at[11]),
    ]
    wout_fetch = fetch(wout, wout_own, fetched.at[12])
    pl.semaphore_wait(barrier, len(peers) + 1)

    for far in line:
        to = far * 2 + y
        put(k.at[:, cols(far, HD)], kg.at[c], r_k.at[c], to, t)
        put(v.at[:, cols(far, HD)], vg.at[c], r_v.at[c], to, t)
    put(k.at[:, cols(z, HD)], kg.at[c], r_k.at[c], mate, t)
    put(v.at[:, cols(z, HD)], vg.at[c], r_v.at[c], mate, t)

    place = lax.broadcasted_iota(jnp.int32, (rows, rows), 0)
    spot = lax.broadcasted_iota(jnp.int32, (rows, rows), 1)
    side, rest = lax.div(place, half), lax.rem(place, half)
    turn = (spot == lax.rem(rest, each) * 8 + lax.div(rest, each) * 2 + side).astype(BF16)

    q_fetch.wait()
    turned = jnp.dot(turn, q_own[...], preferred_element_type=F32).astype(BF16)
    for s in range(2):
        q_turned[s] = turned[s * half : (s + 1) * half]
    for peer in peers:
        put(
            q_turned.at[lax.rem(peer, 2), :, cols(lax.div(peer, 2), HD)], qg.at[c], r_q.at[c], peer, t
        )
    qg[c] = q_turned[y, :, cols(z, HD)]
    put(wo.at[:, cols(z * 2 + other, width)], wo_all.at[cols(t, inner)], r_wo, c, other)

    for far in range(4):
        ein_fetches[far].wait()
        turned = jnp.dot(turn, ein_own[far], preferred_element_type=F32).astype(BF16)
        for s in range(2):
            ein_turned[far, s] = turned[s * half : (s + 1) * half]

    for far in line:
        source = far * 2 + y
        got(kg.at[source], r_k.at[source])
        put(kg.at[source], kg.at[source], r_k.at[source], mate, t)
        got(vg.at[source], r_v.at[source])
        put(vg.at[source], vg.at[source], r_v.at[source], mate, t)
    for peer in peers:
        put(ein_turned.at[lax.div(peer, 2), lax.rem(peer, 2)], eg.at[c], r_ein.at[c], peer, t)
    eg[c] = ein_turned[z, y]
    put(wk, wk_all.at[y], r_wk, mate, t)
    put(wv, wv_all.at[y], r_wv, mate, t)

    tokens = looked.shape[0]
    looked_fetch.wait()
    put(looked, looked_far, r_look, c, other)

    k_fetch.wait()
    v_fetch.wait()
    for peer in peers:
        got(qg.at[peer], r_q.at[peer])
    for far in range(4):
        source = far * 2 + 1 - y
        got(kg.at[source], r_k.at[source])
        got(vg.at[source], r_v.at[source])

    limit = length[0]
    every_key = kg[...].reshape(8 * rows, HD)
    every_value = vg[...].reshape(8 * rows, HD)
    valid = lax.broadcasted_iota(jnp.int32, (1, 8 * rows), 1) < limit

    def block_at(core, far, chunk):
        return ctx_all.at[chunk, :, cols(core * 4 + far, HD)], r_ctx.at[core * 4 + far, chunk]

    for chunk in ORDER:
        queries = qg[:, chunk * each : (chunk + 1) * each, :].reshape(rows, HD)
        scores = lax.dot_general(
            queries, every_key, (((1,), (1,)), ((), ())), preferred_element_type=F32
        ) * (HD ** (-0.5))
        scores = jnp.where(valid, scores, FLOOR)
        top = jnp.max(scores, axis=-1, keepdims=True)
        probs = jnp.where(valid, jnp.exp(scores - top), 0.0)
        total = jnp.sum(probs, axis=-1, keepdims=True)
        mixed = jnp.dot(probs.astype(BF16), every_value, preferred_element_type=F32)
        ctx_all[chunk, :, cols(t * 4 + z, HD)] = (mixed / total).astype(BF16)
        here, arrival = block_at(t, z, chunk)
        for far in line:
            put(here, here, arrival, far * 2 + y, t)
        put(here, here, arrival, c, other)

    got(looked_far, r_look)
    wq_fetch.wait()
    hidden = looked[...].astype(F32) + looked_far[...].astype(F32)
    hidden_ref[...] = hidden
    scaled = (hidden * gains[0:1]).astype(BF16)
    raw_own[:, :inner] = jnp.dot(scaled, wq_own[...], preferred_element_type=F32)
    raw_own[:, inner:] = jnp.broadcast_to(jnp.sum(hidden * hidden, axis=-1, keepdims=True), (tokens, 128))
    share = tokens // 8
    for j in range(8):
        raw_out[j] = raw_own[j * share : (j + 1) * share, :]
    for peer in peers:
        put(raw_out.at[peer], raw_in.at[c], r_raw.at[c], peer, t)
    raw_in[c] = raw_out[c]

    for copy in late:
        copy.wait()
    got(wo_all.at[cols(other, inner)], r_wo)
    for peer in peers:
        got(eg.at[peer], r_ein.at[peer])
    picked_gain = lax.broadcasted_iota(jnp.int32, (8, width), 0) == own_block
    gain = jnp.sum(jnp.where(picked_gain, gains[8:16], 0.0), axis=0, keepdims=True)

    def relay(chunk):
        for far in line:
            here, arrival = block_at(t, far, chunk)
            got(here, arrival)
            put(here, here, arrival, c, other)

    def project(chunk):
        for far in range(4):
            got(*block_at(other, far, chunk))
        resid = jnp.dot(ctx_all[chunk], wo_all[...], preferred_element_type=F32)
        resid = resid + eg[:, chunk * each : (chunk + 1) * each, :].reshape(rows, width).astype(F32)
        spread = jnp.where(place == spot, jnp.sum(resid * resid, axis=-1, keepdims=True), 0.0)
        square_own[chunk] = jnp.sum(spread, axis=0, keepdims=True)
        gained[chunk, t] = (resid * gain).astype(BF16)
        put(gained.at[chunk, t], gained.at[chunk, t], r_gained.at[chunk], c, other)
        put(square_own.at[chunk], square_far.at[chunk], r_square_far.at[chunk], c, other)

    ways = ((part_k, pair_k, near_k, far_k, wk_all, r_wk), (part_v, pair_v, near_v, far_v, wv_all, r_wv))

    def start_only(source, target, arrival, to_z):
        remote(source, target, arrival, to_z * 2 + y, t).start()

    def spread_out(chunk, first):
        got(gained.at[chunk, other], r_gained.at[chunk])
        end = 0 if chunk >= 2 else 3
        for way, (part, pair, near, far, weight, arrival) in enumerate(ways):
            if first:
                got(weight.at[1 - y], arrival)
            total = jnp.dot(gained[chunk, 0], weight[0], preferred_element_type=F32)
            total = total + jnp.dot(gained[chunk, 1], weight[1], preferred_element_type=F32)
            part[chunk] = total.astype(BF16)

            @pl.when(z == end)
            def _():
                start_only(
                    part.at[chunk], pair.at[chunk % 2], r_pair.at[way, chunk % 2], 1 if end == 0 else 2
                )

            @pl.when(z == (chunk + 1 if chunk % 2 == 0 else chunk - 1))
            def _():
                start_only(part.at[chunk], near, r_near.at[way], chunk)

    def join(chunk):
        middle = 1 if chunk >= 2 else 2
        for way, (part, pair, near, far, weight, arrival) in enumerate(ways):

            @pl.when(z == middle)
            def _():
                got(pair.at[chunk % 2], r_pair.at[way, chunk % 2])
                both = part[chunk].astype(F32) + pair[chunk % 2].astype(F32)
                pair[chunk % 2] = both.astype(BF16)
                start_only(pair.at[chunk % 2], far, r_far.at[way], chunk)

    relay(ORDER[0])
    relay(ORDER[1])
    project(ORDER[0])
    relay(ORDER[2])
    project(ORDER[1])
    spread_out(ORDER[0], True)
    relay(ORDER[3])
    project(ORDER[2])
    spread_out(ORDER[1], False)
    project(ORDER[3])
    spread_out(ORDER[2], False)
    spread_out(ORDER[3], False)
    for chunk in range(4):
        got(square_far.at[chunk], r_square_far.at[chunk])
        square_sum[chunk] = square_own[chunk] + square_far[chunk]
    for far in line:
        put(square_sum.at[far], square_in.at[z], r_square.at[z], far * 2 + y, t)
    square_in[z] = square_sum[z]

    join(ORDER[0])
    join(ORDER[1])
    for peer in peers:
        got(raw_in.at[peer], r_raw.at[peer])
    raw = raw_in[0]
    for j in range(1, 8):
        raw = raw + raw_in[j]
    factor = lax.rsqrt(raw[:, inner : inner + 1] / D + EPSILON)
    query_in[c] = (raw[:, :inner] * factor * HD ** (-0.5)).astype(BF16).astype(F32)
    for peer in peers:
        put(query_in.at[c], query_in.at[c], r_query.at[c], peer, t)
    join(ORDER[2])
    join(ORDER[3])

    for far in line:
        got(square_in.at[far], r_square.at[far])
    square = square_in[0] + square_in[1] + square_in[2] + square_in[3]
    column = jnp.sum(jnp.where(place == spot, square, 0.0), axis=-1, keepdims=True)
    scale = lax.rsqrt(column / D + EPSILON)
    for peer in peers:
        got(query_in.at[peer], r_query.at[peer])
    for j in range(8):
        query_all[j * share : (j + 1) * share, :] = query_in[j]

    stores = []
    for way, (own, out) in enumerate(((keys_own, keys_out), (values_own, values_out))):
        part, pair, near, far, weight, arrival = ways[way]
        got(near, r_near.at[way])
        got(far, r_far.at[way])
        total = part[z].astype(F32) + near[...].astype(F32) + far[...].astype(F32)
        own[...] = (total * scale).astype(BF16)
        stores.append(fetch(own, out, stored.at[way]))

    own_valid = lax.broadcasted_iota(jnp.int32, (1, rows), 1) * 8 + c < limit
    lanes = lax.broadcasted_iota(jnp.int32, (tokens, 128), 1)
    stats = jnp.zeros((tokens, 128), F32)
    for head in range(heads):
        part = slice(head * HD, (head + 1) * HD)
        scores = lax.dot_general(
            query_all[:, part].astype(BF16), keys_own[:, part], (((1,), (1,)), ((), ())),
            preferred_element_type=F32,
        )
        scores = jnp.where(own_valid, scores, FLOOR)
        top = jnp.max(scores, axis=-1, keepdims=True)
        probs = jnp.where(own_valid, jnp.exp(scores - top), 0.0)
        stats = jnp.where(lanes == head, top, stats)
        stats = jnp.where(lanes == heads + head, jnp.sum(probs, axis=-1, keepdims=True), stats)
        mix_own[:, part] = jnp.dot(probs.astype(BF16), values_own[:, part], preferred_element_type=F32)
    mix_own[:, inner:] = stats
    for j in range(8):
        mix_out[j] = mix_own[j * share : (j + 1) * share, :]
    for peer in peers:
        put(mix_out.at[peer], mix_in.at[c], r_mix.at[c], peer, t)
    mix_in[c] = mix_out[c]
    for peer in peers:
        got(mix_in.at[peer], r_mix.at[peer])
    for head in range(heads):
        part = slice(head * HD, (head + 1) * HD)
        tops = [mix_in[j][:, inner + head : inner + head + 1] for j in range(8)]
        top = tops[0]
        for j in range(1, 8):
            top = jnp.maximum(top, tops[j])
        total = jnp.zeros_like(top)
        mixed = jnp.zeros((share, HD), F32)
        for j in range(8):
            weight = jnp.exp(tops[j] - top)
            total = total + mix_in[j][:, inner + heads + head : inner + heads + head + 1] * weight
            mixed = mixed + mix_in[j][:, part] * weight
        attn_in[c, :, part] = (mixed / total).astype(BF16).astype(F32)
    for peer in peers:
        put(attn_in.at[c], attn_in.at[c], r_attn.at[c], peer, t)
    for peer in peers:
        got(attn_in.at[peer], r_attn.at[peer])
    for j in range(8):
        attn_all[j * share : (j + 1) * share, :] = attn_in[j]
    wout_fetch.wait()
    proj_out[...] = jnp.dot(attn_all[...].astype(BF16), wout_own[...], preferred_element_type=F32)
    put(proj_out, proj_in, r_proj, c, other)
    got(proj_in, r_proj)
    decoded_out[...] = proj_out[...] + proj_in[...] + hidden_ref[...]
    for copy in stores:
        copy.wait()
    for copy in pending:
        copy.wait_send()
    for i in range(6):
        remote(near_k, near_k, r_near.at[0], mate, t).wait_send()


def local_fused(
    enc_input, enc_query, enc_key, enc_value, seq_length, attn_out_weight, enc_gain, cross_key_weight,
    cross_value_weight, embed_table, dec_ids, dec_gain, cross_query_weight, cross_out_weight,
):
    rows, inner = enc_query.shape
    width = cross_query_weight.shape[0]
    tokens = dec_ids.size
    whole = pl.BlockSpec(memory_space=pltpu.VMEM)
    scalars = pl.BlockSpec(memory_space=pltpu.SMEM)
    anywhere = pl.BlockSpec(memory_space=pl.ANY)
    gains = jnp.concatenate(
        [jnp.broadcast_to(dec_gain[None], (8, width)), enc_gain.reshape(8, width)], axis=0
    ).astype(F32)
    dma = pltpu.SemaphoreType.DMA
    share = tokens // 8
    half = rows // 2
    looked = pl.pallas_call(
        pick_kernel,
        out_shape=jax.ShapeDtypeStruct((tokens, width), BF16),
        in_specs=[scalars, anywhere],
        out_specs=whole,
        scratch_shapes=[
            pltpu.VMEM((tokens, 16, width), BF16),
            pltpu.VMEM((tokens, width), F32),
            pltpu.SemaphoreType.DMA((tokens,)),
        ],
    )(dec_ids.T, embed_table)
    keys, values, decoded = pl.pallas_call(
        fused_kernel,
        out_shape=(
            jax.ShapeDtypeStruct((rows, inner), BF16),
            jax.ShapeDtypeStruct((rows, inner), BF16),
            jax.ShapeDtypeStruct((tokens, width), F32),
        ),
        in_specs=[scalars, whole] + [anywhere] * 10,
        out_specs=(anywhere, anywhere, whole),
        scratch_shapes=[
            pltpu.VMEM((rows, inner), BF16),
            pltpu.VMEM((2, half, inner), BF16),
            pltpu.VMEM((4, rows, width), BF16),
            pltpu.VMEM((4, 2, half, width), BF16),
            pltpu.VMEM((tokens, width), BF16),
            pltpu.VMEM((tokens, width), BF16),
            pltpu.VMEM((width, inner), BF16),
            pltpu.VMEM((inner, width), BF16),
            pltpu.VMEM((8, rows, HD), BF16),
            pltpu.VMEM((8, rows, HD), BF16),
            pltpu.VMEM((8, half, HD), BF16),
            pltpu.VMEM((8, half, width), BF16),
            pltpu.VMEM((2 * inner, width), BF16),
            pltpu.VMEM((2, width, inner), BF16),
            pltpu.VMEM((2, width, inner), BF16),
            pltpu.VMEM((4, rows, 2 * inner), BF16),
            pltpu.VMEM((4, 2, rows, width), BF16),
            pltpu.VMEM((4, 1, rows), F32),
            pltpu.VMEM((4, 1, rows), F32),
            pltpu.VMEM((4, 1, rows), F32),
            pltpu.VMEM((4, 1, rows), F32),
            pltpu.VMEM((4, rows, inner), BF16),
            pltpu.VMEM((4, rows, inner), BF16),
            pltpu.VMEM((2, rows, inner), BF16),
            pltpu.VMEM((2, rows, inner), BF16),
            pltpu.VMEM((rows, inner), BF16),
            pltpu.VMEM((rows, inner), BF16),
            pltpu.VMEM((rows, inner), BF16),
            pltpu.VMEM((rows, inner), BF16),
            pltpu.VMEM((rows, inner), BF16),
            pltpu.VMEM((rows, inner), BF16),
            pltpu.VMEM((tokens, inner + 128), F32),
            pltpu.VMEM((8, share, inner + 128), F32),
            pltpu.VMEM((8, share, inner + 128), F32),
            pltpu.VMEM((8, share, inner), F32),
            pltpu.VMEM((tokens, inner), F32),
            pltpu.VMEM((tokens, inner + 128), F32),
            pltpu.VMEM((8, share, inner + 128), F32),
            pltpu.VMEM((8, share, inner + 128), F32),
            pltpu.VMEM((8, share, inner), F32),
            pltpu.VMEM((tokens, inner), F32),
            pltpu.VMEM((tokens, width), F32),
            pltpu.VMEM((tokens, width), F32),
            pltpu.VMEM((tokens, width), F32),
            dma, dma, dma, dma((8,)), dma((8,)), dma((8,)), dma, dma, dma((8,)), dma((8,)), dma((8,)),
            dma((8, 4)), dma((4,)), dma((4,)), dma((4,)),
            dma((2, 2)), dma((2,)), dma((2,)), dma((8,)), dma((8,)), dma, dma((13,)), dma((2,)),
        ],
        compiler_params=pltpu.CompilerParams(
            collective_id=0, has_side_effects=True, vmem_limit_bytes=60 * 1024 * 1024
        ),
    )(
        seq_length, gains, enc_query, enc_key, enc_value, enc_input, looked,
        cross_query_weight, attn_out_weight, cross_key_weight, cross_value_weight, cross_out_weight,
    )
    return pl.pallas_call(
        hand_kernel,
        out_shape=(
            jax.ShapeDtypeStruct((1, rows, inner), BF16),
            jax.ShapeDtypeStruct((1, rows, inner), BF16),
            jax.ShapeDtypeStruct((tokens // 2, 2, width), BF16),
        ),
        in_specs=[whole] * 3,
        out_specs=(whole, whole, whole),
    )(keys, values, decoded)


def chosen(*arrays):
    rows, inner = arrays[1].shape
    fits = lax.axis_size("ctx") == 8 and lax.axis_size("tp") == 2 and (rows, inner) == (128, 4 * HD)
    return (local_fused if fits else local)(*arrays)


def solution(mesh):
    placed = (
        P(("groups", "ctx"), None),
        P(("groups", "ctx"), "tp"),
        P(("groups", "ctx"), "tp"),
        P(("groups", "ctx"), "tp"),
        P("groups"),
        P("tp", None),
        P(),
        P("ctx", "tp"),
        P("ctx", "tp"),
        P("tp", "ctx"),
        P("groups", None),
        P("ctx"),
        P("ctx", "tp"),
        P("tp", "ctx"),
    )
    return jax.shard_map(
        chosen,
        mesh=mesh,
        in_specs=placed,
        out_specs=(
            P(("groups", "ctx"), None, "tp"),
            P(("groups", "ctx"), None, "tp"),
            P("groups", None, "ctx"),
        ),
        check_vma=False,
    )
```

```python
import math

import jax
import jax.numpy as jnp
from jax import lax
from jax.experimental import pallas as pl
from jax.experimental.pallas import tpu as pltpu
from jax.sharding import PartitionSpec as P

D = 4096
HD = 128


EPSILON = 1e-06
FLOOR = -1e30


def joined(value, axis, join):
    pieces = jax.tree.map(lambda part: lax.all_gather(part, axis), value)
    head = jax.tree.map(lambda part: part[0], pieces)
    tail = jax.tree.map(lambda part: part[1:], pieces)
    total, _ = lax.scan(lambda total, piece: (join(total, piece), None), head, tail)
    return total


def softmax_merge(first, second):
    top_first, total_first, mixed_first = first
    top_second, total_second, mixed_second = second
    top = jnp.maximum(top_first, top_second)
    weight_first = jnp.exp(top_first - top)
    weight_second = jnp.exp(top_second - top)
    total = total_first * weight_first + total_second * weight_second
    mixed = mixed_first * weight_first[..., None] + mixed_second * weight_second[..., None]
    return (top, total, mixed)


def partial_softmax(queries, keys, values, valid, factor):
    scores = jnp.einsum("qhd,khd->hqk", queries, keys, preferred_element_type=jnp.float32) * factor
    scores = jnp.where(valid[None, None, :], scores, FLOOR)
    top = jnp.max(scores, axis=-1)
    probs = jnp.where(valid[None, None, :], jnp.exp(scores - top[..., None]), 0.0)
    total = jnp.sum(probs, axis=-1)
    mixed = jnp.einsum(
        "hqk,khd->hqd", probs.astype(jnp.bfloat16), values, preferred_element_type=jnp.float32
    )
    return (top, total, mixed)


def norm_rows(resid, gain):
    scale = lax.rsqrt(jnp.mean(resid * resid, axis=-1, keepdims=True) + EPSILON)
    return (resid * scale * gain.astype(jnp.float32)).astype(jnp.bfloat16)


def local(
    enc_input,
    enc_query,
    enc_key,
    enc_value,
    seq_length,
    attn_out_weight,
    enc_gain,
    cross_key_weight,
    cross_value_weight,
    embed_table,
    dec_ids,
    dec_gain,
    cross_query_weight,
    cross_out_weight,
):
    rows, inner_local = enc_query.shape
    heads_local = inner_local // HD
    limit = seq_length[0]
    queries = enc_query.reshape(rows, heads_local, HD)
    start_state = (
        jnp.full((heads_local, rows), FLOOR, jnp.float32),
        jnp.zeros((heads_local, rows), jnp.float32),
        jnp.zeros((heads_local, rows, HD), jnp.float32),
    )
    carry = start_state
    key_rows = lax.all_gather(enc_key, "ctx", axis=0, tiled=True)
    value_rows = lax.all_gather(enc_value, "ctx", axis=0, tiled=True)
    count = key_rows.shape[0]
    block = math.gcd(count, 2048)
    blocks = count // block
    key_blocks = key_rows.reshape(blocks, block, heads_local, HD)
    value_blocks = value_rows.reshape(blocks, block, heads_local, HD)
    offsets = jnp.arange(blocks, dtype=jnp.int32) * block

    def one_block(state, item):
        key_block, value_block, offset = item
        positions = offset + jnp.arange(block, dtype=jnp.int32)
        update = partial_softmax(queries, key_block, value_block, positions < limit, HD ** (-0.5))
        return (softmax_merge(state, update), None)

    carry, unused = lax.scan(one_block, carry, (key_blocks, value_blocks, offsets))
    top, total, mixed = carry
    context = (
        jnp.transpose(mixed / total[..., None], (1, 0, 2))
        .reshape(rows, inner_local)
        .astype(jnp.bfloat16)
    )
    summed = lax.psum(jnp.dot(context, attn_out_weight, preferred_element_type=jnp.float32), "tp")
    memory = norm_rows(enc_input.astype(jnp.float32) + summed, enc_gain)
    ctx_count = lax.axis_size("ctx")
    slots = rows // ctx_count
    key_sum = jnp.dot(
        memory,
        lax.all_gather(cross_key_weight, "ctx", axis=0, tiled=True),
        preferred_element_type=jnp.float32,
    )
    value_sum = jnp.dot(
        memory,
        lax.all_gather(cross_value_weight, "ctx", axis=0, tiled=True),
        preferred_element_type=jnp.float32,
    )
    key_rows = key_sum.astype(jnp.bfloat16)
    value_rows = value_sum.astype(jnp.bfloat16)
    keys_moved, values_moved = (
        lax.all_to_all(
            key_rows.reshape(slots, ctx_count, inner_local),
            "ctx",
            split_axis=1,
            concat_axis=0,
            tiled=True,
        ),
        lax.all_to_all(
            value_rows.reshape(slots, ctx_count, inner_local),
            "ctx",
            split_axis=1,
            concat_axis=0,
            tiled=True,
        ),
    )
    keys_cache = keys_moved.reshape(rows, inner_local)
    values_cache = values_moved.reshape(rows, inner_local)
    beams = dec_ids.shape[0]
    vocab_local = embed_table.shape[0]
    flat_ids = dec_ids.reshape(-1) - lax.axis_index("tp") * vocab_local
    inside = (flat_ids >= 0) & (flat_ids < vocab_local)
    looked = jnp.take(embed_table, jnp.clip(flat_ids, 0, vocab_local - 1), axis=0)
    own_rows = jnp.where(inside[:, None], looked.astype(jnp.float32), 0.0)
    hidden = lax.psum(own_rows.astype(jnp.bfloat16), "tp").astype(jnp.float32)
    scaled = (hidden * dec_gain.astype(jnp.float32)).astype(jnp.bfloat16)
    raw_part = jnp.dot(scaled, cross_query_weight, preferred_element_type=jnp.float32)
    square_part = jnp.sum(hidden * hidden, axis=-1)
    raw, squares = lax.psum((raw_part, square_part), "ctx")
    factor = lax.rsqrt(squares / D + EPSILON)
    query = (raw * factor[:, None] * HD ** (-0.5)).astype(jnp.bfloat16).reshape(-1, heads_local, HD)
    positions = jnp.arange(rows, dtype=jnp.int32) * ctx_count + lax.axis_index("ctx")
    local_part = partial_softmax(
        query,
        keys_cache.reshape(rows, heads_local, HD),
        values_cache.reshape(rows, heads_local, HD),
        positions < limit,
        1.0,
    )
    top_all, total_all, mixed_all = joined(local_part, "ctx", softmax_merge)
    attn = (
        jnp.transpose(mixed_all / total_all[..., None], (1, 0, 2))
        .reshape(-1, inner_local)
        .astype(jnp.bfloat16)
    )
    out_part = jnp.dot(attn, cross_out_weight, preferred_element_type=jnp.float32)
    out = lax.psum(out_part, "tp")
    decoded = (out + hidden).astype(jnp.bfloat16).reshape(beams, 2, -1)
    return (keys_cache[None], values_cache[None], decoded)


MESH = pl.DeviceIdType.MESH
F32 = jnp.float32
BF16 = jnp.bfloat16
ORDER = (3, 0, 2, 1)


def pick_kernel(ids_ref, table_ref, out_ref, held, rows, sems):
    count = out_ref.shape[0]
    vocab_local = table_ref.shape[0]
    base = lax.axis_index("tp") * vocab_local
    copies = []
    for j in range(count):
        own = jnp.clip(ids_ref[j % 2, j // 2] - base, 0, vocab_local - 1)
        start = pl.multiple_of(lax.div(own, 16) * 16, 16)
        copy = pltpu.make_async_copy(table_ref.at[pl.ds(start, 16)], held.at[j], sems.at[j])
        copy.start()
        copies.append(copy)
    spots = lax.broadcasted_iota(jnp.int32, held.shape[1:], 0)
    for j in range(count):
        copies[j].wait()
        own = ids_ref[j % 2, j // 2] - base
        inside = (own >= 0) & (own < vocab_local)
        spot = jnp.where(inside, lax.rem(jnp.clip(own, 0, vocab_local - 1), 16), -1)
        block = held[j].astype(F32)
        rows[pl.ds(j, 1)] = jnp.sum(jnp.where(spots == spot, block, 0.0), axis=0, keepdims=True)
    out_ref[...] = rows[...].astype(BF16)


def hand_kernel(keys_ref, values_ref, decoded_ref, keys_out, values_out, decoded_out):
    keys_out[0] = keys_ref[...]
    values_out[0] = values_ref[...]
    for i in range(decoded_out.shape[0]):
        decoded_out[i] = decoded_ref[2 * i : 2 * i + 2].astype(BF16)


def fused_kernel(
    length, gains, q, k, v, ein, looked_hbm, wq, wo, wk, wv, wout,
    keys_out, values_out, decoded_out,
    q_own, q_turned, ein_own, ein_turned, looked, looked_far, wq_own, wout_own,
    kg, vg, qg, eg, wo_all, wk_all, wv_all, ctx_all, gained, square_own, square_far, square_sum, square_in,
    part_k, part_v, pair_k, pair_v, near_k, near_v, far_k, far_v, keys_own, values_own,
    raw_own, raw_out, raw_in, query_in, query_all, mix_own, mix_in, stat_own, stat_in, proj_out, proj_in, hidden_ref,
    send, r_look, r_wo, r_q, r_k, r_v, r_wk, r_wv, t_wk, t_wv, r_raw, r_query, r_ein, r_ctx, r_gained, r_square_far, r_square,
    r_pair, r_near, r_far, r_mix, r_stat, r_proj, fetched, stored,
):
    g = lax.axis_index("groups")
    c = lax.axis_index("ctx")
    t = lax.axis_index("tp")
    z, y = lax.div(c, 2), lax.rem(c, 2)
    mate, other = c + 1 - 2 * y, 1 - t
    line = [lax.rem(z + d, 4) for d in (2, 1, 3)]
    near_z = z + 1 - 2 * lax.rem(z, 2)
    across = 2 - 2 * lax.div(z, 2)
    across_middle = 2 - lax.div(z, 2)
    in_middle = (z == 1) | (z == 2)
    peers = [lax.rem(c + d, 8) for d in range(1, 8)]
    rows = q.shape[0]
    inner = q.shape[1]
    width = wq.shape[0]
    half = rows // 2
    each = rows // 8
    own_block = z * 2 + t
    heads = inner // HD
    pending = []

    def remote(source, target, arrival, to_ctx, to_tp):
        return pltpu.make_async_remote_copy(
            src_ref=source, dst_ref=target, send_sem=send, recv_sem=arrival,
            device_id={"ctx": to_ctx, "tp": to_tp}, device_id_type=MESH,
        )

    def put(source, target, arrival, to_ctx, to_tp):
        copy = remote(source, target, arrival, to_ctx, to_tp)
        copy.start()
        pending.append(copy)

    def put_twin(source, target, arrival):
        copy = pltpu.make_async_remote_copy(
            src_ref=source, dst_ref=target, send_sem=send, recv_sem=arrival,
            device_id={"groups": 1 - g, "ctx": c, "tp": t}, device_id_type=MESH,
        )
        copy.start()
        pending.append(copy)

    def got(target, arrival):
        remote(target, target, arrival, mate, t).wait_recv()

    def fetch(source, target, arrival):
        copy = pltpu.make_async_copy(source, target, arrival)
        copy.start()
        return copy

    def cols(index, size):
        return pl.ds(pl.multiple_of(index * size, size), size)

    barrier = pltpu.get_barrier_semaphore()
    for peer in peers:
        pl.semaphore_signal(barrier, inc=1, device_id={"ctx": peer, "tp": t}, device_id_type=MESH)
    pl.semaphore_signal(barrier, inc=1, device_id={"ctx": c, "tp": other}, device_id_type=MESH)
    pl.semaphore_signal(barrier, inc=1, device_id={"groups": 1 - g, "ctx": c, "tp": t}, device_id_type=MESH)

    q_fetch = fetch(q, q_own, fetched.at[0])
    k_fetch = fetch(k.at[:, cols(z, HD)], kg.at[c], fetched.at[1])
    v_fetch = fetch(v.at[:, cols(z, HD)], vg.at[c], fetched.at[2])
    ein_fetches = [
        fetch(ein.at[:, cols(far * 2 + t, width)], ein_own.at[far], fetched.at[3 + far]) for far in range(4)
    ]
    looked_fetch = fetch(looked_hbm, looked, fetched.at[7])
    wq_fetch = fetch(wq, wq_own, fetched.at[8])
    late = [
        fetch(wo.at[:, cols(own_block, width)], wo_all.at[cols(t, inner)], fetched.at[9]),
        fetch(wk, wk_all.at[y], fetched.at[10]),
        fetch(wv, wv_all.at[y], fetched.at[11]),
    ]
    wout_fetch = fetch(wout, wout_own, fetched.at[12])
    pl.semaphore_wait(barrier, len(peers) + 2)

    for far in line:
        to = far * 2 + y
        put(k.at[:, cols(far, HD)], kg.at[c], r_k.at[c], to, t)
        put(v.at[:, cols(far, HD)], vg.at[c], r_v.at[c], to, t)
    put(k.at[:, cols(z, HD)], kg.at[c], r_k.at[c], mate, t)
    put(v.at[:, cols(z, HD)], vg.at[c], r_v.at[c], mate, t)

    place = lax.broadcasted_iota(jnp.int32, (rows, rows), 0)
    spot = lax.broadcasted_iota(jnp.int32, (rows, rows), 1)
    side, rest = lax.div(place, half), lax.rem(place, half)
    turn = (spot == lax.rem(rest, each) * 8 + lax.div(rest, each) * 2 + side).astype(BF16)

    q_fetch.wait()
    turned = jnp.dot(turn, q_own[...], preferred_element_type=F32).astype(BF16)
    for s in range(2):
        q_turned[s] = turned[s * half : (s + 1) * half]
    for peer in peers:
        put(
            q_turned.at[lax.rem(peer, 2), :, cols(lax.div(peer, 2), HD)], qg.at[c], r_q.at[c], peer, t
        )
    qg[c] = q_turned[y, :, cols(z, HD)]
    put(wo.at[:, cols(z * 2 + other, width)], wo_all.at[cols(t, inner)], r_wo, c, other)
    piece = width // 4

    def weight_rows(index):
        return pl.ds(pl.multiple_of(index * piece, piece), piece)

    def send_weight(weight, whole, arrivals):
        for part in range(2):
            where = weight_rows(g * 2 + part)
            put(weight.at[where], whole.at[y, where], arrivals.at[part], mate, t)

    def relay_weight(whole, arrivals, twins):
        for part in range(2):
            where = weight_rows(g * 2 + part)
            here = whole.at[1 - y, where]
            got(here, arrivals.at[part])
            put_twin(here, here, twins.at[part])

    def whole_weight(whole, twins):
        for part in range(2):
            got(whole.at[1 - y, weight_rows((1 - g) * 2 + part)], twins.at[part])

    send_weight(wk, wk_all, r_wk)

    for far in range(4):
        ein_fetches[far].wait()
        turned = jnp.dot(turn, ein_own[far], preferred_element_type=F32).astype(BF16)
        for s in range(2):
            ein_turned[far, s] = turned[s * half : (s + 1) * half]

    for far in line:
        source = far * 2 + y
        got(kg.at[source], r_k.at[source])
        put(kg.at[source], kg.at[source], r_k.at[source], mate, t)
        got(vg.at[source], r_v.at[source])
        put(vg.at[source], vg.at[source], r_v.at[source], mate, t)
    for peer in peers:
        put(ein_turned.at[lax.div(peer, 2), lax.rem(peer, 2)], eg.at[c], r_ein.at[c], peer, t)
    eg[c] = ein_turned[z, y]
    send_weight(wv, wv_all, r_wv)
    relay_weight(wk_all, r_wk, t_wk)

    tokens = looked.shape[0]
    looked_fetch.wait()
    put(looked, looked_far, r_look, c, other)

    k_fetch.wait()
    v_fetch.wait()
    for peer in peers:
        got(qg.at[peer], r_q.at[peer])
    for far in range(4):
        source = far * 2 + 1 - y
        got(kg.at[source], r_k.at[source])
        got(vg.at[source], r_v.at[source])

    limit = length[0]
    every_key = kg[...].reshape(8 * rows, HD)
    every_value = vg[...].reshape(8 * rows, HD)
    valid = lax.broadcasted_iota(jnp.int32, (1, 8 * rows), 1) < limit

    def block_at(core, far, chunk):
        return ctx_all.at[chunk, :, cols(core * 4 + far, HD)], r_ctx.at[core * 4 + far, chunk]

    for chunk in ORDER:
        queries = qg[:, chunk * each : (chunk + 1) * each, :].reshape(rows, HD)
        scores = lax.dot_general(
            queries, every_key, (((1,), (1,)), ((), ())), preferred_element_type=F32
        ) * (HD ** (-0.5))
        scores = jnp.where(valid, scores, FLOOR)
        top = jnp.max(scores, axis=-1, keepdims=True)
        probs = jnp.where(valid, jnp.exp(scores - top), 0.0)
        total = jnp.sum(probs, axis=-1, keepdims=True)
        mixed = jnp.dot(probs.astype(BF16), every_value, preferred_element_type=F32)
        ctx_all[chunk, :, cols(t * 4 + z, HD)] = (mixed / total).astype(BF16)
        here, arrival = block_at(t, z, chunk)
        put(here, here, arrival, across_middle * 2 + y, t)
        put(here, here, arrival, near_z * 2 + y, t)
        put(here, here, arrival, c, other)

    got(looked_far, r_look)
    wq_fetch.wait()
    hidden = looked[...].astype(F32) + looked_far[...].astype(F32)
    hidden_ref[...] = hidden
    scaled = (hidden * gains[0:1]).astype(BF16)
    raw_own[:, :inner] = jnp.dot(scaled, wq_own[...], preferred_element_type=F32)
    raw_own[:, inner:] = jnp.broadcast_to(jnp.sum(hidden * hidden, axis=-1, keepdims=True), (tokens, 128))
    share = tokens // 8
    for j in range(8):
        raw_out[j] = raw_own[j * share : (j + 1) * share, :]
    for peer in peers:
        put(raw_out.at[peer], raw_in.at[c], r_raw.at[c], peer, t)
    raw_in[c] = raw_out[c]
    relay_weight(wv_all, r_wv, t_wv)

    for copy in late:
        copy.wait()
    got(wo_all.at[cols(other, inner)], r_wo)
    for peer in peers:
        got(eg.at[peer], r_ein.at[peer])
    picked_gain = lax.broadcasted_iota(jnp.int32, (8, width), 0) == own_block
    gain = jnp.sum(jnp.where(picked_gain, gains[8:16], 0.0), axis=0, keepdims=True)

    def relay(chunk):
        for far in (near_z, across, across + 1):
            here, arrival = block_at(t, far, chunk)
            got(here, arrival)
            if far is not near_z:

                @pl.when(in_middle)
                def _():
                    remote(here, here, arrival, near_z * 2 + y, t).start()

            put(here, here, arrival, c, other)

    def project(chunk):
        for far in range(4):
            got(*block_at(other, far, chunk))
        resid = jnp.dot(ctx_all[chunk], wo_all[...], preferred_element_type=F32)
        resid = resid + eg[:, chunk * each : (chunk + 1) * each, :].reshape(rows, width).astype(F32)
        spread = jnp.where(place == spot, jnp.sum(resid * resid, axis=-1, keepdims=True), 0.0)
        square_own[chunk] = jnp.sum(spread, axis=0, keepdims=True)
        gained[chunk, t] = (resid * gain).astype(BF16)
        put(gained.at[chunk, t], gained.at[chunk, t], r_gained.at[chunk], c, other)
        put(square_own.at[chunk], square_far.at[chunk], r_square_far.at[chunk], c, other)

    ways = ((part_k, pair_k, near_k, far_k, wk_all, t_wk), (part_v, pair_v, near_v, far_v, wv_all, t_wv))

    def start_only(source, target, arrival, to_z):
        remote(source, target, arrival, to_z * 2 + y, t).start()

    def spread_out(chunk, first):
        got(gained.at[chunk, other], r_gained.at[chunk])
        end = 0 if chunk >= 2 else 3
        for way, (part, pair, near, far, weight, arrival) in enumerate(ways):
            if first:
                whole_weight(weight, arrival)
            total = jnp.dot(gained[chunk, 0], weight[0], preferred_element_type=F32)
            total = total + jnp.dot(gained[chunk, 1], weight[1], preferred_element_type=F32)
            part[chunk] = total.astype(BF16)

            @pl.when(z == end)
            def _():
                start_only(
                    part.at[chunk], pair.at[chunk % 2], r_pair.at[way, chunk % 2], 1 if end == 0 else 2
                )

            @pl.when(z == (chunk + 1 if chunk % 2 == 0 else chunk - 1))
            def _():
                start_only(part.at[chunk], near, r_near.at[way], chunk)

    def join(chunk):
        middle = 1 if chunk >= 2 else 2
        for way, (part, pair, near, far, weight, arrival) in enumerate(ways):

            @pl.when(z == middle)
            def _():
                got(pair.at[chunk % 2], r_pair.at[way, chunk % 2])
                both = part[chunk].astype(F32) + pair[chunk % 2].astype(F32)
                pair[chunk % 2] = both.astype(BF16)
                start_only(pair.at[chunk % 2], far, r_far.at[way], chunk)

    relay(ORDER[0])
    relay(ORDER[1])
    project(ORDER[0])
    relay(ORDER[2])
    project(ORDER[1])
    spread_out(ORDER[0], True)
    relay(ORDER[3])
    project(ORDER[2])
    spread_out(ORDER[1], False)
    project(ORDER[3])
    spread_out(ORDER[2], False)
    spread_out(ORDER[3], False)
    for chunk in range(4):
        got(square_far.at[chunk], r_square_far.at[chunk])
        square_sum[chunk] = square_own[chunk] + square_far[chunk]
    for far in line:
        put(square_sum.at[far], square_in.at[z], r_square.at[z], far * 2 + y, t)
    square_in[z] = square_sum[z]

    join(ORDER[0])
    join(ORDER[1])
    for peer in peers:
        got(raw_in.at[peer], r_raw.at[peer])
    raw = raw_in[0]
    for j in range(1, 8):
        raw = raw + raw_in[j]
    factor = lax.rsqrt(raw[:, inner : inner + 1] / D + EPSILON)
    query_in[c] = (raw[:, :inner] * factor * HD ** (-0.5)).astype(BF16).astype(F32)
    for peer in peers:
        put(query_in.at[c], query_in.at[c], r_query.at[c], peer, t)
    join(ORDER[2])
    join(ORDER[3])

    for far in line:
        got(square_in.at[far], r_square.at[far])
    square = square_in[0] + square_in[1] + square_in[2] + square_in[3]
    column = jnp.sum(jnp.where(place == spot, square, 0.0), axis=-1, keepdims=True)
    scale = lax.rsqrt(column / D + EPSILON)
    for peer in peers:
        got(query_in.at[peer], r_query.at[peer])
    for j in range(8):
        query_all[j * share : (j + 1) * share, :] = query_in[j]

    stores = []
    for way, (own, out) in enumerate(((keys_own, keys_out), (values_own, values_out))):
        part, pair, near, far, weight, arrival = ways[way]
        got(near, r_near.at[way])
        got(far, r_far.at[way])
        total = part[z].astype(F32) + near[...].astype(F32) + far[...].astype(F32)
        own[...] = (total * scale).astype(BF16)
        stores.append(fetch(own, out, stored.at[way]))

    own_valid = lax.broadcasted_iota(jnp.int32, (1, rows), 1) * 8 + c < limit
    scores = jnp.concatenate(
        [
            lax.dot_general(
                query_all[:, h * HD : (h + 1) * HD].astype(BF16), keys_own[:, h * HD : (h + 1) * HD],
                (((1,), (1,)), ((), ())), preferred_element_type=F32,
            )
            for h in range(heads)
        ],
        axis=0,
    )
    scores = jnp.where(own_valid, scores, FLOOR)
    top = jnp.max(scores, axis=-1, keepdims=True)
    probs = jnp.where(own_valid, jnp.exp(scores - top), 0.0)
    total = jnp.sum(probs, axis=-1, keepdims=True)
    stat_own[0:1] = jnp.sum(jnp.where(place == spot, top, 0.0), axis=0, keepdims=True)
    stat_own[1:2] = jnp.sum(jnp.where(place == spot, total, 0.0), axis=0, keepdims=True)
    for h in range(heads):
        mix_own[h * tokens : (h + 1) * tokens] = jnp.dot(
            probs[h * tokens : (h + 1) * tokens].astype(BF16), values_own[:, h * HD : (h + 1) * HD],
            preferred_element_type=F32,
        ).astype(BF16)
    for peer in peers:
        put(stat_own, stat_in.at[c], r_stat.at[c], peer, t)
        put(mix_own, mix_in.at[c], r_mix.at[c], peer, t)
    stat_in[c] = stat_own[...]
    mix_in[c] = mix_own[...]
    wout_fetch.wait()
    for peer in peers:
        got(stat_in.at[peer], r_stat.at[peer])
    top = stat_in[0][0:1]
    for j in range(1, 8):
        top = jnp.maximum(top, stat_in[j][0:1])
    factors = [jnp.exp(stat_in[j][0:1] - top) for j in range(8)]
    total = factors[0] * stat_in[0][1:2]
    for j in range(1, 8):
        total = total + factors[j] * stat_in[j][1:2]
    for peer in peers:
        got(mix_in.at[peer], r_mix.at[peer])
    mixed = jnp.zeros((rows, HD), F32)
    for j in range(8):
        column = jnp.sum(jnp.where(place == spot, factors[j] / total, 0.0), axis=-1, keepdims=True)
        mixed = mixed + mix_in[j].astype(F32) * column
    attn = mixed.astype(BF16)
    proj = jnp.zeros(proj_out.shape, F32)
    for h in range(heads):
        proj = proj + jnp.dot(
            attn[h * tokens : (h + 1) * tokens], wout_own[h * HD : (h + 1) * HD], preferred_element_type=F32
        )
    proj_out[...] = proj
    put(proj_out, proj_in, r_proj, c, other)
    got(proj_in, r_proj)
    decoded_out[...] = proj_out[...] + proj_in[...] + hidden_ref[...]
    for copy in stores:
        copy.wait()
    for copy in pending:
        copy.wait_send()
    for i in range(6):
        remote(near_k, near_k, r_near.at[0], mate, t).wait_send()

    @pl.when(in_middle)
    def _():
        for i in range(8):
            remote(ctx_all.at[0, :, cols(z, HD)], ctx_all.at[0, :, cols(z, HD)], r_near.at[0], mate, t).wait_send()


def local_fused(
    enc_input, enc_query, enc_key, enc_value, seq_length, attn_out_weight, enc_gain, cross_key_weight,
    cross_value_weight, embed_table, dec_ids, dec_gain, cross_query_weight, cross_out_weight,
):
    rows, inner = enc_query.shape
    width = cross_query_weight.shape[0]
    tokens = dec_ids.size
    whole = pl.BlockSpec(memory_space=pltpu.VMEM)
    scalars = pl.BlockSpec(memory_space=pltpu.SMEM)
    anywhere = pl.BlockSpec(memory_space=pl.ANY)
    gains = jnp.concatenate(
        [jnp.broadcast_to(dec_gain[None], (8, width)), enc_gain.reshape(8, width)], axis=0
    ).astype(F32)
    dma = pltpu.SemaphoreType.DMA
    share = tokens // 8
    half = rows // 2
    looked = pl.pallas_call(
        pick_kernel,
        out_shape=jax.ShapeDtypeStruct((tokens, width), BF16),
        in_specs=[scalars, anywhere],
        out_specs=whole,
        scratch_shapes=[
            pltpu.VMEM((tokens, 16, width), BF16),
            pltpu.VMEM((tokens, width), F32),
            pltpu.SemaphoreType.DMA((tokens,)),
        ],
    )(dec_ids.T, embed_table)
    keys, values, decoded = pl.pallas_call(
        fused_kernel,
        out_shape=(
            jax.ShapeDtypeStruct((rows, inner), BF16),
            jax.ShapeDtypeStruct((rows, inner), BF16),
            jax.ShapeDtypeStruct((tokens, width), F32),
        ),
        in_specs=[scalars, whole] + [anywhere] * 10,
        out_specs=(anywhere, anywhere, whole),
        scratch_shapes=[
            pltpu.VMEM((rows, inner), BF16),
            pltpu.VMEM((2, half, inner), BF16),
            pltpu.VMEM((4, rows, width), BF16),
            pltpu.VMEM((4, 2, half, width), BF16),
            pltpu.VMEM((tokens, width), BF16),
            pltpu.VMEM((tokens, width), BF16),
            pltpu.VMEM((width, inner), BF16),
            pltpu.VMEM((inner, width), BF16),
            pltpu.VMEM((8, rows, HD), BF16),
            pltpu.VMEM((8, rows, HD), BF16),
            pltpu.VMEM((8, half, HD), BF16),
            pltpu.VMEM((8, half, width), BF16),
            pltpu.VMEM((2 * inner, width), BF16),
            pltpu.VMEM((2, width, inner), BF16),
            pltpu.VMEM((2, width, inner), BF16),
            pltpu.VMEM((4, rows, 2 * inner), BF16),
            pltpu.VMEM((4, 2, rows, width), BF16),
            pltpu.VMEM((4, 1, rows), F32),
            pltpu.VMEM((4, 1, rows), F32),
            pltpu.VMEM((4, 1, rows), F32),
            pltpu.VMEM((4, 1, rows), F32),
            pltpu.VMEM((4, rows, inner), BF16),
            pltpu.VMEM((4, rows, inner), BF16),
            pltpu.VMEM((2, rows, inner), BF16),
            pltpu.VMEM((2, rows, inner), BF16),
            pltpu.VMEM((rows, inner), BF16),
            pltpu.VMEM((rows, inner), BF16),
            pltpu.VMEM((rows, inner), BF16),
            pltpu.VMEM((rows, inner), BF16),
            pltpu.VMEM((rows, inner), BF16),
            pltpu.VMEM((rows, inner), BF16),
            pltpu.VMEM((tokens, inner + 128), F32),
            pltpu.VMEM((8, share, inner + 128), F32),
            pltpu.VMEM((8, share, inner + 128), F32),
            pltpu.VMEM((8, share, inner), F32),
            pltpu.VMEM((tokens, inner), F32),
            pltpu.VMEM((rows, HD), BF16),
            pltpu.VMEM((8, rows, HD), BF16),
            pltpu.VMEM((2, rows), F32),
            pltpu.VMEM((8, 2, rows), F32),
            pltpu.VMEM((tokens, width), F32),
            pltpu.VMEM((tokens, width), F32),
            pltpu.VMEM((tokens, width), F32),
            dma, dma, dma, dma((8,)), dma((8,)), dma((8,)), dma((2,)), dma((2,)), dma((2,)), dma((2,)), dma((8,)), dma((8,)), dma((8,)),
            dma((8, 4)), dma((4,)), dma((4,)), dma((4,)),
            dma((2, 2)), dma((2,)), dma((2,)), dma((8,)), dma((8,)), dma, dma((13,)), dma((2,)),
        ],
        compiler_params=pltpu.CompilerParams(
            collective_id=0, has_side_effects=True, vmem_limit_bytes=60 * 1024 * 1024
        ),
    )(
        seq_length, gains, enc_query, enc_key, enc_value, enc_input, looked,
        cross_query_weight, attn_out_weight, cross_key_weight, cross_value_weight, cross_out_weight,
    )
    return pl.pallas_call(
        hand_kernel,
        out_shape=(
            jax.ShapeDtypeStruct((1, rows, inner), BF16),
            jax.ShapeDtypeStruct((1, rows, inner), BF16),
            jax.ShapeDtypeStruct((tokens // 2, 2, width), BF16),
        ),
        in_specs=[whole] * 3,
        out_specs=(whole, whole, whole),
    )(keys, values, decoded)


def chosen(*arrays):
    rows, inner = arrays[1].shape
    fits = lax.axis_size("ctx") == 8 and lax.axis_size("tp") == 2 and (rows, inner) == (128, 4 * HD)
    return (local_fused if fits else local)(*arrays)


def solution(mesh):
    placed = (
        P(("groups", "ctx"), None),
        P(("groups", "ctx"), "tp"),
        P(("groups", "ctx"), "tp"),
        P(("groups", "ctx"), "tp"),
        P("groups"),
        P("tp", None),
        P(),
        P("ctx", "tp"),
        P("ctx", "tp"),
        P("tp", "ctx"),
        P("groups", None),
        P("ctx"),
        P("ctx", "tp"),
        P("tp", "ctx"),
    )
    return jax.shard_map(
        chosen,
        mesh=mesh,
        in_specs=placed,
        out_specs=(
            P(("groups", "ctx"), None, "tp"),
            P(("groups", "ctx"), None, "tp"),
            P("groups", None, "ctx"),
        ),
        check_vma=False,
    )
```

```python
import math

import jax
import jax.numpy as jnp
from jax import lax
from jax.experimental import pallas as pl
from jax.experimental.pallas import tpu as pltpu
from jax.sharding import PartitionSpec as P

D = 4096
HD = 128


EPSILON = 1e-06
FLOOR = -1e30


def joined(value, axis, join):
    pieces = jax.tree.map(lambda part: lax.all_gather(part, axis), value)
    head = jax.tree.map(lambda part: part[0], pieces)
    tail = jax.tree.map(lambda part: part[1:], pieces)
    total, _ = lax.scan(lambda total, piece: (join(total, piece), None), head, tail)
    return total


def softmax_merge(first, second):
    top_first, total_first, mixed_first = first
    top_second, total_second, mixed_second = second
    top = jnp.maximum(top_first, top_second)
    weight_first = jnp.exp(top_first - top)
    weight_second = jnp.exp(top_second - top)
    total = total_first * weight_first + total_second * weight_second
    mixed = mixed_first * weight_first[..., None] + mixed_second * weight_second[..., None]
    return (top, total, mixed)


def partial_softmax(queries, keys, values, valid, factor):
    scores = jnp.einsum("qhd,khd->hqk", queries, keys, preferred_element_type=jnp.float32) * factor
    scores = jnp.where(valid[None, None, :], scores, FLOOR)
    top = jnp.max(scores, axis=-1)
    probs = jnp.where(valid[None, None, :], jnp.exp(scores - top[..., None]), 0.0)
    total = jnp.sum(probs, axis=-1)
    mixed = jnp.einsum(
        "hqk,khd->hqd", probs.astype(jnp.bfloat16), values, preferred_element_type=jnp.float32
    )
    return (top, total, mixed)


def norm_rows(resid, gain):
    scale = lax.rsqrt(jnp.mean(resid * resid, axis=-1, keepdims=True) + EPSILON)
    return (resid * scale * gain.astype(jnp.float32)).astype(jnp.bfloat16)


def local(
    enc_input,
    enc_query,
    enc_key,
    enc_value,
    seq_length,
    attn_out_weight,
    enc_gain,
    cross_key_weight,
    cross_value_weight,
    embed_table,
    dec_ids,
    dec_gain,
    cross_query_weight,
    cross_out_weight,
):
    rows, inner_local = enc_query.shape
    heads_local = inner_local // HD
    limit = seq_length[0]
    queries = enc_query.reshape(rows, heads_local, HD)
    start_state = (
        jnp.full((heads_local, rows), FLOOR, jnp.float32),
        jnp.zeros((heads_local, rows), jnp.float32),
        jnp.zeros((heads_local, rows, HD), jnp.float32),
    )
    carry = start_state
    key_rows = lax.all_gather(enc_key, "ctx", axis=0, tiled=True)
    value_rows = lax.all_gather(enc_value, "ctx", axis=0, tiled=True)
    count = key_rows.shape[0]
    block = math.gcd(count, 2048)
    blocks = count // block
    key_blocks = key_rows.reshape(blocks, block, heads_local, HD)
    value_blocks = value_rows.reshape(blocks, block, heads_local, HD)
    offsets = jnp.arange(blocks, dtype=jnp.int32) * block

    def one_block(state, item):
        key_block, value_block, offset = item
        positions = offset + jnp.arange(block, dtype=jnp.int32)
        update = partial_softmax(queries, key_block, value_block, positions < limit, HD ** (-0.5))
        return (softmax_merge(state, update), None)

    carry, unused = lax.scan(one_block, carry, (key_blocks, value_blocks, offsets))
    top, total, mixed = carry
    context = (
        jnp.transpose(mixed / total[..., None], (1, 0, 2))
        .reshape(rows, inner_local)
        .astype(jnp.bfloat16)
    )
    summed = lax.psum(jnp.dot(context, attn_out_weight, preferred_element_type=jnp.float32), "tp")
    memory = norm_rows(enc_input.astype(jnp.float32) + summed, enc_gain)
    ctx_count = lax.axis_size("ctx")
    slots = rows // ctx_count
    key_sum = jnp.dot(
        memory,
        lax.all_gather(cross_key_weight, "ctx", axis=0, tiled=True),
        preferred_element_type=jnp.float32,
    )
    value_sum = jnp.dot(
        memory,
        lax.all_gather(cross_value_weight, "ctx", axis=0, tiled=True),
        preferred_element_type=jnp.float32,
    )
    key_rows = key_sum.astype(jnp.bfloat16)
    value_rows = value_sum.astype(jnp.bfloat16)
    keys_moved, values_moved = (
        lax.all_to_all(
            key_rows.reshape(slots, ctx_count, inner_local),
            "ctx",
            split_axis=1,
            concat_axis=0,
            tiled=True,
        ),
        lax.all_to_all(
            value_rows.reshape(slots, ctx_count, inner_local),
            "ctx",
            split_axis=1,
            concat_axis=0,
            tiled=True,
        ),
    )
    keys_cache = keys_moved.reshape(rows, inner_local)
    values_cache = values_moved.reshape(rows, inner_local)
    beams = dec_ids.shape[0]
    vocab_local = embed_table.shape[0]
    flat_ids = dec_ids.reshape(-1) - lax.axis_index("tp") * vocab_local
    inside = (flat_ids >= 0) & (flat_ids < vocab_local)
    looked = jnp.take(embed_table, jnp.clip(flat_ids, 0, vocab_local - 1), axis=0)
    own_rows = jnp.where(inside[:, None], looked.astype(jnp.float32), 0.0)
    hidden = lax.psum(own_rows.astype(jnp.bfloat16), "tp").astype(jnp.float32)
    scaled = (hidden * dec_gain.astype(jnp.float32)).astype(jnp.bfloat16)
    raw_part = jnp.dot(scaled, cross_query_weight, preferred_element_type=jnp.float32)
    square_part = jnp.sum(hidden * hidden, axis=-1)
    raw, squares = lax.psum((raw_part, square_part), "ctx")
    factor = lax.rsqrt(squares / D + EPSILON)
    query = (raw * factor[:, None] * HD ** (-0.5)).astype(jnp.bfloat16).reshape(-1, heads_local, HD)
    positions = jnp.arange(rows, dtype=jnp.int32) * ctx_count + lax.axis_index("ctx")
    local_part = partial_softmax(
        query,
        keys_cache.reshape(rows, heads_local, HD),
        values_cache.reshape(rows, heads_local, HD),
        positions < limit,
        1.0,
    )
    top_all, total_all, mixed_all = joined(local_part, "ctx", softmax_merge)
    attn = (
        jnp.transpose(mixed_all / total_all[..., None], (1, 0, 2))
        .reshape(-1, inner_local)
        .astype(jnp.bfloat16)
    )
    out_part = jnp.dot(attn, cross_out_weight, preferred_element_type=jnp.float32)
    out = lax.psum(out_part, "tp")
    decoded = (out + hidden).astype(jnp.bfloat16).reshape(beams, 2, -1)
    return (keys_cache[None], values_cache[None], decoded)


MESH = pl.DeviceIdType.MESH
F32 = jnp.float32
BF16 = jnp.bfloat16
ORDER = (3, 0, 2, 1)


def hand_kernel(keys_ref, values_ref, decoded_ref, keys_out, values_out, decoded_out):
    keys_out[0] = keys_ref[...]
    values_out[0] = values_ref[...]
    for i in range(decoded_out.shape[0]):
        decoded_out[i] = decoded_ref[2 * i : 2 * i + 2].astype(BF16)


def fused_kernel(
    ids, length, dec_gain, enc_gain, q, k, v, ein, table, wq, wo, wk, wv, wout,
    keys_out, values_out, decoded_out,
    q_own, q_turned, ein_own, ein_turned, table_own, rows_own, looked, looked_far, wq_own, wout_own,
    kg, vg, qg, eg, wo_all, wk_all, wv_all, ctx_all, gained, square_own, square_far, square_sum, square_in,
    part_k, part_v, pair_k, pair_v, near_k, near_v, far_k, far_v, keys_own, values_own,
    raw_own, raw_out, raw_in, query_in, query_all, mix_own, mix_in, stat_own, stat_in, proj_out, proj_in, hidden_ref,
    send, r_look, r_wo, r_q, r_k, r_v, r_wk, r_wv, t_wk, t_wv, r_raw, r_query, r_ein, r_ctx, r_gained, r_square_far, r_square,
    r_pair, r_near, r_far, r_mix, r_stat, r_proj, fetched, stored,
):
    g = lax.axis_index("groups")
    c = lax.axis_index("ctx")
    t = lax.axis_index("tp")
    z, y = lax.div(c, 2), lax.rem(c, 2)
    mate, other = c + 1 - 2 * y, 1 - t
    line = [lax.rem(z + d, 4) for d in (2, 1, 3)]
    near_z = z + 1 - 2 * lax.rem(z, 2)
    across = 2 - 2 * lax.div(z, 2)
    across_middle = 2 - lax.div(z, 2)
    in_middle = (z == 1) | (z == 2)
    peers = [lax.rem(c + d, 8) for d in range(1, 8)]
    rows = q.shape[0]
    inner = q.shape[1]
    width = wq.shape[0]
    half = rows // 2
    each = rows // 8
    own_block = z * 2 + t
    heads = inner // HD
    pending = []

    def remote(source, target, arrival, to_ctx, to_tp):
        return pltpu.make_async_remote_copy(
            src_ref=source, dst_ref=target, send_sem=send, recv_sem=arrival,
            device_id={"ctx": to_ctx, "tp": to_tp}, device_id_type=MESH,
        )

    def put(source, target, arrival, to_ctx, to_tp):
        copy = remote(source, target, arrival, to_ctx, to_tp)
        copy.start()
        pending.append(copy)

    def put_twin(source, target, arrival):
        copy = pltpu.make_async_remote_copy(
            src_ref=source, dst_ref=target, send_sem=send, recv_sem=arrival,
            device_id={"groups": 1 - g, "ctx": c, "tp": t}, device_id_type=MESH,
        )
        copy.start()
        pending.append(copy)

    def got(target, arrival):
        remote(target, target, arrival, mate, t).wait_recv()

    def fetch(source, target, arrival):
        copy = pltpu.make_async_copy(source, target, arrival)
        copy.start()
        return copy

    def cols(index, size):
        return pl.ds(pl.multiple_of(index * size, size), size)

    barrier = pltpu.get_barrier_semaphore()
    for peer in peers:
        pl.semaphore_signal(barrier, inc=1, device_id={"ctx": peer, "tp": t}, device_id_type=MESH)
    pl.semaphore_signal(barrier, inc=1, device_id={"ctx": c, "tp": other}, device_id_type=MESH)
    pl.semaphore_signal(barrier, inc=1, device_id={"groups": 1 - g, "ctx": c, "tp": t}, device_id_type=MESH)

    q_fetch = fetch(q, q_own, fetched.at[0])
    k_fetch = fetch(k.at[:, cols(z, HD)], kg.at[c], fetched.at[1])
    v_fetch = fetch(v.at[:, cols(z, HD)], vg.at[c], fetched.at[2])
    ein_fetches = [
        fetch(ein.at[:, cols(far * 2 + t, width)], ein_own.at[far], fetched.at[3 + far]) for far in range(4)
    ]
    table_fetch = fetch(table, table_own, fetched.at[7])
    wq_fetch = fetch(wq, wq_own, fetched.at[8])
    late = [
        fetch(wo.at[:, cols(own_block, width)], wo_all.at[cols(t, inner)], fetched.at[9]),
        fetch(wk, wk_all.at[y], fetched.at[10]),
        fetch(wv, wv_all.at[y], fetched.at[11]),
    ]
    wout_fetch = fetch(wout, wout_own, fetched.at[12])
    pl.semaphore_wait(barrier, len(peers) + 2)

    for far in line:
        to = far * 2 + y
        put(k.at[:, cols(far, HD)], kg.at[c], r_k.at[c], to, t)
        put(v.at[:, cols(far, HD)], vg.at[c], r_v.at[c], to, t)
    put(k.at[:, cols(z, HD)], kg.at[c], r_k.at[c], mate, t)
    put(v.at[:, cols(z, HD)], vg.at[c], r_v.at[c], mate, t)

    place = lax.broadcasted_iota(jnp.int32, (rows, rows), 0)
    spot = lax.broadcasted_iota(jnp.int32, (rows, rows), 1)
    side, rest = lax.div(place, half), lax.rem(place, half)
    turn = (spot == lax.rem(rest, each) * 8 + lax.div(rest, each) * 2 + side).astype(BF16)

    q_fetch.wait()
    turned = jnp.dot(turn, q_own[...], preferred_element_type=F32).astype(BF16)
    for s in range(2):
        q_turned[s] = turned[s * half : (s + 1) * half]
    for peer in peers:
        put(
            q_turned.at[lax.rem(peer, 2), :, cols(lax.div(peer, 2), HD)], qg.at[c], r_q.at[c], peer, t
        )
    qg[c] = q_turned[y, :, cols(z, HD)]
    put(wo.at[:, cols(z * 2 + other, width)], wo_all.at[cols(t, inner)], r_wo, c, other)
    piece = width // 4

    def weight_rows(index):
        return pl.ds(pl.multiple_of(index * piece, piece), piece)

    def send_weight(weight, whole, arrivals):
        for part in range(2):
            where = weight_rows(g * 2 + part)
            put(weight.at[where], whole.at[y, where], arrivals.at[part], mate, t)

    def relay_weight(whole, arrivals, twins):
        for part in range(2):
            where = weight_rows(g * 2 + part)
            here = whole.at[1 - y, where]
            got(here, arrivals.at[part])
            put_twin(here, here, twins.at[part])

    def whole_weight(whole, twins):
        for part in range(2):
            got(whole.at[1 - y, weight_rows((1 - g) * 2 + part)], twins.at[part])

    send_weight(wk, wk_all, r_wk)

    tokens = looked.shape[0]
    for far in range(4):
        ein_fetches[far].wait()
        turned = jnp.dot(turn, ein_own[far], preferred_element_type=F32).astype(BF16)
        for s in range(2):
            ein_turned[far, s] = turned[s * half : (s + 1) * half]

    for peer in peers:
        put(ein_turned.at[lax.div(peer, 2), lax.rem(peer, 2)], eg.at[c], r_ein.at[c], peer, t)
    eg[c] = ein_turned[z, y]
    for far in line:
        source = far * 2 + y
        got(kg.at[source], r_k.at[source])
        put(kg.at[source], kg.at[source], r_k.at[source], mate, t)
        got(vg.at[source], r_v.at[source])
        put(vg.at[source], vg.at[source], r_v.at[source], mate, t)
    send_weight(wv, wv_all, r_wv)
    relay_weight(wk_all, r_wk, t_wk)

    table_fetch.wait()
    first = t * table.shape[0] * 16
    spots = lax.broadcasted_iota(jnp.int32, (16, width), 0)
    for j in range(tokens):
        own = ids[j % 2, j // 2] - first
        near = jnp.clip(own, 0, table.shape[0] * 16 - 1)
        block = table_own[lax.div(near, 16)].astype(F32)
        picked = spots + lax.div(near, 16) * 16 == own
        rows_own[j : j + 1] = jnp.sum(jnp.where(picked, block, 0.0), axis=0, keepdims=True)
    looked[...] = rows_own[...].astype(BF16)
    put(looked, looked_far, r_look, c, other)
    got(looked_far, r_look)
    wq_fetch.wait()
    hidden = looked[...].astype(F32) + looked_far[...].astype(F32)
    hidden_ref[...] = hidden
    scaled = (hidden * dec_gain[...].astype(F32).reshape(1, width)).astype(BF16)
    raw_own[:, :inner] = jnp.dot(scaled, wq_own[...], preferred_element_type=F32)
    raw_own[:, inner:] = jnp.broadcast_to(jnp.sum(hidden * hidden, axis=-1, keepdims=True), (tokens, 128))
    share = tokens // 8
    for j in range(8):
        raw_out[j] = raw_own[j * share : (j + 1) * share, :]
    for peer in peers:
        put(raw_out.at[peer], raw_in.at[c], r_raw.at[c], peer, t)
    raw_in[c] = raw_out[c]

    k_fetch.wait()
    v_fetch.wait()
    for peer in peers:
        got(qg.at[peer], r_q.at[peer])
    for far in range(4):
        source = far * 2 + 1 - y
        got(kg.at[source], r_k.at[source])
        got(vg.at[source], r_v.at[source])

    limit = length[0]
    every_key = kg[...].reshape(8 * rows, HD)
    every_value = vg[...].reshape(8 * rows, HD)
    valid = lax.broadcasted_iota(jnp.int32, (1, 8 * rows), 1) < limit

    def block_at(core, far, chunk):
        return ctx_all.at[chunk, :, cols(core * 4 + far, HD)], r_ctx.at[core * 4 + far, chunk]

    for chunk in ORDER:
        queries = qg[:, chunk * each : (chunk + 1) * each, :].reshape(rows, HD)
        scores = lax.dot_general(
            queries, every_key, (((1,), (1,)), ((), ())), preferred_element_type=F32
        ) * (HD ** (-0.5))
        scores = jnp.where(valid, scores, FLOOR)
        top = jnp.max(scores, axis=-1, keepdims=True)
        probs = jnp.where(valid, jnp.exp(scores - top), 0.0)
        total = jnp.sum(probs, axis=-1, keepdims=True)
        mixed = jnp.dot(probs.astype(BF16), every_value, preferred_element_type=F32)
        ctx_all[chunk, :, cols(t * 4 + z, HD)] = (mixed / total).astype(BF16)
        here, arrival = block_at(t, z, chunk)
        put(here, here, arrival, across_middle * 2 + y, t)
        put(here, here, arrival, near_z * 2 + y, t)
        put(here, here, arrival, c, other)

    relay_weight(wv_all, r_wv, t_wv)

    for copy in late:
        copy.wait()
    got(wo_all.at[cols(other, inner)], r_wo)
    for peer in peers:
        got(eg.at[peer], r_ein.at[peer])
    gain = enc_gain[cols(own_block, width)].astype(F32).reshape(1, width)

    def relay(chunk):
        for far in (near_z, across, across + 1):
            here, arrival = block_at(t, far, chunk)
            got(here, arrival)
            if far is not near_z:

                @pl.when(in_middle)
                def _():
                    remote(here, here, arrival, near_z * 2 + y, t).start()

            put(here, here, arrival, c, other)

    def project(chunk):
        for far in range(4):
            got(*block_at(other, far, chunk))
        resid = jnp.dot(ctx_all[chunk], wo_all[...], preferred_element_type=F32)
        resid = resid + eg[:, chunk * each : (chunk + 1) * each, :].reshape(rows, width).astype(F32)
        spread = jnp.where(place == spot, jnp.sum(resid * resid, axis=-1, keepdims=True), 0.0)
        square_own[chunk] = jnp.sum(spread, axis=0, keepdims=True)
        gained[chunk, t] = (resid * gain).astype(BF16)
        put(gained.at[chunk, t], gained.at[chunk, t], r_gained.at[chunk], c, other)
        put(square_own.at[chunk], square_far.at[chunk], r_square_far.at[chunk], c, other)

    ways = ((part_k, pair_k, near_k, far_k, wk_all, t_wk), (part_v, pair_v, near_v, far_v, wv_all, t_wv))

    def start_only(source, target, arrival, to_z):
        remote(source, target, arrival, to_z * 2 + y, t).start()

    def spread_out(chunk, first):
        got(gained.at[chunk, other], r_gained.at[chunk])
        end = 0 if chunk >= 2 else 3
        for way, (part, pair, near, far, weight, arrival) in enumerate(ways):
            if first:
                whole_weight(weight, arrival)
            total = jnp.dot(gained[chunk, 0], weight[0], preferred_element_type=F32)
            total = total + jnp.dot(gained[chunk, 1], weight[1], preferred_element_type=F32)
            part[chunk] = total.astype(BF16)

            @pl.when(z == end)
            def _():
                start_only(
                    part.at[chunk], pair.at[chunk % 2], r_pair.at[way, chunk % 2], 1 if end == 0 else 2
                )

            if chunk in (0, 3):

                @pl.when(z == (1 if chunk == 0 else 2))
                def _():
                    start_only(part.at[chunk], near, r_near.at[way], chunk)

    def last_near():
        for way, (part, pair, near, far, weight, arrival) in enumerate(ways):

            @pl.when((z == 0) | (z == 3))
            def _():
                start_only(part.at[near_z], near, r_near.at[way], near_z)

    def join(chunk):
        middle = 1 if chunk >= 2 else 2
        for way, (part, pair, near, far, weight, arrival) in enumerate(ways):

            @pl.when(z == middle)
            def _():
                got(pair.at[chunk % 2], r_pair.at[way, chunk % 2])
                both = part[chunk].astype(F32) + pair[chunk % 2].astype(F32)
                pair[chunk % 2] = both.astype(BF16)
                start_only(pair.at[chunk % 2], far, r_far.at[way], chunk)

    relay(ORDER[0])
    relay(ORDER[1])
    project(ORDER[0])
    relay(ORDER[2])
    spread_out(ORDER[0], True)
    project(ORDER[1])
    relay(ORDER[3])
    spread_out(ORDER[1], False)
    project(ORDER[2])
    spread_out(ORDER[2], False)
    project(ORDER[3])
    spread_out(ORDER[3], False)
    last_near()
    for chunk in range(4):
        got(square_far.at[chunk], r_square_far.at[chunk])
        square_sum[chunk] = square_own[chunk] + square_far[chunk]
    for far in line:
        put(square_sum.at[far], square_in.at[z], r_square.at[z], far * 2 + y, t)
    square_in[z] = square_sum[z]

    join(ORDER[0])
    join(ORDER[1])
    for peer in peers:
        got(raw_in.at[peer], r_raw.at[peer])
    raw = raw_in[0]
    for j in range(1, 8):
        raw = raw + raw_in[j]
    factor = lax.rsqrt(raw[:, inner : inner + 1] / D + EPSILON)
    query_in[c] = (raw[:, :inner] * factor * HD ** (-0.5)).astype(BF16).astype(F32)
    for peer in peers:
        put(query_in.at[c], query_in.at[c], r_query.at[c], peer, t)
    join(ORDER[2])
    join(ORDER[3])

    for far in line:
        got(square_in.at[far], r_square.at[far])
    square = square_in[0] + square_in[1] + square_in[2] + square_in[3]
    column = jnp.sum(jnp.where(place == spot, square, 0.0), axis=-1, keepdims=True)
    scale = lax.rsqrt(column / D + EPSILON)
    for peer in peers:
        got(query_in.at[peer], r_query.at[peer])
    for j in range(8):
        query_all[j * share : (j + 1) * share, :] = query_in[j]

    stores = []

    def settle(way, own, out):
        part, pair, near, far, weight, arrival = ways[way]
        got(far, r_far.at[way])
        got(near, r_near.at[way])
        total = part[z].astype(F32) + near[...].astype(F32) + far[...].astype(F32)
        own[...] = (total * scale).astype(BF16)
        stores.append(fetch(own, out, stored.at[way]))

    settle(0, keys_own, keys_out)
    own_valid = lax.broadcasted_iota(jnp.int32, (1, rows), 1) * 8 + c < limit
    scores = jnp.concatenate(
        [
            lax.dot_general(
                query_all[:, h * HD : (h + 1) * HD].astype(BF16), keys_own[:, h * HD : (h + 1) * HD],
                (((1,), (1,)), ((), ())), preferred_element_type=F32,
            )
            for h in range(heads)
        ],
        axis=0,
    )
    scores = jnp.where(own_valid, scores, FLOOR)
    top = jnp.max(scores, axis=-1, keepdims=True)
    probs = jnp.where(own_valid, jnp.exp(scores - top), 0.0)
    total = jnp.sum(probs, axis=-1, keepdims=True)
    stat_own[0:1] = jnp.sum(jnp.where(place == spot, top, 0.0), axis=0, keepdims=True)
    stat_own[1:2] = jnp.sum(jnp.where(place == spot, total, 0.0), axis=0, keepdims=True)
    for peer in peers:
        put(stat_own, stat_in.at[c], r_stat.at[c], peer, t)
    settle(1, values_own, values_out)
    for h in range(heads):
        mix_own[h * tokens : (h + 1) * tokens] = jnp.dot(
            probs[h * tokens : (h + 1) * tokens].astype(BF16), values_own[:, h * HD : (h + 1) * HD],
            preferred_element_type=F32,
        ).astype(BF16)
    for peer in peers:
        put(mix_own, mix_in.at[c], r_mix.at[c], peer, t)
    stat_in[c] = stat_own[...]
    mix_in[c] = mix_own[...]
    wout_fetch.wait()
    for peer in peers:
        got(stat_in.at[peer], r_stat.at[peer])
    top = stat_in[0][0:1]
    for j in range(1, 8):
        top = jnp.maximum(top, stat_in[j][0:1])
    factors = [jnp.exp(stat_in[j][0:1] - top) for j in range(8)]
    total = factors[0] * stat_in[0][1:2]
    for j in range(1, 8):
        total = total + factors[j] * stat_in[j][1:2]
    for peer in peers:
        got(mix_in.at[peer], r_mix.at[peer])
    mixed = jnp.zeros((rows, HD), F32)
    for j in range(8):
        column = jnp.sum(jnp.where(place == spot, factors[j] / total, 0.0), axis=-1, keepdims=True)
        mixed = mixed + mix_in[j].astype(F32) * column
    attn = mixed.astype(BF16)
    proj = jnp.zeros(proj_out.shape, F32)
    for h in range(heads):
        proj = proj + jnp.dot(
            attn[h * tokens : (h + 1) * tokens], wout_own[h * HD : (h + 1) * HD], preferred_element_type=F32
        )
    proj_out[...] = proj
    put(proj_out, proj_in, r_proj, c, other)
    got(proj_in, r_proj)
    decoded_out[...] = proj_out[...] + proj_in[...] + hidden_ref[...]
    for copy in stores:
        copy.wait()
    for copy in pending:
        copy.wait_send()
    for i in range(6):
        remote(near_k, near_k, r_near.at[0], mate, t).wait_send()

    @pl.when(in_middle)
    def _():
        for i in range(8):
            remote(ctx_all.at[0, :, cols(z, HD)], ctx_all.at[0, :, cols(z, HD)], r_near.at[0], mate, t).wait_send()


def local_fused(
    enc_input, enc_query, enc_key, enc_value, seq_length, attn_out_weight, enc_gain, cross_key_weight,
    cross_value_weight, embed_table, dec_ids, dec_gain, cross_query_weight, cross_out_weight,
):
    rows, inner = enc_query.shape
    width = cross_query_weight.shape[0]
    tokens = dec_ids.size
    whole = pl.BlockSpec(memory_space=pltpu.VMEM)
    scalars = pl.BlockSpec(memory_space=pltpu.SMEM)
    anywhere = pl.BlockSpec(memory_space=pl.ANY)
    dma = pltpu.SemaphoreType.DMA
    share = tokens // 8
    half = rows // 2
    keys, values, decoded = pl.pallas_call(
        fused_kernel,
        out_shape=(
            jax.ShapeDtypeStruct((rows, inner), BF16),
            jax.ShapeDtypeStruct((rows, inner), BF16),
            jax.ShapeDtypeStruct((tokens, width), F32),
        ),
        in_specs=[scalars, scalars, whole, whole] + [anywhere] * 10,
        out_specs=(anywhere, anywhere, whole),
        scratch_shapes=[
            pltpu.VMEM((rows, inner), BF16),
            pltpu.VMEM((2, half, inner), BF16),
            pltpu.VMEM((4, rows, width), BF16),
            pltpu.VMEM((4, 2, half, width), BF16),
            pltpu.VMEM((embed_table.shape[0] // 16, 16, width), BF16),
            pltpu.VMEM((tokens, width), F32),
            pltpu.VMEM((tokens, width), BF16),
            pltpu.VMEM((tokens, width), BF16),
            pltpu.VMEM((width, inner), BF16),
            pltpu.VMEM((inner, width), BF16),
            pltpu.VMEM((8, rows, HD), BF16),
            pltpu.VMEM((8, rows, HD), BF16),
            pltpu.VMEM((8, half, HD), BF16),
            pltpu.VMEM((8, half, width), BF16),
            pltpu.VMEM((2 * inner, width), BF16),
            pltpu.VMEM((2, width, inner), BF16),
            pltpu.VMEM((2, width, inner), BF16),
            pltpu.VMEM((4, rows, 2 * inner), BF16),
            pltpu.VMEM((4, 2, rows, width), BF16),
            pltpu.VMEM((4, 1, rows), F32),
            pltpu.VMEM((4, 1, rows), F32),
            pltpu.VMEM((4, 1, rows), F32),
            pltpu.VMEM((4, 1, rows), F32),
            pltpu.VMEM((4, rows, inner), BF16),
            pltpu.VMEM((4, rows, inner), BF16),
            pltpu.VMEM((2, rows, inner), BF16),
            pltpu.VMEM((2, rows, inner), BF16),
            pltpu.VMEM((rows, inner), BF16),
            pltpu.VMEM((rows, inner), BF16),
            pltpu.VMEM((rows, inner), BF16),
            pltpu.VMEM((rows, inner), BF16),
            pltpu.VMEM((rows, inner), BF16),
            pltpu.VMEM((rows, inner), BF16),
            pltpu.VMEM((tokens, inner + 128), F32),
            pltpu.VMEM((8, share, inner + 128), F32),
            pltpu.VMEM((8, share, inner + 128), F32),
            pltpu.VMEM((8, share, inner), F32),
            pltpu.VMEM((tokens, inner), F32),
            pltpu.VMEM((rows, HD), BF16),
            pltpu.VMEM((8, rows, HD), BF16),
            pltpu.VMEM((2, rows), F32),
            pltpu.VMEM((8, 2, rows), F32),
            pltpu.VMEM((tokens, width), F32),
            pltpu.VMEM((tokens, width), F32),
            pltpu.VMEM((tokens, width), F32),
            dma, dma, dma, dma((8,)), dma((8,)), dma((8,)), dma((2,)), dma((2,)), dma((2,)), dma((2,)), dma((8,)), dma((8,)), dma((8,)),
            dma((8, 4)), dma((4,)), dma((4,)), dma((4,)),
            dma((2, 2)), dma((2,)), dma((2,)), dma((8,)), dma((8,)), dma, dma((13,)), dma((2,)),
        ],
        compiler_params=pltpu.CompilerParams(
            collective_id=0, has_side_effects=True, vmem_limit_bytes=60 * 1024 * 1024
        ),
    )(
        dec_ids.T, seq_length, dec_gain, enc_gain, enc_query, enc_key, enc_value, enc_input,
        embed_table.reshape(embed_table.shape[0] // 16, 16, width),
        cross_query_weight, attn_out_weight, cross_key_weight, cross_value_weight, cross_out_weight,
    )
    return pl.pallas_call(
        hand_kernel,
        out_shape=(
            jax.ShapeDtypeStruct((1, rows, inner), BF16),
            jax.ShapeDtypeStruct((1, rows, inner), BF16),
            jax.ShapeDtypeStruct((tokens // 2, 2, width), BF16),
        ),
        in_specs=[whole] * 3,
        out_specs=(whole, whole, whole),
    )(keys, values, decoded)


def chosen(*arrays):
    rows, inner = arrays[1].shape
    fits = lax.axis_size("ctx") == 8 and lax.axis_size("tp") == 2 and (rows, inner) == (128, 4 * HD)
    fits = fits and arrays[9].shape[0] % 16 == 0
    return (local_fused if fits else local)(*arrays)


def solution(mesh):
    placed = (
        P(("groups", "ctx"), None),
        P(("groups", "ctx"), "tp"),
        P(("groups", "ctx"), "tp"),
        P(("groups", "ctx"), "tp"),
        P("groups"),
        P("tp", None),
        P(),
        P("ctx", "tp"),
        P("ctx", "tp"),
        P("tp", "ctx"),
        P("groups", None),
        P("ctx"),
        P("ctx", "tp"),
        P("tp", "ctx"),
    )
    return jax.shard_map(
        chosen,
        mesh=mesh,
        in_specs=placed,
        out_specs=(
            P(("groups", "ctx"), None, "tp"),
            P(("groups", "ctx"), None, "tp"),
            P("groups", None, "ctx"),
        ),
        check_vma=False,
    )
```

```python
import math

import jax
import jax.numpy as jnp
from jax import lax
from jax.experimental import pallas as pl
from jax.experimental.pallas import tpu as pltpu
from jax.sharding import PartitionSpec as P

D = 4096
HD = 128


EPSILON = 1e-06
FLOOR = -1e30


def joined(value, axis, join):
    pieces = jax.tree.map(lambda part: lax.all_gather(part, axis), value)
    head = jax.tree.map(lambda part: part[0], pieces)
    tail = jax.tree.map(lambda part: part[1:], pieces)
    total, _ = lax.scan(lambda total, piece: (join(total, piece), None), head, tail)
    return total


def softmax_merge(first, second):
    top_first, total_first, mixed_first = first
    top_second, total_second, mixed_second = second
    top = jnp.maximum(top_first, top_second)
    weight_first = jnp.exp(top_first - top)
    weight_second = jnp.exp(top_second - top)
    total = total_first * weight_first + total_second * weight_second
    mixed = mixed_first * weight_first[..., None] + mixed_second * weight_second[..., None]
    return (top, total, mixed)


def partial_softmax(queries, keys, values, valid, factor):
    scores = jnp.einsum("qhd,khd->hqk", queries, keys, preferred_element_type=jnp.float32) * factor
    scores = jnp.where(valid[None, None, :], scores, FLOOR)
    top = jnp.max(scores, axis=-1)
    probs = jnp.where(valid[None, None, :], jnp.exp(scores - top[..., None]), 0.0)
    total = jnp.sum(probs, axis=-1)
    mixed = jnp.einsum(
        "hqk,khd->hqd", probs.astype(jnp.bfloat16), values, preferred_element_type=jnp.float32
    )
    return (top, total, mixed)


def norm_rows(resid, gain):
    scale = lax.rsqrt(jnp.mean(resid * resid, axis=-1, keepdims=True) + EPSILON)
    return (resid * scale * gain.astype(jnp.float32)).astype(jnp.bfloat16)


def local(
    enc_input,
    enc_query,
    enc_key,
    enc_value,
    seq_length,
    attn_out_weight,
    enc_gain,
    cross_key_weight,
    cross_value_weight,
    embed_table,
    dec_ids,
    dec_gain,
    cross_query_weight,
    cross_out_weight,
):
    rows, inner_local = enc_query.shape
    heads_local = inner_local // HD
    limit = seq_length[0]
    queries = enc_query.reshape(rows, heads_local, HD)
    start_state = (
        jnp.full((heads_local, rows), FLOOR, jnp.float32),
        jnp.zeros((heads_local, rows), jnp.float32),
        jnp.zeros((heads_local, rows, HD), jnp.float32),
    )
    carry = start_state
    key_rows = lax.all_gather(enc_key, "ctx", axis=0, tiled=True)
    value_rows = lax.all_gather(enc_value, "ctx", axis=0, tiled=True)
    count = key_rows.shape[0]
    block = math.gcd(count, 2048)
    blocks = count // block
    key_blocks = key_rows.reshape(blocks, block, heads_local, HD)
    value_blocks = value_rows.reshape(blocks, block, heads_local, HD)
    offsets = jnp.arange(blocks, dtype=jnp.int32) * block

    def one_block(state, item):
        key_block, value_block, offset = item
        positions = offset + jnp.arange(block, dtype=jnp.int32)
        update = partial_softmax(queries, key_block, value_block, positions < limit, HD ** (-0.5))
        return (softmax_merge(state, update), None)

    carry, unused = lax.scan(one_block, carry, (key_blocks, value_blocks, offsets))
    top, total, mixed = carry
    context = (
        jnp.transpose(mixed / total[..., None], (1, 0, 2))
        .reshape(rows, inner_local)
        .astype(jnp.bfloat16)
    )
    summed = lax.psum(jnp.dot(context, attn_out_weight, preferred_element_type=jnp.float32), "tp")
    memory = norm_rows(enc_input.astype(jnp.float32) + summed, enc_gain)
    ctx_count = lax.axis_size("ctx")
    slots = rows // ctx_count
    key_sum = jnp.dot(
        memory,
        lax.all_gather(cross_key_weight, "ctx", axis=0, tiled=True),
        preferred_element_type=jnp.float32,
    )
    value_sum = jnp.dot(
        memory,
        lax.all_gather(cross_value_weight, "ctx", axis=0, tiled=True),
        preferred_element_type=jnp.float32,
    )
    key_rows = key_sum.astype(jnp.bfloat16)
    value_rows = value_sum.astype(jnp.bfloat16)
    keys_moved, values_moved = (
        lax.all_to_all(
            key_rows.reshape(slots, ctx_count, inner_local),
            "ctx",
            split_axis=1,
            concat_axis=0,
            tiled=True,
        ),
        lax.all_to_all(
            value_rows.reshape(slots, ctx_count, inner_local),
            "ctx",
            split_axis=1,
            concat_axis=0,
            tiled=True,
        ),
    )
    keys_cache = keys_moved.reshape(rows, inner_local)
    values_cache = values_moved.reshape(rows, inner_local)
    beams = dec_ids.shape[0]
    vocab_local = embed_table.shape[0]
    flat_ids = dec_ids.reshape(-1) - lax.axis_index("tp") * vocab_local
    inside = (flat_ids >= 0) & (flat_ids < vocab_local)
    looked = jnp.take(embed_table, jnp.clip(flat_ids, 0, vocab_local - 1), axis=0)
    own_rows = jnp.where(inside[:, None], looked.astype(jnp.float32), 0.0)
    hidden = lax.psum(own_rows.astype(jnp.bfloat16), "tp").astype(jnp.float32)
    scaled = (hidden * dec_gain.astype(jnp.float32)).astype(jnp.bfloat16)
    raw_part = jnp.dot(scaled, cross_query_weight, preferred_element_type=jnp.float32)
    square_part = jnp.sum(hidden * hidden, axis=-1)
    raw, squares = lax.psum((raw_part, square_part), "ctx")
    factor = lax.rsqrt(squares / D + EPSILON)
    query = (raw * factor[:, None] * HD ** (-0.5)).astype(jnp.bfloat16).reshape(-1, heads_local, HD)
    positions = jnp.arange(rows, dtype=jnp.int32) * ctx_count + lax.axis_index("ctx")
    local_part = partial_softmax(
        query,
        keys_cache.reshape(rows, heads_local, HD),
        values_cache.reshape(rows, heads_local, HD),
        positions < limit,
        1.0,
    )
    top_all, total_all, mixed_all = joined(local_part, "ctx", softmax_merge)
    attn = (
        jnp.transpose(mixed_all / total_all[..., None], (1, 0, 2))
        .reshape(-1, inner_local)
        .astype(jnp.bfloat16)
    )
    out_part = jnp.dot(attn, cross_out_weight, preferred_element_type=jnp.float32)
    out = lax.psum(out_part, "tp")
    decoded = (out + hidden).astype(jnp.bfloat16).reshape(beams, 2, -1)
    return (keys_cache[None], values_cache[None], decoded)


MESH = pl.DeviceIdType.MESH
F32 = jnp.float32
BF16 = jnp.bfloat16
ORDER = (3, 0, 2, 1)


def hand_kernel(keys_ref, values_ref, decoded_ref, keys_out, values_out, decoded_out):
    keys_out[0] = keys_ref[...]
    values_out[0] = values_ref[...]
    for i in range(decoded_out.shape[0]):
        decoded_out[i] = decoded_ref[2 * i : 2 * i + 2].astype(BF16)


def fused_kernel(
    ids, length, dec_gain_far, enc_gain_far, q, k, v, ein, table, wq, wo, wk, wv, wout,
    keys_out, values_out, decoded_out,
    dec_gain, enc_gain, q_own, q_turned, ein_own, ein_turned, table_own, rows_own, looked, looked_far, wq_own, wout_own,
    kg, vg, qg, eg, wo_all, wk_all, wv_all, ctx_all, gained, square_own, square_far, square_sum, square_in,
    part_k, part_v, pair_k, pair_v, near_k, near_v, far_k, far_v, keys_own, values_own,
    raw_own, raw_out, raw_in, query_in, query_all, mix_own, mix_in, stat_own, stat_in, proj_out, proj_in, hidden_ref,
    send, r_look, r_wo, r_q, r_k, r_v, r_wk, r_wv, t_wk, t_wv, r_raw, r_query, r_ein, r_ctx, r_gained, r_square_far, r_square,
    r_pair, r_near, r_far, r_mix, r_stat, r_proj, fetched, stored,
):
    g = lax.axis_index("groups")
    c = lax.axis_index("ctx")
    t = lax.axis_index("tp")
    z, y = lax.div(c, 2), lax.rem(c, 2)
    mate, other = c + 1 - 2 * y, 1 - t
    line = [lax.rem(z + d, 4) for d in (2, 1, 3)]
    near_z = z + 1 - 2 * lax.rem(z, 2)
    across = 2 - 2 * lax.div(z, 2)
    across_middle = 2 - lax.div(z, 2)
    in_middle = (z == 1) | (z == 2)
    peers = [lax.rem(c + d, 8) for d in range(1, 8)]
    rows = q.shape[0]
    inner = q.shape[1]
    width = wq.shape[0]
    half = rows // 2
    each = rows // 8
    own_block = z * 2 + t
    heads = inner // HD
    pending = []

    def remote(source, target, arrival, to_ctx, to_tp):
        return pltpu.make_async_remote_copy(
            src_ref=source, dst_ref=target, send_sem=send, recv_sem=arrival,
            device_id={"ctx": to_ctx, "tp": to_tp}, device_id_type=MESH,
        )

    def put(source, target, arrival, to_ctx, to_tp):
        copy = remote(source, target, arrival, to_ctx, to_tp)
        copy.start()
        pending.append(copy)

    def put_twin(source, target, arrival):
        copy = pltpu.make_async_remote_copy(
            src_ref=source, dst_ref=target, send_sem=send, recv_sem=arrival,
            device_id={"groups": 1 - g, "ctx": c, "tp": t}, device_id_type=MESH,
        )
        copy.start()
        pending.append(copy)

    def got(target, arrival):
        remote(target, target, arrival, mate, t).wait_recv()

    def fetch(source, target, arrival):
        copy = pltpu.make_async_copy(source, target, arrival)
        copy.start()
        return copy

    def cols(index, size):
        return pl.ds(pl.multiple_of(index * size, size), size)

    barrier = pltpu.get_barrier_semaphore()
    for peer in peers:
        pl.semaphore_signal(barrier, inc=1, device_id={"ctx": peer, "tp": t}, device_id_type=MESH)
    pl.semaphore_signal(barrier, inc=1, device_id={"ctx": c, "tp": other}, device_id_type=MESH)
    pl.semaphore_signal(barrier, inc=1, device_id={"groups": 1 - g, "ctx": c, "tp": t}, device_id_type=MESH)

    gain_fetches = [fetch(dec_gain_far, dec_gain, fetched.at[13]), fetch(enc_gain_far, enc_gain, fetched.at[14])]
    q_fetch = fetch(q, q_own, fetched.at[0])
    k_fetch = fetch(k.at[:, cols(z, HD)], kg.at[c], fetched.at[1])
    v_fetch = fetch(v.at[:, cols(z, HD)], vg.at[c], fetched.at[2])
    ein_fetches = [
        fetch(ein.at[:, cols(far * 2 + t, width)], ein_own.at[far], fetched.at[3 + far]) for far in range(4)
    ]
    table_fetch = fetch(table, table_own, fetched.at[7])
    wq_fetch = fetch(wq, wq_own, fetched.at[8])
    late = [
        fetch(wo.at[:, cols(own_block, width)], wo_all.at[cols(t, inner)], fetched.at[9]),
        fetch(wk, wk_all.at[y], fetched.at[10]),
        fetch(wv, wv_all.at[y], fetched.at[11]),
    ]
    wout_fetch = fetch(wout, wout_own, fetched.at[12])
    pl.semaphore_wait(barrier, len(peers) + 2)

    for far in line:
        to = far * 2 + y
        put(k.at[:, cols(far, HD)], kg.at[c], r_k.at[c], to, t)
        put(v.at[:, cols(far, HD)], vg.at[c], r_v.at[c], to, t)
    put(k.at[:, cols(z, HD)], kg.at[c], r_k.at[c], mate, t)
    put(v.at[:, cols(z, HD)], vg.at[c], r_v.at[c], mate, t)

    place = lax.broadcasted_iota(jnp.int32, (rows, rows), 0)
    spot = lax.broadcasted_iota(jnp.int32, (rows, rows), 1)
    side, rest = lax.div(place, half), lax.rem(place, half)
    turn = (spot == lax.rem(rest, each) * 8 + lax.div(rest, each) * 2 + side).astype(BF16)

    q_fetch.wait()
    for copy in gain_fetches:
        copy.wait()
    turned = jnp.dot(turn, q_own[...], preferred_element_type=F32).astype(BF16)
    for s in range(2):
        q_turned[s] = turned[s * half : (s + 1) * half]
    for peer in peers:
        put(
            q_turned.at[lax.rem(peer, 2), :, cols(lax.div(peer, 2), HD)], qg.at[c], r_q.at[c], peer, t
        )
    qg[c] = q_turned[y, :, cols(z, HD)]
    put(wo.at[:, cols(z * 2 + other, width)], wo_all.at[cols(t, inner)], r_wo, c, other)
    piece = width // 4

    def weight_rows(index):
        return pl.ds(pl.multiple_of(index * piece, piece), piece)

    def send_weight(weight, whole, arrivals):
        for part in range(2):
            where = weight_rows(g * 2 + part)
            put(weight.at[where], whole.at[y, where], arrivals.at[part], mate, t)

    def relay_weight(whole, arrivals, twins):
        for part in range(2):
            where = weight_rows(g * 2 + part)
            here = whole.at[1 - y, where]
            got(here, arrivals.at[part])
            put_twin(here, here, twins.at[part])

    def whole_weight(whole, twins):
        for part in range(2):
            got(whole.at[1 - y, weight_rows((1 - g) * 2 + part)], twins.at[part])

    send_weight(wk, wk_all, r_wk)

    tokens = looked.shape[0]
    for far in range(4):
        ein_fetches[far].wait()
        turned = jnp.dot(turn, ein_own[far], preferred_element_type=F32).astype(BF16)
        for s in range(2):
            ein_turned[far, s] = turned[s * half : (s + 1) * half]

    eg[c] = ein_turned[z, y]
    for far in line:
        source = far * 2 + y
        got(kg.at[source], r_k.at[source])
        put(kg.at[source], kg.at[source], r_k.at[source], mate, t)
        got(vg.at[source], r_v.at[source])
        put(vg.at[source], vg.at[source], r_v.at[source], mate, t)
    send_weight(wv, wv_all, r_wv)
    def send_rows(chunk):
        where = slice(chunk * each, (chunk + 1) * each)
        for peer in peers:
            put(
                ein_turned.at[lax.div(peer, 2), lax.rem(peer, 2), where], eg.at[c, where], r_ein.at[c, chunk], peer, t
            )

    send_rows(ORDER[0])
    send_rows(ORDER[1])
    relay_weight(wk_all, r_wk, t_wk)

    table_fetch.wait()
    first = t * table.shape[0] * 16
    spots = lax.broadcasted_iota(jnp.int32, (16, width), 0)
    for j in range(tokens):
        own = ids[j % 2, j // 2] - first
        near = jnp.clip(own, 0, table.shape[0] * 16 - 1)
        block = table_own[lax.div(near, 16)].astype(F32)
        picked = spots + lax.div(near, 16) * 16 == own
        rows_own[j : j + 1] = jnp.sum(jnp.where(picked, block, 0.0), axis=0, keepdims=True)
    looked[...] = rows_own[...].astype(BF16)
    put(looked, looked_far, r_look, c, other)
    got(looked_far, r_look)
    wq_fetch.wait()
    hidden = looked[...].astype(F32) + looked_far[...].astype(F32)
    hidden_ref[...] = hidden
    scaled = (hidden * dec_gain[...].astype(F32).reshape(1, width)).astype(BF16)
    raw_own[:, :inner] = jnp.dot(scaled, wq_own[...], preferred_element_type=F32)
    raw_own[:, inner:] = jnp.broadcast_to(jnp.sum(hidden * hidden, axis=-1, keepdims=True), (tokens, 128))
    share = tokens // 8
    for j in range(8):
        raw_out[j] = raw_own[j * share : (j + 1) * share, :]
    for peer in peers:
        put(raw_out.at[peer], raw_in.at[c], r_raw.at[c], peer, t)
    raw_in[c] = raw_out[c]

    k_fetch.wait()
    v_fetch.wait()
    for peer in peers:
        got(qg.at[peer], r_q.at[peer])
    for far in range(4):
        source = far * 2 + 1 - y
        got(kg.at[source], r_k.at[source])
        got(vg.at[source], r_v.at[source])

    limit = length[0]
    every_key = kg[...].reshape(8 * rows, HD)
    every_value = vg[...].reshape(8 * rows, HD)
    valid = lax.broadcasted_iota(jnp.int32, (1, 8 * rows), 1) < limit

    def block_at(core, far, chunk):
        return ctx_all.at[chunk, :, cols(core * 4 + far, HD)], r_ctx.at[core * 4 + far, chunk]

    for chunk in ORDER:
        queries = qg[:, chunk * each : (chunk + 1) * each, :].reshape(rows, HD)
        scores = lax.dot_general(
            queries, every_key, (((1,), (1,)), ((), ())), preferred_element_type=F32
        ) * (HD ** (-0.5))
        scores = jnp.where(valid, scores, FLOOR)
        top = jnp.max(scores, axis=-1, keepdims=True)
        probs = jnp.where(valid, jnp.exp(scores - top), 0.0)
        total = jnp.sum(probs, axis=-1, keepdims=True)
        mixed = jnp.dot(probs.astype(BF16), every_value, preferred_element_type=F32)
        ctx_all[chunk, :, cols(t * 4 + z, HD)] = (mixed / total).astype(BF16)
        here, arrival = block_at(t, z, chunk)
        put(here, here, arrival, across_middle * 2 + y, t)
        put(here, here, arrival, near_z * 2 + y, t)
        put(here, here, arrival, c, other)

    send_rows(ORDER[2])
    relay_weight(wv_all, r_wv, t_wv)

    for copy in late:
        copy.wait()
    got(wo_all.at[cols(other, inner)], r_wo)
    gain = enc_gain[cols(own_block, width)].astype(F32).reshape(1, width)

    def relay(chunk):
        for far in (near_z, across, across + 1):
            here, arrival = block_at(t, far, chunk)
            got(here, arrival)
            if far is not near_z:

                @pl.when(in_middle)
                def _():
                    remote(here, here, arrival, near_z * 2 + y, t).start()

            put(here, here, arrival, c, other)

    def project(chunk):
        for far in range(4):
            got(*block_at(other, far, chunk))
        for peer in peers:
            got(eg.at[peer, chunk * each : (chunk + 1) * each], r_ein.at[peer, chunk])
        resid = jnp.dot(ctx_all[chunk], wo_all[...], preferred_element_type=F32)
        resid = resid + eg[:, chunk * each : (chunk + 1) * each, :].reshape(rows, width).astype(F32)
        spread = jnp.where(place == spot, jnp.sum(resid * resid, axis=-1, keepdims=True), 0.0)
        square_own[chunk] = jnp.sum(spread, axis=0, keepdims=True)
        gained[chunk, t] = (resid * gain).astype(BF16)
        put(gained.at[chunk, t], gained.at[chunk, t], r_gained.at[chunk], c, other)
        put(square_own.at[chunk], square_far.at[chunk], r_square_far.at[chunk], c, other)

    ways = ((part_k, pair_k, near_k, far_k, wk_all, t_wk), (part_v, pair_v, near_v, far_v, wv_all, t_wv))

    def start_only(source, target, arrival, to_z):
        remote(source, target, arrival, to_z * 2 + y, t).start()

    def spread_out(chunk, first):
        got(gained.at[chunk, other], r_gained.at[chunk])
        end = 0 if chunk >= 2 else 3
        for way, (part, pair, near, far, weight, arrival) in enumerate(ways):
            if first:
                whole_weight(weight, arrival)
            total = jnp.dot(gained[chunk, 0], weight[0], preferred_element_type=F32)
            total = total + jnp.dot(gained[chunk, 1], weight[1], preferred_element_type=F32)
            part[chunk] = total.astype(BF16)

            @pl.when(z == end)
            def _():
                start_only(
                    part.at[chunk], pair.at[chunk % 2], r_pair.at[way, chunk % 2], 1 if end == 0 else 2
                )

            if chunk in (0, 3):

                @pl.when(z == (1 if chunk == 0 else 2))
                def _():
                    start_only(part.at[chunk], near, r_near.at[way], chunk)

    def last_near():
        for way, (part, pair, near, far, weight, arrival) in enumerate(ways):

            @pl.when((z == 0) | (z == 3))
            def _():
                start_only(part.at[near_z], near, r_near.at[way], near_z)

    def join(chunk):
        middle = 1 if chunk >= 2 else 2
        for way, (part, pair, near, far, weight, arrival) in enumerate(ways):

            @pl.when(z == middle)
            def _():
                got(pair.at[chunk % 2], r_pair.at[way, chunk % 2])
                both = part[chunk].astype(F32) + pair[chunk % 2].astype(F32)
                pair[chunk % 2] = both.astype(BF16)
                start_only(pair.at[chunk % 2], far, r_far.at[way], chunk)

    relay(ORDER[0])
    relay(ORDER[1])
    project(ORDER[0])
    send_rows(ORDER[3])
    relay(ORDER[2])
    spread_out(ORDER[0], True)
    project(ORDER[1])
    relay(ORDER[3])
    spread_out(ORDER[1], False)
    project(ORDER[2])
    spread_out(ORDER[2], False)
    project(ORDER[3])
    spread_out(ORDER[3], False)
    last_near()
    for chunk in range(4):
        got(square_far.at[chunk], r_square_far.at[chunk])
        square_sum[chunk] = square_own[chunk] + square_far[chunk]
    for far in line:
        put(square_sum.at[far], square_in.at[z], r_square.at[z], far * 2 + y, t)
    square_in[z] = square_sum[z]

    join(ORDER[0])
    join(ORDER[1])
    for peer in peers:
        got(raw_in.at[peer], r_raw.at[peer])
    raw = raw_in[0]
    for j in range(1, 8):
        raw = raw + raw_in[j]
    factor = lax.rsqrt(raw[:, inner : inner + 1] / D + EPSILON)
    query_in[c] = (raw[:, :inner] * factor * HD ** (-0.5)).astype(BF16).astype(F32)
    for peer in peers:
        put(query_in.at[c], query_in.at[c], r_query.at[c], peer, t)
    join(ORDER[2])
    join(ORDER[3])

    for far in line:
        got(square_in.at[far], r_square.at[far])
    square = square_in[0] + square_in[1] + square_in[2] + square_in[3]
    column = jnp.sum(jnp.where(place == spot, square, 0.0), axis=-1, keepdims=True)
    scale = lax.rsqrt(column / D + EPSILON)
    for peer in peers:
        got(query_in.at[peer], r_query.at[peer])
    for j in range(8):
        query_all[j * share : (j + 1) * share, :] = query_in[j]

    stores = []

    def settle(way, own, out):
        part, pair, near, far, weight, arrival = ways[way]
        got(far, r_far.at[way])
        got(near, r_near.at[way])
        total = part[z].astype(F32) + near[...].astype(F32) + far[...].astype(F32)
        own[...] = (total * scale).astype(BF16)
        stores.append(fetch(own, out, stored.at[way]))

    settle(0, keys_own, keys_out)
    own_valid = lax.broadcasted_iota(jnp.int32, (1, rows), 1) * 8 + c < limit
    scores = jnp.concatenate(
        [
            lax.dot_general(
                query_all[:, h * HD : (h + 1) * HD].astype(BF16), keys_own[:, h * HD : (h + 1) * HD],
                (((1,), (1,)), ((), ())), preferred_element_type=F32,
            )
            for h in range(heads)
        ],
        axis=0,
    )
    scores = jnp.where(own_valid, scores, FLOOR)
    top = jnp.max(scores, axis=-1, keepdims=True)
    probs = jnp.where(own_valid, jnp.exp(scores - top), 0.0)
    total = jnp.sum(probs, axis=-1, keepdims=True)
    stat_own[0:1] = jnp.sum(jnp.where(place == spot, top, 0.0), axis=0, keepdims=True)
    stat_own[1:2] = jnp.sum(jnp.where(place == spot, total, 0.0), axis=0, keepdims=True)
    for peer in peers:
        put(stat_own, stat_in.at[c], r_stat.at[c], peer, t)
    settle(1, values_own, values_out)
    for h in range(heads):
        mix_own[h * tokens : (h + 1) * tokens] = jnp.dot(
            probs[h * tokens : (h + 1) * tokens].astype(BF16), values_own[:, h * HD : (h + 1) * HD],
            preferred_element_type=F32,
        ).astype(BF16)
    for peer in peers:
        put(mix_own, mix_in.at[c], r_mix.at[c], peer, t)
    stat_in[c] = stat_own[...]
    mix_in[c] = mix_own[...]
    wout_fetch.wait()
    for peer in peers:
        got(stat_in.at[peer], r_stat.at[peer])
    top = stat_in[0][0:1]
    for j in range(1, 8):
        top = jnp.maximum(top, stat_in[j][0:1])
    factors = [jnp.exp(stat_in[j][0:1] - top) for j in range(8)]
    total = factors[0] * stat_in[0][1:2]
    for j in range(1, 8):
        total = total + factors[j] * stat_in[j][1:2]
    for peer in peers:
        got(mix_in.at[peer], r_mix.at[peer])
    mixed = jnp.zeros((rows, HD), F32)
    for j in range(8):
        column = jnp.sum(jnp.where(place == spot, factors[j] / total, 0.0), axis=-1, keepdims=True)
        mixed = mixed + mix_in[j].astype(F32) * column
    attn = mixed.astype(BF16)
    proj = jnp.zeros(proj_out.shape, F32)
    for h in range(heads):
        proj = proj + jnp.dot(
            attn[h * tokens : (h + 1) * tokens], wout_own[h * HD : (h + 1) * HD], preferred_element_type=F32
        )
    proj_out[...] = proj
    put(proj_out, proj_in, r_proj, c, other)
    got(proj_in, r_proj)
    decoded_out[...] = proj_out[...] + proj_in[...] + hidden_ref[...]
    for copy in stores:
        copy.wait()
    for copy in pending:
        copy.wait_send()
    for i in range(6):
        remote(near_k, near_k, r_near.at[0], mate, t).wait_send()

    @pl.when(in_middle)
    def _():
        for i in range(8):
            remote(ctx_all.at[0, :, cols(z, HD)], ctx_all.at[0, :, cols(z, HD)], r_near.at[0], mate, t).wait_send()


def local_fused(
    enc_input, enc_query, enc_key, enc_value, seq_length, attn_out_weight, enc_gain, cross_key_weight,
    cross_value_weight, embed_table, dec_ids, dec_gain, cross_query_weight, cross_out_weight,
):
    rows, inner = enc_query.shape
    width = cross_query_weight.shape[0]
    tokens = dec_ids.size
    whole = pl.BlockSpec(memory_space=pltpu.VMEM)
    scalars = pl.BlockSpec(memory_space=pltpu.SMEM)
    anywhere = pl.BlockSpec(memory_space=pl.ANY)
    dma = pltpu.SemaphoreType.DMA
    share = tokens // 8
    half = rows // 2
    keys, values, decoded = pl.pallas_call(
        fused_kernel,
        out_shape=(
            jax.ShapeDtypeStruct((rows, inner), BF16),
            jax.ShapeDtypeStruct((rows, inner), BF16),
            jax.ShapeDtypeStruct((tokens, width), F32),
        ),
        in_specs=[scalars, scalars] + [anywhere] * 12,
        out_specs=(anywhere, anywhere, whole),
        scratch_shapes=[
            pltpu.VMEM(dec_gain.shape, BF16),
            pltpu.VMEM(enc_gain.shape, BF16),
            pltpu.VMEM((rows, inner), BF16),
            pltpu.VMEM((2, half, inner), BF16),
            pltpu.VMEM((4, rows, width), BF16),
            pltpu.VMEM((4, 2, half, width), BF16),
            pltpu.VMEM((embed_table.shape[0] // 16, 16, width), BF16),
            pltpu.VMEM((tokens, width), F32),
            pltpu.VMEM((tokens, width), BF16),
            pltpu.VMEM((tokens, width), BF16),
            pltpu.VMEM((width, inner), BF16),
            pltpu.VMEM((inner, width), BF16),
            pltpu.VMEM((8, rows, HD), BF16),
            pltpu.VMEM((8, rows, HD), BF16),
            pltpu.VMEM((8, half, HD), BF16),
            pltpu.VMEM((8, half, width), BF16),
            pltpu.VMEM((2 * inner, width), BF16),
            pltpu.VMEM((2, width, inner), BF16),
            pltpu.VMEM((2, width, inner), BF16),
            pltpu.VMEM((4, rows, 2 * inner), BF16),
            pltpu.VMEM((4, 2, rows, width), BF16),
            pltpu.VMEM((4, 1, rows), F32),
            pltpu.VMEM((4, 1, rows), F32),
            pltpu.VMEM((4, 1, rows), F32),
            pltpu.VMEM((4, 1, rows), F32),
            pltpu.VMEM((4, rows, inner), BF16),
            pltpu.VMEM((4, rows, inner), BF16),
            pltpu.VMEM((2, rows, inner), BF16),
            pltpu.VMEM((2, rows, inner), BF16),
            pltpu.VMEM((rows, inner), BF16),
            pltpu.VMEM((rows, inner), BF16),
            pltpu.VMEM((rows, inner), BF16),
            pltpu.VMEM((rows, inner), BF16),
            pltpu.VMEM((rows, inner), BF16),
            pltpu.VMEM((rows, inner), BF16),
            pltpu.VMEM((tokens, inner + 128), F32),
            pltpu.VMEM((8, share, inner + 128), F32),
            pltpu.VMEM((8, share, inner + 128), F32),
            pltpu.VMEM((8, share, inner), F32),
            pltpu.VMEM((tokens, inner), F32),
            pltpu.VMEM((rows, HD), BF16),
            pltpu.VMEM((8, rows, HD), BF16),
            pltpu.VMEM((2, rows), F32),
            pltpu.VMEM((8, 2, rows), F32),
            pltpu.VMEM((tokens, width), F32),
            pltpu.VMEM((tokens, width), F32),
            pltpu.VMEM((tokens, width), F32),
            dma, dma, dma, dma((8,)), dma((8,)), dma((8,)), dma((2,)), dma((2,)), dma((2,)), dma((2,)), dma((8,)), dma((8,)), dma((8, 4)),
            dma((8, 4)), dma((4,)), dma((4,)), dma((4,)),
            dma((2, 2)), dma((2,)), dma((2,)), dma((8,)), dma((8,)), dma, dma((15,)), dma((2,)),
        ],
        compiler_params=pltpu.CompilerParams(
            collective_id=0, has_side_effects=True, vmem_limit_bytes=60 * 1024 * 1024
        ),
    )(
        dec_ids.T, seq_length, dec_gain, enc_gain, enc_query, enc_key, enc_value, enc_input,
        embed_table.reshape(embed_table.shape[0] // 16, 16, width),
        cross_query_weight, attn_out_weight, cross_key_weight, cross_value_weight, cross_out_weight,
    )
    return pl.pallas_call(
        hand_kernel,
        out_shape=(
            jax.ShapeDtypeStruct((1, rows, inner), BF16),
            jax.ShapeDtypeStruct((1, rows, inner), BF16),
            jax.ShapeDtypeStruct((tokens // 2, 2, width), BF16),
        ),
        in_specs=[whole] * 3,
        out_specs=(whole, whole, whole),
    )(keys, values, decoded)


def chosen(*arrays):
    rows, inner = arrays[1].shape
    fits = lax.axis_size("ctx") == 8 and lax.axis_size("tp") == 2 and (rows, inner) == (128, 4 * HD)
    fits = fits and arrays[9].shape[0] % 16 == 0
    return (local_fused if fits else local)(*arrays)


def solution(mesh):
    placed = (
        P(("groups", "ctx"), None),
        P(("groups", "ctx"), "tp"),
        P(("groups", "ctx"), "tp"),
        P(("groups", "ctx"), "tp"),
        P("groups"),
        P("tp", None),
        P(),
        P("ctx", "tp"),
        P("ctx", "tp"),
        P("tp", "ctx"),
        P("groups", None),
        P("ctx"),
        P("ctx", "tp"),
        P("tp", "ctx"),
    )
    return jax.shard_map(
        chosen,
        mesh=mesh,
        in_specs=placed,
        out_specs=(
            P(("groups", "ctx"), None, "tp"),
            P(("groups", "ctx"), None, "tp"),
            P("groups", None, "ctx"),
        ),
        check_vma=False,
    )
```

```python
import math

import jax
import jax.numpy as jnp
from jax import lax
from jax.experimental import pallas as pl
from jax.experimental.pallas import tpu as pltpu
from jax.sharding import PartitionSpec as P

D = 4096
HD = 128


EPSILON = 1e-06
FLOOR = -1e30


def joined(value, axis, join):
    pieces = jax.tree.map(lambda part: lax.all_gather(part, axis), value)
    head = jax.tree.map(lambda part: part[0], pieces)
    tail = jax.tree.map(lambda part: part[1:], pieces)
    total, _ = lax.scan(lambda total, piece: (join(total, piece), None), head, tail)
    return total


def softmax_merge(first, second):
    top_first, total_first, mixed_first = first
    top_second, total_second, mixed_second = second
    top = jnp.maximum(top_first, top_second)
    weight_first = jnp.exp(top_first - top)
    weight_second = jnp.exp(top_second - top)
    total = total_first * weight_first + total_second * weight_second
    mixed = mixed_first * weight_first[..., None] + mixed_second * weight_second[..., None]
    return (top, total, mixed)


def partial_softmax(queries, keys, values, valid, factor):
    scores = jnp.einsum("qhd,khd->hqk", queries, keys, preferred_element_type=jnp.float32) * factor
    scores = jnp.where(valid[None, None, :], scores, FLOOR)
    top = jnp.max(scores, axis=-1)
    probs = jnp.where(valid[None, None, :], jnp.exp(scores - top[..., None]), 0.0)
    total = jnp.sum(probs, axis=-1)
    mixed = jnp.einsum(
        "hqk,khd->hqd", probs.astype(jnp.bfloat16), values, preferred_element_type=jnp.float32
    )
    return (top, total, mixed)


def norm_rows(resid, gain):
    scale = lax.rsqrt(jnp.mean(resid * resid, axis=-1, keepdims=True) + EPSILON)
    return (resid * scale * gain.astype(jnp.float32)).astype(jnp.bfloat16)


def local(
    enc_input,
    enc_query,
    enc_key,
    enc_value,
    seq_length,
    attn_out_weight,
    enc_gain,
    cross_key_weight,
    cross_value_weight,
    embed_table,
    dec_ids,
    dec_gain,
    cross_query_weight,
    cross_out_weight,
):
    rows, inner_local = enc_query.shape
    heads_local = inner_local // HD
    limit = seq_length[0]
    queries = enc_query.reshape(rows, heads_local, HD)
    start_state = (
        jnp.full((heads_local, rows), FLOOR, jnp.float32),
        jnp.zeros((heads_local, rows), jnp.float32),
        jnp.zeros((heads_local, rows, HD), jnp.float32),
    )
    carry = start_state
    key_rows = lax.all_gather(enc_key, "ctx", axis=0, tiled=True)
    value_rows = lax.all_gather(enc_value, "ctx", axis=0, tiled=True)
    count = key_rows.shape[0]
    block = math.gcd(count, 2048)
    blocks = count // block
    key_blocks = key_rows.reshape(blocks, block, heads_local, HD)
    value_blocks = value_rows.reshape(blocks, block, heads_local, HD)
    offsets = jnp.arange(blocks, dtype=jnp.int32) * block

    def one_block(state, item):
        key_block, value_block, offset = item
        positions = offset + jnp.arange(block, dtype=jnp.int32)
        update = partial_softmax(queries, key_block, value_block, positions < limit, HD ** (-0.5))
        return (softmax_merge(state, update), None)

    carry, unused = lax.scan(one_block, carry, (key_blocks, value_blocks, offsets))
    top, total, mixed = carry
    context = (
        jnp.transpose(mixed / total[..., None], (1, 0, 2))
        .reshape(rows, inner_local)
        .astype(jnp.bfloat16)
    )
    summed = lax.psum(jnp.dot(context, attn_out_weight, preferred_element_type=jnp.float32), "tp")
    memory = norm_rows(enc_input.astype(jnp.float32) + summed, enc_gain)
    ctx_count = lax.axis_size("ctx")
    slots = rows // ctx_count
    key_sum = jnp.dot(
        memory,
        lax.all_gather(cross_key_weight, "ctx", axis=0, tiled=True),
        preferred_element_type=jnp.float32,
    )
    value_sum = jnp.dot(
        memory,
        lax.all_gather(cross_value_weight, "ctx", axis=0, tiled=True),
        preferred_element_type=jnp.float32,
    )
    key_rows = key_sum.astype(jnp.bfloat16)
    value_rows = value_sum.astype(jnp.bfloat16)
    keys_moved, values_moved = (
        lax.all_to_all(
            key_rows.reshape(slots, ctx_count, inner_local),
            "ctx",
            split_axis=1,
            concat_axis=0,
            tiled=True,
        ),
        lax.all_to_all(
            value_rows.reshape(slots, ctx_count, inner_local),
            "ctx",
            split_axis=1,
            concat_axis=0,
            tiled=True,
        ),
    )
    keys_cache = keys_moved.reshape(rows, inner_local)
    values_cache = values_moved.reshape(rows, inner_local)
    beams = dec_ids.shape[0]
    vocab_local = embed_table.shape[0]
    flat_ids = dec_ids.reshape(-1) - lax.axis_index("tp") * vocab_local
    inside = (flat_ids >= 0) & (flat_ids < vocab_local)
    looked = jnp.take(embed_table, jnp.clip(flat_ids, 0, vocab_local - 1), axis=0)
    own_rows = jnp.where(inside[:, None], looked.astype(jnp.float32), 0.0)
    hidden = lax.psum(own_rows.astype(jnp.bfloat16), "tp").astype(jnp.float32)
    scaled = (hidden * dec_gain.astype(jnp.float32)).astype(jnp.bfloat16)
    raw_part = jnp.dot(scaled, cross_query_weight, preferred_element_type=jnp.float32)
    square_part = jnp.sum(hidden * hidden, axis=-1)
    raw, squares = lax.psum((raw_part, square_part), "ctx")
    factor = lax.rsqrt(squares / D + EPSILON)
    query = (raw * factor[:, None] * HD ** (-0.5)).astype(jnp.bfloat16).reshape(-1, heads_local, HD)
    positions = jnp.arange(rows, dtype=jnp.int32) * ctx_count + lax.axis_index("ctx")
    local_part = partial_softmax(
        query,
        keys_cache.reshape(rows, heads_local, HD),
        values_cache.reshape(rows, heads_local, HD),
        positions < limit,
        1.0,
    )
    top_all, total_all, mixed_all = joined(local_part, "ctx", softmax_merge)
    attn = (
        jnp.transpose(mixed_all / total_all[..., None], (1, 0, 2))
        .reshape(-1, inner_local)
        .astype(jnp.bfloat16)
    )
    out_part = jnp.dot(attn, cross_out_weight, preferred_element_type=jnp.float32)
    out = lax.psum(out_part, "tp")
    decoded = (out + hidden).astype(jnp.bfloat16).reshape(beams, 2, -1)
    return (keys_cache[None], values_cache[None], decoded)


MESH = pl.DeviceIdType.MESH
F32 = jnp.float32
BF16 = jnp.bfloat16
ORDER = (3, 0, 2, 1)


def hand_kernel(keys_ref, values_ref, decoded_ref, keys_out, values_out, decoded_out):
    keys_out[0] = keys_ref[...]
    values_out[0] = values_ref[...]
    for i in range(decoded_out.shape[0]):
        decoded_out[i] = decoded_ref[2 * i : 2 * i + 2].astype(BF16)


def fused_kernel(
    ids, length, dec_gain_far, enc_gain_far, q, k, v, ein, table, wq, wo, wk, wv, wout,
    keys_out, values_out, decoded_out,
    dec_gain, enc_gain, q_own, q_turned, ein_own, ein_turned, table_own, rows_own, looked, looked_far, wq_own, wout_own,
    kg, vg, qg, eg, wo_all, wk_all, wv_all, ctx_all, gained, square_own, square_far, square_sum, square_in,
    part_k, part_v, pair_k, pair_v, near_k, near_v, far_k, far_v, keys_own, values_own,
    raw_own, raw_out, raw_in, query_in, query_all, mix_own, mix_in, stat_own, stat_in, proj_out, proj_in, hidden_ref,
    send, r_look, r_wo, r_q, r_k, r_v, r_wk, r_wv, t_wk, t_wv, r_raw, r_query, r_ein, r_ctx, r_gained, r_square_far, r_square,
    r_pair, r_near, r_far, r_mix, r_stat, r_proj, fetched, stored,
):
    g = lax.axis_index("groups")
    c = lax.axis_index("ctx")
    t = lax.axis_index("tp")
    z, y = lax.div(c, 2), lax.rem(c, 2)
    mate, other = c + 1 - 2 * y, 1 - t
    line = [lax.rem(z + d, 4) for d in (2, 1, 3)]
    near_z = z + 1 - 2 * lax.rem(z, 2)
    across = 2 - 2 * lax.div(z, 2)
    across_middle = 2 - lax.div(z, 2)
    in_middle = (z == 1) | (z == 2)
    peers = [lax.rem(c + d, 8) for d in range(1, 8)]
    rows = q.shape[0]
    inner = q.shape[1]
    width = wq.shape[0]
    half = rows // 2
    each = rows // 8
    own_block = z * 2 + t
    heads = inner // HD
    pending = []

    def remote(source, target, arrival, to_ctx, to_tp):
        return pltpu.make_async_remote_copy(
            src_ref=source, dst_ref=target, send_sem=send, recv_sem=arrival,
            device_id={"ctx": to_ctx, "tp": to_tp}, device_id_type=MESH,
        )

    def put(source, target, arrival, to_ctx, to_tp):
        copy = remote(source, target, arrival, to_ctx, to_tp)
        copy.start()
        pending.append(copy)

    def put_twin(source, target, arrival):
        copy = pltpu.make_async_remote_copy(
            src_ref=source, dst_ref=target, send_sem=send, recv_sem=arrival,
            device_id={"groups": 1 - g, "ctx": c, "tp": t}, device_id_type=MESH,
        )
        copy.start()
        pending.append(copy)

    def got(target, arrival):
        remote(target, target, arrival, mate, t).wait_recv()

    def fetch(source, target, arrival):
        copy = pltpu.make_async_copy(source, target, arrival)
        copy.start()
        return copy

    def cols(index, size):
        return pl.ds(pl.multiple_of(index * size, size), size)

    barrier = pltpu.get_barrier_semaphore()
    for peer in peers:
        pl.semaphore_signal(barrier, inc=1, device_id={"ctx": peer, "tp": t}, device_id_type=MESH)
    pl.semaphore_signal(barrier, inc=1, device_id={"ctx": c, "tp": other}, device_id_type=MESH)
    pl.semaphore_signal(barrier, inc=1, device_id={"groups": 1 - g, "ctx": c, "tp": t}, device_id_type=MESH)

    gain_fetches = [fetch(dec_gain_far, dec_gain, fetched.at[13]), fetch(enc_gain_far, enc_gain, fetched.at[14])]
    q_fetch = fetch(q, q_own, fetched.at[0])
    k_fetch = fetch(k.at[:, cols(z, HD)], kg.at[c], fetched.at[1])
    v_fetch = fetch(v.at[:, cols(z, HD)], vg.at[c], fetched.at[2])
    ein_fetches = [
        fetch(ein.at[:, cols(far * 2 + t, width)], ein_own.at[far], fetched.at[3 + far]) for far in range(4)
    ]
    table_fetch = fetch(table, table_own, fetched.at[7])
    wq_fetch = fetch(wq, wq_own, fetched.at[8])
    late = [
        fetch(wo.at[:, cols(own_block, width)], wo_all.at[cols(t, inner)], fetched.at[9]),
        fetch(wk, wk_all.at[y], fetched.at[10]),
        fetch(wv, wv_all.at[y], fetched.at[11]),
    ]
    wout_fetch = fetch(wout, wout_own, fetched.at[12])
    pl.semaphore_wait(barrier, len(peers) + 2)

    for far in line:
        to = far * 2 + y
        put(k.at[:, cols(far, HD)], kg.at[c], r_k.at[c], to, t)
        put(v.at[:, cols(far, HD)], vg.at[c], r_v.at[c], to, t)
    put(k.at[:, cols(z, HD)], kg.at[c], r_k.at[c], mate, t)
    put(v.at[:, cols(z, HD)], vg.at[c], r_v.at[c], mate, t)

    place = lax.broadcasted_iota(jnp.int32, (rows, rows), 0)
    spot = lax.broadcasted_iota(jnp.int32, (rows, rows), 1)
    side, rest = lax.div(place, half), lax.rem(place, half)
    turn = (spot == lax.rem(rest, each) * 8 + lax.div(rest, each) * 2 + side).astype(BF16)

    q_fetch.wait()
    for copy in gain_fetches:
        copy.wait()
    turned = jnp.dot(turn, q_own[...], preferred_element_type=F32).astype(BF16)
    for s in range(2):
        q_turned[s] = turned[s * half : (s + 1) * half]
    for peer in peers:
        put(
            q_turned.at[lax.rem(peer, 2), :, cols(lax.div(peer, 2), HD)], qg.at[c], r_q.at[c], peer, t
        )
    qg[c] = q_turned[y, :, cols(z, HD)]
    put(wo.at[:, cols(z * 2 + other, width)], wo_all.at[cols(t, inner)], r_wo, c, other)
    piece = width // 4

    def weight_rows(index):
        return pl.ds(pl.multiple_of(index * piece, piece), piece)

    def send_weight(weight, whole, arrivals):
        for part in range(2):
            where = weight_rows(g * 2 + part)
            put(weight.at[where], whole.at[y, where], arrivals.at[part], mate, t)

    def relay_weight(whole, arrivals, twins):
        for part in range(2):
            where = weight_rows(g * 2 + part)
            here = whole.at[1 - y, where]
            got(here, arrivals.at[part])
            put_twin(here, here, twins.at[part])

    def whole_weight(whole, twins):
        for part in range(2):
            got(whole.at[1 - y, weight_rows((1 - g) * 2 + part)], twins.at[part])

    send_weight(wk, wk_all, r_wk)

    tokens = looked.shape[0]
    for far in range(4):
        ein_fetches[far].wait()
        turned = jnp.dot(turn, ein_own[far], preferred_element_type=F32).astype(BF16)
        for s in range(2):
            ein_turned[far, s] = turned[s * half : (s + 1) * half]

    eg[c] = ein_turned[z, y]
    for far in line:
        source = far * 2 + y
        got(kg.at[source], r_k.at[source])
        put(kg.at[source], kg.at[source], r_k.at[source], mate, t)
        got(vg.at[source], r_v.at[source])
        put(vg.at[source], vg.at[source], r_v.at[source], mate, t)
    send_weight(wv, wv_all, r_wv)
    def send_rows(chunk):
        where = slice(chunk * each, (chunk + 1) * each)
        for peer in peers:
            put(
                ein_turned.at[lax.div(peer, 2), lax.rem(peer, 2), where], eg.at[c, where], r_ein.at[c, chunk], peer, t
            )

    send_rows(ORDER[0])
    send_rows(ORDER[1])
    relay_weight(wk_all, r_wk, t_wk)

    table_fetch.wait()
    first = t * table.shape[0] * 16
    spots = lax.broadcasted_iota(jnp.int32, (16, width), 0)
    for j in range(tokens):
        own = ids[j % 2, j // 2] - first
        near = jnp.clip(own, 0, table.shape[0] * 16 - 1)
        block = table_own[lax.div(near, 16)].astype(F32)
        picked = spots + lax.div(near, 16) * 16 == own
        rows_own[j : j + 1] = jnp.sum(jnp.where(picked, block, 0.0), axis=0, keepdims=True)
    looked[...] = rows_own[...].astype(BF16)
    put(looked, looked_far, r_look, c, other)
    got(looked_far, r_look)
    wq_fetch.wait()
    hidden = looked[...].astype(F32) + looked_far[...].astype(F32)
    hidden_ref[...] = hidden
    scaled = (hidden * dec_gain[...].astype(F32).reshape(1, width)).astype(BF16)
    raw_own[:, :inner] = jnp.dot(scaled, wq_own[...], preferred_element_type=F32)
    raw_own[:, inner:] = jnp.broadcast_to(jnp.sum(hidden * hidden, axis=-1, keepdims=True), (tokens, 128))
    share = tokens // 8
    for j in range(8):
        raw_out[j] = raw_own[j * share : (j + 1) * share, :]
    for peer in peers:
        put(raw_out.at[peer], raw_in.at[c], r_raw.at[c], peer, t)
    raw_in[c] = raw_out[c]

    k_fetch.wait()
    v_fetch.wait()
    for peer in peers:
        got(qg.at[peer], r_q.at[peer])
    for far in range(4):
        source = far * 2 + 1 - y
        got(kg.at[source], r_k.at[source])
        got(vg.at[source], r_v.at[source])

    limit = length[0]
    every_key = kg[...].reshape(8 * rows, HD)
    every_value = vg[...].reshape(8 * rows, HD)
    valid = lax.broadcasted_iota(jnp.int32, (1, 8 * rows), 1) < limit

    def block_at(core, far, chunk):
        return ctx_all.at[chunk, :, cols(core * 4 + far, HD)], r_ctx.at[core * 4 + far, chunk]

    for chunk in ORDER:
        queries = qg[:, chunk * each : (chunk + 1) * each, :].reshape(rows, HD)
        scores = lax.dot_general(
            queries, every_key, (((1,), (1,)), ((), ())), preferred_element_type=F32
        ) * (HD ** (-0.5))
        scores = jnp.where(valid, scores, FLOOR)
        top = jnp.max(scores, axis=-1, keepdims=True)
        probs = jnp.where(valid, jnp.exp(scores - top), 0.0)
        total = jnp.sum(probs, axis=-1, keepdims=True)
        mixed = jnp.dot(probs.astype(BF16), every_value, preferred_element_type=F32)
        ctx_all[chunk, :, cols(t * 4 + z, HD)] = (mixed / total).astype(BF16)
        here, arrival = block_at(t, z, chunk)
        put(here, here, arrival, across_middle * 2 + y, t)
        put(here, here, arrival, near_z * 2 + y, t)
        put(here, here, arrival, c, other)

    send_rows(ORDER[2])
    relay_weight(wv_all, r_wv, t_wv)

    for copy in late:
        copy.wait()
    got(wo_all.at[cols(other, inner)], r_wo)
    gain = enc_gain[cols(own_block, width)].astype(F32).reshape(1, width)

    def relay(chunk):
        for far in (near_z, across, across + 1):
            here, arrival = block_at(t, far, chunk)
            got(here, arrival)
            if far is not near_z:

                @pl.when(in_middle)
                def _():
                    remote(here, here, arrival, near_z * 2 + y, t).start()

            put(here, here, arrival, c, other)

    def project(chunk):
        for far in range(4):
            got(*block_at(other, far, chunk))
        for peer in peers:
            got(eg.at[peer, chunk * each : (chunk + 1) * each], r_ein.at[peer, chunk])
        resid = jnp.dot(ctx_all[chunk], wo_all[...], preferred_element_type=F32)
        resid = resid + eg[:, chunk * each : (chunk + 1) * each, :].reshape(rows, width).astype(F32)
        spread = jnp.where(place == spot, jnp.sum(resid * resid, axis=-1, keepdims=True), 0.0)
        square_own[chunk] = jnp.sum(spread, axis=0, keepdims=True)
        gained[chunk, t] = (resid * gain).astype(BF16)
        put(gained.at[chunk, t], gained.at[chunk, t], r_gained.at[chunk], c, other)
        put(square_own.at[chunk], square_far.at[chunk], r_square_far.at[chunk], c, other)

    ways = ((part_k, pair_k, near_k, far_k, wk_all, t_wk), (part_v, pair_v, near_v, far_v, wv_all, t_wv))

    def start_only(source, target, arrival, to_z):
        remote(source, target, arrival, to_z * 2 + y, t).start()

    def spread_out(chunk, first):
        got(gained.at[chunk, other], r_gained.at[chunk])
        end = 0 if chunk >= 2 else 3
        for way, (part, pair, near, far, weight, arrival) in enumerate(ways):
            if first:
                whole_weight(weight, arrival)
            total = jnp.dot(gained[chunk, 0], weight[0], preferred_element_type=F32)
            total = total + jnp.dot(gained[chunk, 1], weight[1], preferred_element_type=F32)
            part[chunk] = total.astype(BF16)

            @pl.when(z == end)
            def _():
                start_only(
                    part.at[chunk], pair.at[chunk % 2], r_pair.at[way, chunk % 2], 1 if end == 0 else 2
                )

            if chunk in (0, 3):

                @pl.when(z == (1 if chunk == 0 else 2))
                def _():
                    start_only(part.at[chunk], near, r_near.at[way], chunk)

    def last_near():
        for way, (part, pair, near, far, weight, arrival) in enumerate(ways):

            @pl.when((z == 0) | (z == 3))
            def _():
                start_only(part.at[near_z], near, r_near.at[way], near_z)

    def join(chunk):
        middle = 1 if chunk >= 2 else 2
        for way, (part, pair, near, far, weight, arrival) in enumerate(ways):

            @pl.when(z == middle)
            def _():
                got(pair.at[chunk % 2], r_pair.at[way, chunk % 2])
                both = part[chunk].astype(F32) + pair[chunk % 2].astype(F32)
                pair[chunk % 2] = both.astype(BF16)
                start_only(pair.at[chunk % 2], far, r_far.at[way], chunk)

    relay(ORDER[0])
    relay(ORDER[1])
    project(ORDER[0])
    send_rows(ORDER[3])
    relay(ORDER[2])
    spread_out(ORDER[0], True)
    project(ORDER[1])
    relay(ORDER[3])
    spread_out(ORDER[1], False)
    project(ORDER[2])
    spread_out(ORDER[2], False)
    project(ORDER[3])
    spread_out(ORDER[3], False)
    last_near()
    for chunk in range(4):
        got(square_far.at[chunk], r_square_far.at[chunk])
        square_sum[chunk] = square_own[chunk] + square_far[chunk]
    for far in line:
        put(square_sum.at[far], square_in.at[z], r_square.at[z], far * 2 + y, t)
    square_in[z] = square_sum[z]

    join(ORDER[0])
    join(ORDER[1])
    for peer in peers:
        got(raw_in.at[peer], r_raw.at[peer])
    raw = raw_in[0]
    for j in range(1, 8):
        raw = raw + raw_in[j]
    factor = lax.rsqrt(raw[:, inner : inner + 1] / D + EPSILON)
    query_in[c] = (raw[:, :inner] * factor * HD ** (-0.5)).astype(BF16)
    for peer in peers:
        put(query_in.at[c], query_in.at[c], r_query.at[c], peer, t)
    join(ORDER[2])
    join(ORDER[3])

    for far in line:
        got(square_in.at[far], r_square.at[far])
    square = square_in[0] + square_in[1] + square_in[2] + square_in[3]
    column = jnp.sum(jnp.where(place == spot, square, 0.0), axis=-1, keepdims=True)
    scale = lax.rsqrt(column / D + EPSILON)
    for peer in peers:
        got(query_in.at[peer], r_query.at[peer])
    for j in range(8):
        query_all[j * share : (j + 1) * share, :] = query_in[j].astype(F32)

    stores = []

    def settle(way, own, out):
        part, pair, near, far, weight, arrival = ways[way]
        got(far, r_far.at[way])
        got(near, r_near.at[way])
        total = part[z].astype(F32) + near[...].astype(F32) + far[...].astype(F32)
        own[...] = (total * scale).astype(BF16)
        stores.append(fetch(own, out, stored.at[way]))

    settle(0, keys_own, keys_out)
    own_valid = lax.broadcasted_iota(jnp.int32, (1, rows), 1) * 8 + c < limit
    scores = jnp.concatenate(
        [
            lax.dot_general(
                query_all[:, h * HD : (h + 1) * HD].astype(BF16), keys_own[:, h * HD : (h + 1) * HD],
                (((1,), (1,)), ((), ())), preferred_element_type=F32,
            )
            for h in range(heads)
        ],
        axis=0,
    )
    scores = jnp.where(own_valid, scores, FLOOR)
    top = jnp.max(scores, axis=-1, keepdims=True)
    probs = jnp.where(own_valid, jnp.exp(scores - top), 0.0)
    total = jnp.sum(probs, axis=-1, keepdims=True)
    stat_own[0:1] = jnp.sum(jnp.where(place == spot, top, 0.0), axis=0, keepdims=True)
    stat_own[1:2] = jnp.sum(jnp.where(place == spot, total, 0.0), axis=0, keepdims=True)
    for peer in peers:
        put(stat_own, stat_in.at[c], r_stat.at[c], peer, t)
    settle(1, values_own, values_out)
    for h in range(heads):
        mix_own[h * tokens : (h + 1) * tokens] = jnp.dot(
            probs[h * tokens : (h + 1) * tokens].astype(BF16), values_own[:, h * HD : (h + 1) * HD],
            preferred_element_type=F32,
        ).astype(BF16)
    for peer in peers:
        put(mix_own, mix_in.at[c], r_mix.at[c], peer, t)
    stat_in[c] = stat_own[...]
    mix_in[c] = mix_own[...]
    wout_fetch.wait()
    for peer in peers:
        got(stat_in.at[peer], r_stat.at[peer])
    top = stat_in[0][0:1]
    for j in range(1, 8):
        top = jnp.maximum(top, stat_in[j][0:1])
    factors = [jnp.exp(stat_in[j][0:1] - top) for j in range(8)]
    total = factors[0] * stat_in[0][1:2]
    for j in range(1, 8):
        total = total + factors[j] * stat_in[j][1:2]
    for peer in peers:
        got(mix_in.at[peer], r_mix.at[peer])
    mixed = jnp.zeros((rows, HD), F32)
    for j in range(8):
        column = jnp.sum(jnp.where(place == spot, factors[j] / total, 0.0), axis=-1, keepdims=True)
        mixed = mixed + mix_in[j].astype(F32) * column
    attn = mixed.astype(BF16)
    proj = jnp.zeros(proj_out.shape, F32)
    for h in range(heads):
        proj = proj + jnp.dot(
            attn[h * tokens : (h + 1) * tokens], wout_own[h * HD : (h + 1) * HD], preferred_element_type=F32
        )
    proj_out[...] = proj
    put(proj_out, proj_in, r_proj, c, other)
    got(proj_in, r_proj)
    decoded_out[...] = proj_out[...] + proj_in[...] + hidden_ref[...]
    for copy in stores:
        copy.wait()
    for copy in pending:
        copy.wait_send()
    for i in range(6):
        remote(near_k, near_k, r_near.at[0], mate, t).wait_send()

    @pl.when(in_middle)
    def _():
        for i in range(8):
            remote(ctx_all.at[0, :, cols(z, HD)], ctx_all.at[0, :, cols(z, HD)], r_near.at[0], mate, t).wait_send()


def local_fused(
    enc_input, enc_query, enc_key, enc_value, seq_length, attn_out_weight, enc_gain, cross_key_weight,
    cross_value_weight, embed_table, dec_ids, dec_gain, cross_query_weight, cross_out_weight,
):
    rows, inner = enc_query.shape
    width = cross_query_weight.shape[0]
    tokens = dec_ids.size
    whole = pl.BlockSpec(memory_space=pltpu.VMEM)
    scalars = pl.BlockSpec(memory_space=pltpu.SMEM)
    anywhere = pl.BlockSpec(memory_space=pl.ANY)
    dma = pltpu.SemaphoreType.DMA
    share = tokens // 8
    half = rows // 2
    keys, values, decoded = pl.pallas_call(
        fused_kernel,
        out_shape=(
            jax.ShapeDtypeStruct((rows, inner), BF16),
            jax.ShapeDtypeStruct((rows, inner), BF16),
            jax.ShapeDtypeStruct((tokens, width), F32),
        ),
        in_specs=[scalars, scalars] + [anywhere] * 12,
        out_specs=(anywhere, anywhere, whole),
        scratch_shapes=[
            pltpu.VMEM(dec_gain.shape, BF16),
            pltpu.VMEM(enc_gain.shape, BF16),
            pltpu.VMEM((rows, inner), BF16),
            pltpu.VMEM((2, half, inner), BF16),
            pltpu.VMEM((4, rows, width), BF16),
            pltpu.VMEM((4, 2, half, width), BF16),
            pltpu.VMEM((embed_table.shape[0] // 16, 16, width), BF16),
            pltpu.VMEM((tokens, width), F32),
            pltpu.VMEM((tokens, width), BF16),
            pltpu.VMEM((tokens, width), BF16),
            pltpu.VMEM((width, inner), BF16),
            pltpu.VMEM((inner, width), BF16),
            pltpu.VMEM((8, rows, HD), BF16),
            pltpu.VMEM((8, rows, HD), BF16),
            pltpu.VMEM((8, half, HD), BF16),
            pltpu.VMEM((8, half, width), BF16),
            pltpu.VMEM((2 * inner, width), BF16),
            pltpu.VMEM((2, width, inner), BF16),
            pltpu.VMEM((2, width, inner), BF16),
            pltpu.VMEM((4, rows, 2 * inner), BF16),
            pltpu.VMEM((4, 2, rows, width), BF16),
            pltpu.VMEM((4, 1, rows), F32),
            pltpu.VMEM((4, 1, rows), F32),
            pltpu.VMEM((4, 1, rows), F32),
            pltpu.VMEM((4, 1, rows), F32),
            pltpu.VMEM((4, rows, inner), BF16),
            pltpu.VMEM((4, rows, inner), BF16),
            pltpu.VMEM((2, rows, inner), BF16),
            pltpu.VMEM((2, rows, inner), BF16),
            pltpu.VMEM((rows, inner), BF16),
            pltpu.VMEM((rows, inner), BF16),
            pltpu.VMEM((rows, inner), BF16),
            pltpu.VMEM((rows, inner), BF16),
            pltpu.VMEM((rows, inner), BF16),
            pltpu.VMEM((rows, inner), BF16),
            pltpu.VMEM((tokens, inner + 128), F32),
            pltpu.VMEM((8, share, inner + 128), F32),
            pltpu.VMEM((8, share, inner + 128), F32),
            pltpu.VMEM((8, share, inner), BF16),
            pltpu.VMEM((tokens, inner), F32),
            pltpu.VMEM((rows, HD), BF16),
            pltpu.VMEM((8, rows, HD), BF16),
            pltpu.VMEM((2, rows), F32),
            pltpu.VMEM((8, 2, rows), F32),
            pltpu.VMEM((tokens, width), F32),
            pltpu.VMEM((tokens, width), F32),
            pltpu.VMEM((tokens, width), F32),
            dma, dma, dma, dma((8,)), dma((8,)), dma((8,)), dma((2,)), dma((2,)), dma((2,)), dma((2,)), dma((8,)), dma((8,)), dma((8, 4)),
            dma((8, 4)), dma((4,)), dma((4,)), dma((4,)),
            dma((2, 2)), dma((2,)), dma((2,)), dma((8,)), dma((8,)), dma, dma((15,)), dma((2,)),
        ],
        compiler_params=pltpu.CompilerParams(
            collective_id=0, has_side_effects=True, vmem_limit_bytes=60 * 1024 * 1024
        ),
    )(
        dec_ids.T, seq_length, dec_gain, enc_gain, enc_query, enc_key, enc_value, enc_input,
        embed_table.reshape(embed_table.shape[0] // 16, 16, width),
        cross_query_weight, attn_out_weight, cross_key_weight, cross_value_weight, cross_out_weight,
    )
    return pl.pallas_call(
        hand_kernel,
        out_shape=(
            jax.ShapeDtypeStruct((1, rows, inner), BF16),
            jax.ShapeDtypeStruct((1, rows, inner), BF16),
            jax.ShapeDtypeStruct((tokens // 2, 2, width), BF16),
        ),
        in_specs=[whole] * 3,
        out_specs=(whole, whole, whole),
    )(keys, values, decoded)


def chosen(*arrays):
    rows, inner = arrays[1].shape
    fits = lax.axis_size("ctx") == 8 and lax.axis_size("tp") == 2 and (rows, inner) == (128, 4 * HD)
    fits = fits and arrays[9].shape[0] % 16 == 0
    return (local_fused if fits else local)(*arrays)


def solution(mesh):
    placed = (
        P(("groups", "ctx"), None),
        P(("groups", "ctx"), "tp"),
        P(("groups", "ctx"), "tp"),
        P(("groups", "ctx"), "tp"),
        P("groups"),
        P("tp", None),
        P(),
        P("ctx", "tp"),
        P("ctx", "tp"),
        P("tp", "ctx"),
        P("groups", None),
        P("ctx"),
        P("ctx", "tp"),
        P("tp", "ctx"),
    )
    return jax.shard_map(
        chosen,
        mesh=mesh,
        in_specs=placed,
        out_specs=(
            P(("groups", "ctx"), None, "tp"),
            P(("groups", "ctx"), None, "tp"),
            P("groups", None, "ctx"),
        ),
        check_vma=False,
    )
```

```python
import math

import jax
import jax.numpy as jnp
from jax import lax
from jax.experimental import pallas as pl
from jax.experimental.pallas import tpu as pltpu
from jax.sharding import PartitionSpec as P

D = 4096
HD = 128


EPSILON = 1e-06
FLOOR = -1e30


def joined(value, axis, join):
    pieces = jax.tree.map(lambda part: lax.all_gather(part, axis), value)
    head = jax.tree.map(lambda part: part[0], pieces)
    tail = jax.tree.map(lambda part: part[1:], pieces)
    total, _ = lax.scan(lambda total, piece: (join(total, piece), None), head, tail)
    return total


def softmax_merge(first, second):
    top_first, total_first, mixed_first = first
    top_second, total_second, mixed_second = second
    top = jnp.maximum(top_first, top_second)
    weight_first = jnp.exp(top_first - top)
    weight_second = jnp.exp(top_second - top)
    total = total_first * weight_first + total_second * weight_second
    mixed = mixed_first * weight_first[..., None] + mixed_second * weight_second[..., None]
    return (top, total, mixed)


def partial_softmax(queries, keys, values, valid, factor):
    scores = jnp.einsum("qhd,khd->hqk", queries, keys, preferred_element_type=jnp.float32) * factor
    scores = jnp.where(valid[None, None, :], scores, FLOOR)
    top = jnp.max(scores, axis=-1)
    probs = jnp.where(valid[None, None, :], jnp.exp(scores - top[..., None]), 0.0)
    total = jnp.sum(probs, axis=-1)
    mixed = jnp.einsum(
        "hqk,khd->hqd", probs.astype(jnp.bfloat16), values, preferred_element_type=jnp.float32
    )
    return (top, total, mixed)


def norm_rows(resid, gain):
    scale = lax.rsqrt(jnp.mean(resid * resid, axis=-1, keepdims=True) + EPSILON)
    return (resid * scale * gain.astype(jnp.float32)).astype(jnp.bfloat16)


def local(
    enc_input,
    enc_query,
    enc_key,
    enc_value,
    seq_length,
    attn_out_weight,
    enc_gain,
    cross_key_weight,
    cross_value_weight,
    embed_table,
    dec_ids,
    dec_gain,
    cross_query_weight,
    cross_out_weight,
):
    rows, inner_local = enc_query.shape
    heads_local = inner_local // HD
    limit = seq_length[0]
    queries = enc_query.reshape(rows, heads_local, HD)
    start_state = (
        jnp.full((heads_local, rows), FLOOR, jnp.float32),
        jnp.zeros((heads_local, rows), jnp.float32),
        jnp.zeros((heads_local, rows, HD), jnp.float32),
    )
    carry = start_state
    key_rows = lax.all_gather(enc_key, "ctx", axis=0, tiled=True)
    value_rows = lax.all_gather(enc_value, "ctx", axis=0, tiled=True)
    count = key_rows.shape[0]
    block = math.gcd(count, 2048)
    blocks = count // block
    key_blocks = key_rows.reshape(blocks, block, heads_local, HD)
    value_blocks = value_rows.reshape(blocks, block, heads_local, HD)
    offsets = jnp.arange(blocks, dtype=jnp.int32) * block

    def one_block(state, item):
        key_block, value_block, offset = item
        positions = offset + jnp.arange(block, dtype=jnp.int32)
        update = partial_softmax(queries, key_block, value_block, positions < limit, HD ** (-0.5))
        return (softmax_merge(state, update), None)

    carry, unused = lax.scan(one_block, carry, (key_blocks, value_blocks, offsets))
    top, total, mixed = carry
    context = (
        jnp.transpose(mixed / total[..., None], (1, 0, 2))
        .reshape(rows, inner_local)
        .astype(jnp.bfloat16)
    )
    summed = lax.psum(jnp.dot(context, attn_out_weight, preferred_element_type=jnp.float32), "tp")
    memory = norm_rows(enc_input.astype(jnp.float32) + summed, enc_gain)
    ctx_count = lax.axis_size("ctx")
    slots = rows // ctx_count
    key_sum = jnp.dot(
        memory,
        lax.all_gather(cross_key_weight, "ctx", axis=0, tiled=True),
        preferred_element_type=jnp.float32,
    )
    value_sum = jnp.dot(
        memory,
        lax.all_gather(cross_value_weight, "ctx", axis=0, tiled=True),
        preferred_element_type=jnp.float32,
    )
    key_rows = key_sum.astype(jnp.bfloat16)
    value_rows = value_sum.astype(jnp.bfloat16)
    keys_moved, values_moved = (
        lax.all_to_all(
            key_rows.reshape(slots, ctx_count, inner_local),
            "ctx",
            split_axis=1,
            concat_axis=0,
            tiled=True,
        ),
        lax.all_to_all(
            value_rows.reshape(slots, ctx_count, inner_local),
            "ctx",
            split_axis=1,
            concat_axis=0,
            tiled=True,
        ),
    )
    keys_cache = keys_moved.reshape(rows, inner_local)
    values_cache = values_moved.reshape(rows, inner_local)
    beams = dec_ids.shape[0]
    vocab_local = embed_table.shape[0]
    flat_ids = dec_ids.reshape(-1) - lax.axis_index("tp") * vocab_local
    inside = (flat_ids >= 0) & (flat_ids < vocab_local)
    looked = jnp.take(embed_table, jnp.clip(flat_ids, 0, vocab_local - 1), axis=0)
    own_rows = jnp.where(inside[:, None], looked.astype(jnp.float32), 0.0)
    hidden = lax.psum(own_rows.astype(jnp.bfloat16), "tp").astype(jnp.float32)
    scaled = (hidden * dec_gain.astype(jnp.float32)).astype(jnp.bfloat16)
    raw_part = jnp.dot(scaled, cross_query_weight, preferred_element_type=jnp.float32)
    square_part = jnp.sum(hidden * hidden, axis=-1)
    raw, squares = lax.psum((raw_part, square_part), "ctx")
    factor = lax.rsqrt(squares / D + EPSILON)
    query = (raw * factor[:, None] * HD ** (-0.5)).astype(jnp.bfloat16).reshape(-1, heads_local, HD)
    positions = jnp.arange(rows, dtype=jnp.int32) * ctx_count + lax.axis_index("ctx")
    local_part = partial_softmax(
        query,
        keys_cache.reshape(rows, heads_local, HD),
        values_cache.reshape(rows, heads_local, HD),
        positions < limit,
        1.0,
    )
    top_all, total_all, mixed_all = joined(local_part, "ctx", softmax_merge)
    attn = (
        jnp.transpose(mixed_all / total_all[..., None], (1, 0, 2))
        .reshape(-1, inner_local)
        .astype(jnp.bfloat16)
    )
    out_part = jnp.dot(attn, cross_out_weight, preferred_element_type=jnp.float32)
    out = lax.psum(out_part, "tp")
    decoded = (out + hidden).astype(jnp.bfloat16).reshape(beams, 2, -1)
    return (keys_cache[None], values_cache[None], decoded)


MESH = pl.DeviceIdType.MESH
F32 = jnp.float32
BF16 = jnp.bfloat16
ORDER = (3, 0, 2, 1)


def hand_kernel(keys_ref, values_ref, decoded_ref, keys_out, values_out, decoded_out):
    keys_out[0] = keys_ref[...]
    values_out[0] = values_ref[...]
    for i in range(decoded_out.shape[0]):
        decoded_out[i] = decoded_ref[2 * i : 2 * i + 2].astype(BF16)


def fused_kernel(
    ids, length, dec_gain_far, enc_gain_far, q, k, v, ein, table, wq, wo, wk, wv, wout,
    keys_out, values_out, decoded_out,
    dec_gain, enc_gain, q_own, q_turned, ein_own, ein_turned, table_own, rows_own, looked, looked_far, wq_own, wout_own,
    kg, vg, qg, eg, wo_all, wk_all, wv_all, ctx_all, gained, square_own, square_far, square_sum, square_in,
    part_k, part_v, pair_k, pair_v, near_k, near_v, far_k, far_v, keys_own, values_own,
    raw_own, raw_out, raw_in, query_in, query_all, mix_own, mix_in, stat_own, stat_in, proj_out, proj_in, hidden_ref,
    send, r_look, r_wo, r_q, r_k, r_v, r_wk, r_wv, t_wk, t_wv, r_raw, r_query, r_ein, r_ctx, r_gained, r_square_far, r_square,
    r_pair, r_near, r_far, r_mix, r_stat, r_proj, fetched, stored,
):
    g = lax.axis_index("groups")
    c = lax.axis_index("ctx")
    t = lax.axis_index("tp")
    z, y = lax.div(c, 2), lax.rem(c, 2)
    mate, other = c + 1 - 2 * y, 1 - t
    line = [lax.rem(z + d, 4) for d in (2, 1, 3)]
    near_z = z + 1 - 2 * lax.rem(z, 2)
    across = 2 - 2 * lax.div(z, 2)
    across_middle = 2 - lax.div(z, 2)
    in_middle = (z == 1) | (z == 2)
    peers = [lax.rem(c + d, 8) for d in range(1, 8)]
    rows = q.shape[0]
    inner = q.shape[1]
    width = wq.shape[0]
    half = rows // 2
    each = rows // 8
    own_block = z * 2 + t
    heads = inner // HD
    pending = []

    def remote(source, target, arrival, to_ctx, to_tp):
        return pltpu.make_async_remote_copy(
            src_ref=source, dst_ref=target, send_sem=send, recv_sem=arrival,
            device_id={"ctx": to_ctx, "tp": to_tp}, device_id_type=MESH,
        )

    def put(source, target, arrival, to_ctx, to_tp):
        copy = remote(source, target, arrival, to_ctx, to_tp)
        copy.start()
        pending.append(copy)

    def put_twin(source, target, arrival):
        copy = pltpu.make_async_remote_copy(
            src_ref=source, dst_ref=target, send_sem=send, recv_sem=arrival,
            device_id={"groups": 1 - g, "ctx": c, "tp": t}, device_id_type=MESH,
        )
        copy.start()
        pending.append(copy)

    def got(target, arrival):
        remote(target, target, arrival, mate, t).wait_recv()

    def fetch(source, target, arrival):
        copy = pltpu.make_async_copy(source, target, arrival)
        copy.start()
        return copy

    def cols(index, size):
        return pl.ds(pl.multiple_of(index * size, size), size)

    barrier = pltpu.get_barrier_semaphore()
    for peer in peers:
        pl.semaphore_signal(barrier, inc=1, device_id={"ctx": peer, "tp": t}, device_id_type=MESH)
    pl.semaphore_signal(barrier, inc=1, device_id={"ctx": c, "tp": other}, device_id_type=MESH)
    pl.semaphore_signal(barrier, inc=1, device_id={"groups": 1 - g, "ctx": c, "tp": t}, device_id_type=MESH)

    gain_fetches = [fetch(dec_gain_far, dec_gain, fetched.at[13]), fetch(enc_gain_far, enc_gain, fetched.at[14])]
    q_fetch = fetch(q, q_own, fetched.at[0])
    k_fetch = fetch(k.at[:, cols(z, HD)], kg.at[c], fetched.at[1])
    v_fetch = fetch(v.at[:, cols(z, HD)], vg.at[c], fetched.at[2])
    ein_fetches = [
        fetch(ein.at[:, cols(far * 2 + t, width)], ein_own.at[far], fetched.at[3 + far]) for far in range(4)
    ]
    table_fetch = fetch(table, table_own, fetched.at[7])
    wq_fetch = fetch(wq, wq_own, fetched.at[8])
    late = [
        fetch(wo.at[:, cols(own_block, width)], wo_all.at[cols(t, inner)], fetched.at[9]),
        fetch(wk, wk_all.at[y], fetched.at[10]),
        fetch(wv, wv_all.at[y], fetched.at[11]),
    ]
    wout_fetch = fetch(wout, wout_own, fetched.at[12])
    pl.semaphore_wait(barrier, len(peers) + 2)

    for far in line:
        to = far * 2 + y
        put(k.at[:, cols(far, HD)], kg.at[c], r_k.at[c], to, t)
        put(v.at[:, cols(far, HD)], vg.at[c], r_v.at[c], to, t)
    put(k.at[:, cols(z, HD)], kg.at[c], r_k.at[c], mate, t)
    put(v.at[:, cols(z, HD)], vg.at[c], r_v.at[c], mate, t)

    place = lax.broadcasted_iota(jnp.int32, (rows, rows), 0)
    spot = lax.broadcasted_iota(jnp.int32, (rows, rows), 1)
    side, rest = lax.div(place, half), lax.rem(place, half)
    turn = (spot == lax.rem(rest, each) * 8 + lax.div(rest, each) * 2 + side).astype(BF16)

    q_fetch.wait()
    for copy in gain_fetches:
        copy.wait()
    turned = jnp.dot(turn, q_own[...], preferred_element_type=F32).astype(BF16)
    for s in range(2):
        q_turned[s] = turned[s * half : (s + 1) * half]
    for peer in peers:
        put(
            q_turned.at[lax.rem(peer, 2), :, cols(lax.div(peer, 2), HD)], qg.at[c], r_q.at[c], peer, t
        )
    qg[c] = q_turned[y, :, cols(z, HD)]
    put(wo.at[:, cols(z * 2 + other, width)], wo_all.at[cols(t, inner)], r_wo, c, other)
    piece = width // 4

    def weight_rows(index):
        return pl.ds(pl.multiple_of(index * piece, piece), piece)

    def send_weight(weight, whole, arrivals):
        for part in range(2):
            where = weight_rows(g * 2 + part)
            put(weight.at[where], whole.at[y, where], arrivals.at[part], mate, t)

    def relay_weight(whole, arrivals, twins):
        for part in range(2):
            where = weight_rows(g * 2 + part)
            here = whole.at[1 - y, where]
            got(here, arrivals.at[part])
            put_twin(here, here, twins.at[part])

    def whole_weight(whole, twins):
        for part in range(2):
            got(whole.at[1 - y, weight_rows((1 - g) * 2 + part)], twins.at[part])

    send_weight(wk, wk_all, r_wk)

    tokens = looked.shape[0]
    for far in range(4):
        ein_fetches[far].wait()
        turned = jnp.dot(turn, ein_own[far], preferred_element_type=F32).astype(BF16)
        for s in range(2):
            ein_turned[far, s] = turned[s * half : (s + 1) * half]

    eg[c] = ein_turned[z, y]
    for far in line:
        source = far * 2 + y
        got(kg.at[source], r_k.at[source])
        put(kg.at[source], kg.at[source], r_k.at[source], mate, t)
        got(vg.at[source], r_v.at[source])
        put(vg.at[source], vg.at[source], r_v.at[source], mate, t)
    send_weight(wv, wv_all, r_wv)
    def send_rows(chunk):
        where = slice(chunk * each, (chunk + 1) * each)
        for peer in peers:
            put(
                ein_turned.at[lax.div(peer, 2), lax.rem(peer, 2), where], eg.at[c, where], r_ein.at[c, chunk], peer, t
            )

    send_rows(ORDER[0])
    send_rows(ORDER[1])
    relay_weight(wk_all, r_wk, t_wk)

    table_fetch.wait()
    first = t * table.shape[0] * 16
    spots = lax.broadcasted_iota(jnp.int32, (16, width), 0)
    for j in range(tokens):
        own = ids[j % 2, j // 2] - first
        near = jnp.clip(own, 0, table.shape[0] * 16 - 1)
        block = table_own[lax.div(near, 16)].astype(F32)
        picked = spots + lax.div(near, 16) * 16 == own
        rows_own[j : j + 1] = jnp.sum(jnp.where(picked, block, 0.0), axis=0, keepdims=True)
    looked[...] = rows_own[...].astype(BF16)
    put(looked, looked_far, r_look, c, other)
    got(looked_far, r_look)
    wq_fetch.wait()
    hidden = looked[...].astype(F32) + looked_far[...].astype(F32)
    hidden_ref[...] = hidden
    scaled = (hidden * dec_gain[...].astype(F32).reshape(1, width)).astype(BF16)
    raw_own[:, :inner] = jnp.dot(scaled, wq_own[...], preferred_element_type=F32)
    raw_own[:, inner:] = jnp.broadcast_to(jnp.sum(hidden * hidden, axis=-1, keepdims=True), (tokens, 128))
    share = tokens // 8
    for j in range(8):
        raw_out[j] = raw_own[j * share : (j + 1) * share, :]
    for peer in peers:
        put(raw_out.at[peer], raw_in.at[c], r_raw.at[c], peer, t)
    raw_in[c] = raw_out[c]

    k_fetch.wait()
    v_fetch.wait()
    for peer in peers:
        got(qg.at[peer], r_q.at[peer])
    for far in range(4):
        source = far * 2 + 1 - y
        got(kg.at[source], r_k.at[source])
        got(vg.at[source], r_v.at[source])

    limit = length[0]
    every_key = kg[...].reshape(8 * rows, HD)
    every_value = vg[...].reshape(8 * rows, HD)
    valid = lax.broadcasted_iota(jnp.int32, (1, 8 * rows), 1) < limit

    def block_at(core, far, chunk):
        return ctx_all.at[chunk, :, cols(core * 4 + far, HD)], r_ctx.at[core * 4 + far, chunk]

    for chunk in ORDER:
        queries = qg[:, chunk * each : (chunk + 1) * each, :].reshape(rows, HD)
        scores = lax.dot_general(
            queries, every_key, (((1,), (1,)), ((), ())), preferred_element_type=F32
        ) * (HD ** (-0.5))
        scores = jnp.where(valid, scores, FLOOR)
        top = jnp.max(scores, axis=-1, keepdims=True)
        probs = jnp.where(valid, jnp.exp(scores - top), 0.0)
        total = jnp.sum(probs, axis=-1, keepdims=True)
        mixed = jnp.dot(probs.astype(BF16), every_value, preferred_element_type=F32)
        ctx_all[chunk, :, cols(t * 4 + z, HD)] = (mixed / total).astype(BF16)
        here, arrival = block_at(t, z, chunk)
        put(here, here, arrival, across_middle * 2 + y, t)
        put(here, here, arrival, near_z * 2 + y, t)
        put(here, here, arrival, c, other)

    send_rows(ORDER[2])
    relay_weight(wv_all, r_wv, t_wv)

    for copy in late:
        copy.wait()
    got(wo_all.at[cols(other, inner)], r_wo)
    gain = enc_gain[cols(own_block, width)].astype(F32).reshape(1, width)

    def relay(chunk):
        for far in (across_middle, across * 2 + 1 - across_middle, near_z):
            here, arrival = block_at(t, far, chunk)
            got(here, arrival)
            if far is not near_z:

                @pl.when(in_middle)
                def _():
                    remote(here, here, arrival, near_z * 2 + y, t).start()

            put(here, here, arrival, c, other)

    def project(chunk):
        for far in range(4):
            got(*block_at(other, far, chunk))
        for peer in peers:
            got(eg.at[peer, chunk * each : (chunk + 1) * each], r_ein.at[peer, chunk])
        resid = jnp.dot(ctx_all[chunk], wo_all[...], preferred_element_type=F32)
        resid = resid + eg[:, chunk * each : (chunk + 1) * each, :].reshape(rows, width).astype(F32)
        spread = jnp.where(place == spot, jnp.sum(resid * resid, axis=-1, keepdims=True), 0.0)
        square_own[chunk] = jnp.sum(spread, axis=0, keepdims=True)
        gained[chunk, t] = (resid * gain).astype(BF16)
        put(gained.at[chunk, t], gained.at[chunk, t], r_gained.at[chunk], c, other)
        put(square_own.at[chunk], square_far.at[chunk], r_square_far.at[chunk], c, other)

    ways = ((part_k, pair_k, near_k, far_k, wk_all, t_wk), (part_v, pair_v, near_v, far_v, wv_all, t_wv))

    def start_only(source, target, arrival, to_z):
        remote(source, target, arrival, to_z * 2 + y, t).start()

    def spread_out(chunk, first):
        got(gained.at[chunk, other], r_gained.at[chunk])
        end = 0 if chunk >= 2 else 3
        for way, (part, pair, near, far, weight, arrival) in enumerate(ways):
            if first:
                whole_weight(weight, arrival)
            total = jnp.dot(gained[chunk, 0], weight[0], preferred_element_type=F32)
            total = total + jnp.dot(gained[chunk, 1], weight[1], preferred_element_type=F32)
            part[chunk] = total.astype(BF16)

            @pl.when(z == end)
            def _():
                start_only(
                    part.at[chunk], pair.at[chunk % 2], r_pair.at[way, chunk % 2], 1 if end == 0 else 2
                )

            if chunk in (0, 3):

                @pl.when(z == (1 if chunk == 0 else 2))
                def _():
                    start_only(part.at[chunk], near, r_near.at[way], chunk)

    def last_near():
        for way, (part, pair, near, far, weight, arrival) in enumerate(ways):

            @pl.when((z == 0) | (z == 3))
            def _():
                start_only(part.at[near_z], near, r_near.at[way], near_z)

    def join(chunk):
        middle = 1 if chunk >= 2 else 2
        for way, (part, pair, near, far, weight, arrival) in enumerate(ways):

            @pl.when(z == middle)
            def _():
                got(pair.at[chunk % 2], r_pair.at[way, chunk % 2])
                both = part[chunk].astype(F32) + pair[chunk % 2].astype(F32)
                pair[chunk % 2] = both.astype(BF16)
                start_only(pair.at[chunk % 2], far, r_far.at[way], chunk)

    relay(ORDER[0])
    relay(ORDER[1])
    project(ORDER[0])
    relay(ORDER[2])
    send_rows(ORDER[3])
    spread_out(ORDER[0], True)
    project(ORDER[1])
    relay(ORDER[3])
    spread_out(ORDER[1], False)
    project(ORDER[2])
    spread_out(ORDER[2], False)
    project(ORDER[3])
    spread_out(ORDER[3], False)
    last_near()
    for chunk in range(4):
        got(square_far.at[chunk], r_square_far.at[chunk])
        square_sum[chunk] = square_own[chunk] + square_far[chunk]
    for far in line:
        put(square_sum.at[far], square_in.at[z], r_square.at[z], far * 2 + y, t)
    square_in[z] = square_sum[z]

    join(ORDER[0])
    join(ORDER[1])
    join(ORDER[2])
    for peer in peers:
        got(raw_in.at[peer], r_raw.at[peer])
    raw = raw_in[0]
    for j in range(1, 8):
        raw = raw + raw_in[j]
    factor = lax.rsqrt(raw[:, inner : inner + 1] / D + EPSILON)
    query_in[c] = (raw[:, :inner] * factor * HD ** (-0.5)).astype(BF16)
    for peer in peers:
        put(query_in.at[c], query_in.at[c], r_query.at[c], peer, t)
    join(ORDER[3])

    for far in line:
        got(square_in.at[far], r_square.at[far])
    square = square_in[0] + square_in[1] + square_in[2] + square_in[3]
    column = jnp.sum(jnp.where(place == spot, square, 0.0), axis=-1, keepdims=True)
    scale = lax.rsqrt(column / D + EPSILON)
    for peer in peers:
        got(query_in.at[peer], r_query.at[peer])
    for j in range(8):
        query_all[j * share : (j + 1) * share, :] = query_in[j].astype(F32)

    stores = []

    def settle(way, own, out):
        part, pair, near, far, weight, arrival = ways[way]
        got(far, r_far.at[way])
        got(near, r_near.at[way])
        total = part[z].astype(F32) + near[...].astype(F32) + far[...].astype(F32)
        own[...] = (total * scale).astype(BF16)
        stores.append(fetch(own, out, stored.at[way]))

    settle(0, keys_own, keys_out)
    own_valid = lax.broadcasted_iota(jnp.int32, (1, rows), 1) * 8 + c < limit
    scores = jnp.concatenate(
        [
            lax.dot_general(
                query_all[:, h * HD : (h + 1) * HD].astype(BF16), keys_own[:, h * HD : (h + 1) * HD],
                (((1,), (1,)), ((), ())), preferred_element_type=F32,
            )
            for h in range(heads)
        ],
        axis=0,
    )
    scores = jnp.where(own_valid, scores, FLOOR)
    top = jnp.max(scores, axis=-1, keepdims=True)
    probs = jnp.where(own_valid, jnp.exp(scores - top), 0.0)
    total = jnp.sum(probs, axis=-1, keepdims=True)
    stat_own[0:1] = jnp.sum(jnp.where(place == spot, top, 0.0), axis=0, keepdims=True)
    stat_own[1:2] = jnp.sum(jnp.where(place == spot, total, 0.0), axis=0, keepdims=True)
    for peer in peers:
        put(stat_own, stat_in.at[c], r_stat.at[c], peer, t)
    settle(1, values_own, values_out)
    for h in range(heads):
        mix_own[h * tokens : (h + 1) * tokens] = jnp.dot(
            probs[h * tokens : (h + 1) * tokens].astype(BF16), values_own[:, h * HD : (h + 1) * HD],
            preferred_element_type=F32,
        ).astype(BF16)
    for peer in peers:
        put(mix_own, mix_in.at[c], r_mix.at[c], peer, t)
    stat_in[c] = stat_own[...]
    mix_in[c] = mix_own[...]
    wout_fetch.wait()
    for peer in peers:
        got(stat_in.at[peer], r_stat.at[peer])
    top = stat_in[0][0:1]
    for j in range(1, 8):
        top = jnp.maximum(top, stat_in[j][0:1])
    factors = [jnp.exp(stat_in[j][0:1] - top) for j in range(8)]
    total = factors[0] * stat_in[0][1:2]
    for j in range(1, 8):
        total = total + factors[j] * stat_in[j][1:2]
    for peer in peers:
        got(mix_in.at[peer], r_mix.at[peer])
    mixed = jnp.zeros((rows, HD), F32)
    for j in range(8):
        column = jnp.sum(jnp.where(place == spot, factors[j] / total, 0.0), axis=-1, keepdims=True)
        mixed = mixed + mix_in[j].astype(F32) * column
    attn = mixed.astype(BF16)
    proj = jnp.zeros(proj_out.shape, F32)
    for h in range(heads):
        proj = proj + jnp.dot(
            attn[h * tokens : (h + 1) * tokens], wout_own[h * HD : (h + 1) * HD], preferred_element_type=F32
        )
    proj_out[...] = proj
    put(proj_out, proj_in, r_proj, c, other)
    got(proj_in, r_proj)
    decoded_out[...] = proj_out[...] + proj_in[...] + hidden_ref[...]
    for copy in stores:
        copy.wait()
    for copy in pending:
        copy.wait_send()
    for i in range(6):
        remote(near_k, near_k, r_near.at[0], mate, t).wait_send()

    @pl.when(in_middle)
    def _():
        for i in range(8):
            remote(ctx_all.at[0, :, cols(z, HD)], ctx_all.at[0, :, cols(z, HD)], r_near.at[0], mate, t).wait_send()


def local_fused(
    enc_input, enc_query, enc_key, enc_value, seq_length, attn_out_weight, enc_gain, cross_key_weight,
    cross_value_weight, embed_table, dec_ids, dec_gain, cross_query_weight, cross_out_weight,
):
    rows, inner = enc_query.shape
    width = cross_query_weight.shape[0]
    tokens = dec_ids.size
    whole = pl.BlockSpec(memory_space=pltpu.VMEM)
    scalars = pl.BlockSpec(memory_space=pltpu.SMEM)
    anywhere = pl.BlockSpec(memory_space=pl.ANY)
    dma = pltpu.SemaphoreType.DMA
    share = tokens // 8
    half = rows // 2
    keys, values, decoded = pl.pallas_call(
        fused_kernel,
        out_shape=(
            jax.ShapeDtypeStruct((rows, inner), BF16),
            jax.ShapeDtypeStruct((rows, inner), BF16),
            jax.ShapeDtypeStruct((tokens, width), F32),
        ),
        in_specs=[scalars, scalars] + [anywhere] * 12,
        out_specs=(anywhere, anywhere, whole),
        scratch_shapes=[
            pltpu.VMEM(dec_gain.shape, BF16),
            pltpu.VMEM(enc_gain.shape, BF16),
            pltpu.VMEM((rows, inner), BF16),
            pltpu.VMEM((2, half, inner), BF16),
            pltpu.VMEM((4, rows, width), BF16),
            pltpu.VMEM((4, 2, half, width), BF16),
            pltpu.VMEM((embed_table.shape[0] // 16, 16, width), BF16),
            pltpu.VMEM((tokens, width), F32),
            pltpu.VMEM((tokens, width), BF16),
            pltpu.VMEM((tokens, width), BF16),
            pltpu.VMEM((width, inner), BF16),
            pltpu.VMEM((inner, width), BF16),
            pltpu.VMEM((8, rows, HD), BF16),
            pltpu.VMEM((8, rows, HD), BF16),
            pltpu.VMEM((8, half, HD), BF16),
            pltpu.VMEM((8, half, width), BF16),
            pltpu.VMEM((2 * inner, width), BF16),
            pltpu.VMEM((2, width, inner), BF16),
            pltpu.VMEM((2, width, inner), BF16),
            pltpu.VMEM((4, rows, 2 * inner), BF16),
            pltpu.VMEM((4, 2, rows, width), BF16),
            pltpu.VMEM((4, 1, rows), F32),
            pltpu.VMEM((4, 1, rows), F32),
            pltpu.VMEM((4, 1, rows), F32),
            pltpu.VMEM((4, 1, rows), F32),
            pltpu.VMEM((4, rows, inner), BF16),
            pltpu.VMEM((4, rows, inner), BF16),
            pltpu.VMEM((2, rows, inner), BF16),
            pltpu.VMEM((2, rows, inner), BF16),
            pltpu.VMEM((rows, inner), BF16),
            pltpu.VMEM((rows, inner), BF16),
            pltpu.VMEM((rows, inner), BF16),
            pltpu.VMEM((rows, inner), BF16),
            pltpu.VMEM((rows, inner), BF16),
            pltpu.VMEM((rows, inner), BF16),
            pltpu.VMEM((tokens, inner + 128), F32),
            pltpu.VMEM((8, share, inner + 128), F32),
            pltpu.VMEM((8, share, inner + 128), F32),
            pltpu.VMEM((8, share, inner), BF16),
            pltpu.VMEM((tokens, inner), F32),
            pltpu.VMEM((rows, HD), BF16),
            pltpu.VMEM((8, rows, HD), BF16),
            pltpu.VMEM((2, rows), F32),
            pltpu.VMEM((8, 2, rows), F32),
            pltpu.VMEM((tokens, width), F32),
            pltpu.VMEM((tokens, width), F32),
            pltpu.VMEM((tokens, width), F32),
            dma, dma, dma, dma((8,)), dma((8,)), dma((8,)), dma((2,)), dma((2,)), dma((2,)), dma((2,)), dma((8,)), dma((8,)), dma((8, 4)),
            dma((8, 4)), dma((4,)), dma((4,)), dma((4,)),
            dma((2, 2)), dma((2,)), dma((2,)), dma((8,)), dma((8,)), dma, dma((15,)), dma((2,)),
        ],
        compiler_params=pltpu.CompilerParams(
            collective_id=0, has_side_effects=True, vmem_limit_bytes=60 * 1024 * 1024
        ),
    )(
        dec_ids.T, seq_length, dec_gain, enc_gain, enc_query, enc_key, enc_value, enc_input,
        embed_table.reshape(embed_table.shape[0] // 16, 16, width),
        cross_query_weight, attn_out_weight, cross_key_weight, cross_value_weight, cross_out_weight,
    )
    return pl.pallas_call(
        hand_kernel,
        out_shape=(
            jax.ShapeDtypeStruct((1, rows, inner), BF16),
            jax.ShapeDtypeStruct((1, rows, inner), BF16),
            jax.ShapeDtypeStruct((tokens // 2, 2, width), BF16),
        ),
        in_specs=[whole] * 3,
        out_specs=(whole, whole, whole),
    )(keys, values, decoded)


def chosen(*arrays):
    rows, inner = arrays[1].shape
    fits = lax.axis_size("ctx") == 8 and lax.axis_size("tp") == 2 and (rows, inner) == (128, 4 * HD)
    fits = fits and arrays[9].shape[0] % 16 == 0
    return (local_fused if fits else local)(*arrays)


def solution(mesh):
    placed = (
        P(("groups", "ctx"), None),
        P(("groups", "ctx"), "tp"),
        P(("groups", "ctx"), "tp"),
        P(("groups", "ctx"), "tp"),
        P("groups"),
        P("tp", None),
        P(),
        P("ctx", "tp"),
        P("ctx", "tp"),
        P("tp", "ctx"),
        P("groups", None),
        P("ctx"),
        P("ctx", "tp"),
        P("tp", "ctx"),
    )
    return jax.shard_map(
        chosen,
        mesh=mesh,
        in_specs=placed,
        out_specs=(
            P(("groups", "ctx"), None, "tp"),
            P(("groups", "ctx"), None, "tp"),
            P("groups", None, "ctx"),
        ),
        check_vma=False,
    )
```
